32 devices in a mesh: seabed: 8 (over y, x, core), freq: 4 (over z).
Axes of the slice: x: 2, y: 2, z: 4, core: 2. Of those that a mesh axis runs over, the one named last changes fastest.
Arguments:
- uplift: bfloat16 [128, 32, 40, 128], P('freq', None, 'seabed'), may hold values from -6 to 6
- coefficient: float32 [40, 128], P('seabed'), may hold values from 0.06 to 0.24
- transfer: float32 [4, 2, 600, 5120], P('freq', None, None, 'seabed'), may hold values from -0.0625 to 0.0625
Outputs:
- sensors: float32 [128, 4, 2, 600], P('seabed', 'freq')
The draws below stay inside these ranges and needn't reach their ends.
All inputs are finite; a program needn't handle non-finite values.
Results may differ from the reference program's by a relative error of at most 0.0003.
Values sent between devices are 32-bit elements; how exact they have to be, the bound alone decides.
No kernel may reach another device: no remote copies, remote signals or barrier semaphores. Data moves between devices by JAX's collectives and lax.ppermute only.
A program may use at most 64 MiB of HBM per device.

```python
import math
import jax
import jax.numpy as jnp
from jax import lax

PATCH = 128
SENS = 600
NV = 128
PASSES = 3
NT = 32
NF = 4
NR = 40


def block_scale(own_key, extent, cuts, low, high):
    def one(axis_at, shards_of):
        heights = jax.random.uniform(jax.random.fold_in(jax.random.fold_in(own_key, 6), axis_at), (shards_of,), jnp.float32, low / len(cuts), high / len(cuts))
        return jnp.repeat(jnp.exp(heights), extent[axis_at] // shards_of).reshape((-1,) + (1,) * (len(extent) - axis_at - 1))

    gain = one(*cuts[0])
    for cut in cuts[1:]:
        gain = gain * one(*cut)
    return gain


def bell_draw(rng, extent, spread, most, split=(), kind=jnp.bfloat16):
    gain = block_scale(rng, extent, split, -0.22, 0.18) if split else 1.0
    values = jax.random.normal(rng, extent, jnp.float32) * spread * gain
    return jnp.minimum(jnp.maximum(values, -most), most).astype(kind)


def setup_inputs(seed: int = 0) -> dict:
    key_of = jax.random.split(jax.random.key(seed), 4)
    return {
        "uplift": bell_draw(key_of[0], (NV, NT, NR, PATCH), 1.0, 6.0, ((0, 4), (2, 8))),
        "coefficient": jnp.clip(jnp.exp(math.log(0.24) - 1.3862944 * jax.random.uniform(key_of[1], (NR, PATCH), jnp.float32) ** block_scale(key_of[1], (NR, PATCH), ((0, 8),), -0.2, 0.2)), 0.06, 0.24),
        "transfer": bell_draw(key_of[2], (NF, 2, SENS, NR * PATCH), (2 * NR * PATCH) ** -0.5, 0.0625, ((0, 4), (3, 8)), jnp.float32),
    }


def dft_table(steps_count, freq_count):
    times = jnp.arange(steps_count, dtype=jnp.int32)
    freqs = jnp.arange(freq_count, dtype=jnp.int32)
    phase = (freqs[:, None] * times[None, :] % steps_count).astype(jnp.float32) * (2.0 * math.pi / steps_count)
    scale = 1.0 / math.sqrt(steps_count)
    return jnp.stack([jnp.cos(phase), -jnp.sin(phase)], 1).reshape(2 * freq_count, steps_count) * scale

def smooth(field, coefficient):
    padded = jnp.pad(field, ((0, 0), (1, 1), (1, 1)))
    beside = padded[:, 2:, 1:-1] + padded[:, :-2, 1:-1] + padded[:, 1:-1, 2:] + padded[:, 1:-1, :-2]
    return field + coefficient * (beside - 4.0 * field)

def reference(uplift, coefficient, transfer):
    table = dft_table(NT, NF)

    def one_vector(series):
        field = series.astype(jnp.float32)
        for step in range(PASSES):
            field = smooth(field, coefficient)
        flat = field.reshape(NT, NR * PATCH)
        return jnp.dot(table, flat, precision=lax.Precision.HIGHEST).reshape(NF, 2, NR * PATCH)
    spectra = lax.map(one_vector, uplift)
    by_freq = jnp.transpose(spectra, (1, 0, 2, 3))

    def one_freq(pair):
        spectrum, block = pair
        products = jnp.einsum('vbc,asc->vbas', spectrum, block, precision=lax.Precision.HIGHEST)
        real_part = products[:, 0, 0] - products[:, 1, 1]
        imag_part = products[:, 1, 0] + products[:, 0, 1]
        return jnp.stack([real_part, imag_part], 1)
    result = lax.map(one_freq, (by_freq, transfer))
    return jnp.transpose(result, (1, 0, 2, 3))
```

```python
import functools
import math

import jax
import jax.numpy as jnp
import numpy as np
from jax import lax
from jax.experimental import pallas as pl
from jax.experimental.pallas import tpu as pltpu
from jax.sharding import PartitionSpec as P

FD = 1
PASSES = 3
LANE_GROUP = 8
PHASES = 1


def dft_table(steps_count, freq_count):
    times = np.arange(steps_count)
    freqs = np.arange(freq_count)
    phase = (freqs[:, None] * times[None, :] % steps_count) * (2.0 * math.pi / steps_count)
    scale = 1.0 / math.sqrt(steps_count)
    return (np.stack([np.cos(phase), -np.sin(phase)], 1) * scale).astype(np.float32)


def split_bf16(values):
    high = values.astype(jnp.bfloat16)
    low = (values - high.astype(values.dtype)).astype(jnp.bfloat16)
    return high, low


def transform_operand(steps_count, freq_count, order):
    table = dft_table(steps_count, freq_count)[order]
    eye = np.eye(LANE_GROUP, dtype=np.float32)
    high, low = split_bf16(table)
    parts = np.stack([high.astype(np.float32), low.astype(np.float32)], 1)
    full = np.einsum("fpkbt,vw->fpkbvwt", parts, eye)
    sources = full.shape[0]
    return jnp.asarray(full.reshape(sources, -1, LANE_GROUP * steps_count), jnp.bfloat16)


def transform_kernel(slots, table_ref, field_ref, *outs):
    table = table_ref[lax.axis_index("freq") if table_ref.shape[0] > 1 else 0]
    group, rows, steps, width = field_ref.shape
    data = jnp.concatenate(
        [field_ref[:, r].reshape(group * steps, width) for r in range(rows)], axis=1
    )
    both = jnp.dot(table, data, preferred_element_type=jnp.float32)
    half = both.shape[0] // 2
    values = both[:half] + both[half:]
    for slot in range(slots):
        ref = outs[slot] if len(outs) > 1 else outs[0].at[slot]
        for b in range(2):
            at = (slot * 2 + b) * group
            for r in range(rows):
                ref[b, r] = values[at : at + group, r * width : (r + 1) * width]


def transform(field, table, slots, blocks, separate):
    vectors, rows, steps, width = field.shape
    group = LANE_GROUP
    count = len(blocks)
    if count > 1:
        step = blocks[1] - blocks[0]
    else:
        step = 1
    first = blocks[0]
    if separate:
        shape = [jax.ShapeDtypeStruct((2, rows, count * group, width), jnp.float32)] * slots
        spec = [pl.BlockSpec((2, rows, group, width), lambda i: (0, 0, i, 0))] * slots
    else:
        shape = [jax.ShapeDtypeStruct((slots, 2, rows, count * group, width), jnp.float32)]
        spec = [pl.BlockSpec((slots, 2, rows, group, width), lambda i: (0, 0, 0, i, 0))]
    return pl.pallas_call(
        functools.partial(transform_kernel, slots),
        out_shape=shape,
        grid=(count,),
        in_specs=[
            pl.BlockSpec(table.shape, lambda i: (0, 0, 0)),
            pl.BlockSpec((group, rows, steps, width), lambda i: (first + step * i, 0, 0, 0)),
        ],
        out_specs=spec,
        cost_estimate=pl.CostEstimate(
            flops=2 * table.shape[1] * table.shape[2] * rows * width * count,
            bytes_accessed=count * group * rows * width * (2 * steps + 8 * slots),
            transcendentals=0,
        ),
        name="transform",
    )(table, field)


def split_kernel(x_ref, high_ref, low_ref):
    high, low = split_bf16(x_ref[...])
    high_ref[...] = high
    low_ref[...] = low


def split_transfer(transfer):
    parts, sensors, cells = transfer.shape
    block = pl.BlockSpec((1, sensors, cells), lambda a: (a, 0, 0))
    return pl.pallas_call(
        split_kernel,
        out_shape=[jax.ShapeDtypeStruct(transfer.shape, jnp.bfloat16)] * 2,
        grid=(parts,),
        in_specs=[block],
        out_specs=[block, block],
        cost_estimate=pl.CostEstimate(
            flops=2 * transfer.size, bytes_accessed=8 * transfer.size, transcendentals=0
        ),
        name="split_transfer",
    )(transfer)


def relaxed_rows(rows, coefficients):
    width = rows[0].shape[-1]
    lane = lax.broadcasted_iota(jnp.int32, rows[0].shape, 1)
    first, last = lane == 0, lane == width - 1
    out = []
    for i in range(1, len(rows) - 1):
        centre = rows[i]
        left = jnp.where(first, 0.0, pltpu.roll(centre, 1, 1))
        right = jnp.where(last, 0.0, pltpu.roll(centre, width - 1, 1))
        beside = (rows[i + 1] + rows[i - 1]) + (left + right)
        out.append(centre + coefficients[i - 1] * (beside - 4.0 * centre))
    return out


def smoothed(rows, coefficients):
    count = len(coefficients)
    for step in range(PASSES):
        rows = relaxed_rows(rows, coefficients[step : count - step])
    return rows


def coefficient_rows(low_ref, own_ref, high_ref):
    rim = PASSES - 1
    rows = [low_ref[i : i + 1] for i in range(rim)]
    rows += [own_ref[i : i + 1] for i in range(own_ref.shape[0])]
    return rows + [high_ref[i : i + 1] for i in range(rim)]


def finish_kernel(sources, paired, owners_in, smooth, *refs):
    refs = list(refs)
    chunks = [refs.pop(0) for _ in range(sources)]
    if smooth:
        low, high, own_c, low_c, high_c = (refs.pop(0) for _ in range(5))
        coefficients = coefficient_rows(low_c, own_c, high_c)
    t_high, t_low = refs.pop(0), refs.pop(0)
    outs, held = refs[:-1], refs[-1]
    flat = [(c, None) for c in chunks] if paired else [(chunks[0], g) for g in range(chunks[0].shape[0])]
    width = held.shape[-1] // flat_rows(chunks, paired)
    rows = flat_rows(chunks, paired)
    for index, (ref, at) in enumerate(flat):
        ref = ref if at is None else ref.at[at]
        vectors = ref.shape[2]
        each = vectors // owners_in
        for b in range(2):
            for o in range(owners_in):
                span = slice(o * each, (o + 1) * each)
                values = [ref[b, r, span] for r in range(rows)]
                if smooth:
                    before = [low[index, b, r, span] for r in range(PASSES)]
                    after = [high[index, b, r, span] for r in range(PASSES)]
                    values = smoothed(before + values + after, coefficients)
                if paired:
                    group = lax.axis_index("freq") ^ index
                    apart = (group * owners_in + o) ^ lax.axis_index("seabed")
                    place = (apart & 1) * (held.shape[1] // 2) + (apart >> 1)
                else:
                    place = index * owners_in + o
                for r in range(rows):
                    held[b, place, :, r * width : (r + 1) * width] = values[r]
    places, each, cells = held.shape[1:]
    lhs = held[...].reshape(2 * places * each, cells)
    lhs_high, lhs_low = split_bf16(lhs)

    def times(a):
        def dot(x, w):
            return lax.dot_general(
                x, w, (((1,), (1,)), ((), ())), preferred_element_type=jnp.float32
            )

        return (
            dot(lhs_low, t_high[a]) + dot(lhs_high, t_low[a])
        ) + dot(lhs_high, t_high[a])

    half = places * each
    by_real, by_imag = times(0), times(1)
    real = by_real[:half] - by_imag[half:]
    imag = by_imag[:half] + by_real[half:]
    sensors = real.shape[-1]
    if paired:
        for e in range(2):
            at = slice(e * half // 2, (e + 1) * half // 2)
            outs[e][:, 0] = real[at].reshape(places // 2, each, sensors)
            outs[e][:, 1] = imag[at].reshape(places // 2, each, sensors)
    else:
        outs[0][0] = real
        outs[0][1] = imag


def flat_rows(chunks, paired):
    return chunks[0].shape[1] if paired else chunks[0].shape[2]


def finish(chunks, rims, split, owners_in, paired):
    t_high, t_low = split
    sensors, cells = t_high.shape[1:]
    shape = chunks[0].shape if paired else chunks[0].shape[1:]
    count = len(chunks) if paired else chunks[0].shape[0]
    vectors = count * shape[2]
    places = count * owners_in
    each = vectors // places
    if paired:
        out = [jax.ShapeDtypeStruct((places // 2, 2, each, sensors), jnp.float32)] * 2
    else:
        out = [jax.ShapeDtypeStruct((2, vectors, sensors), jnp.float32)]
    return pl.pallas_call(
        functools.partial(finish_kernel, len(chunks), paired, owners_in, rims is not None),
        out_shape=out,
        scratch_shapes=[pltpu.VMEM((2, places, each, cells), jnp.float32)],
        cost_estimate=pl.CostEstimate(
            flops=24 * vectors * sensors * cells,
            bytes_accessed=8 * sensors * cells + 12 * vectors * cells + 8 * vectors * sensors,
            transcendentals=0,
        ),
        name="finish",
    )(*chunks, *(rims or ()), t_high, t_low)


def chain(count):
    up = [(i, i + 1) for i in range(count - 1)]
    return up, [(b, a) for a, b in up]


def xor_pairs(count, apart):
    return [(i, i ^ apart) for i in range(count)]


def shards(uplift, coefficient, transfer):
    vectors, steps, rows, width = uplift.shape
    freq_count, strips = lax.axis_size("freq"), lax.axis_size("seabed")
    owned = vectors * freq_count // strips
    owners_in = max(1, vectors // owned)
    field = jnp.transpose(uplift, (0, 2, 1, 3))
    up, down = chain(strips)
    paired = (
        owners_in == 2
        and strips == 2 * freq_count
        and strips & (strips - 1) == 0
        and owned % (LANE_GROUP * PHASES) == 0
    )
    rim = PASSES - 1
    low_c = lax.ppermute(coefficient[rows - rim :], "seabed", up)
    high_c = lax.ppermute(coefficient[:rim], "seabed", down)
    split = split_transfer(transfer[0])
    if paired:
        order = np.arange(freq_count)[:, None] ^ np.arange(freq_count)[None, :]
    else:
        order = np.arange(freq_count)[None, :]
    table = transform_operand(steps, freq_count, order)
    blocks = list(range(vectors // LANE_GROUP))
    spectrum = transform(field, table, freq_count, blocks, paired)
    if paired:
        chunks = [spectrum[0]] + [
            lax.ppermute(spectrum[m], "freq", xor_pairs(freq_count, m))
            for m in range(1, freq_count)
        ]
        stacked_low = jnp.stack([c[:, rows - PASSES :] for c in chunks])
        stacked_high = jnp.stack([c[:, :PASSES] for c in chunks])
    else:
        chunks = [lax.all_to_all(spectrum[0], "freq", split_axis=0, concat_axis=0, tiled=True)]
        stacked_low = chunks[0][:, :, rows - PASSES :]
        stacked_high = chunks[0][:, :, :PASSES]
    low = lax.ppermute(stacked_low, "seabed", up)
    high = lax.ppermute(stacked_high, "seabed", down)
    partial = finish(chunks, (low, high, coefficient, low_c, high_c), split, owners_in, paired)
    if paired:
        keep, send = partial
        pair = keep + lax.ppermute(send, "seabed", xor_pairs(strips, 1))
        total = pair[0]
        for d in range(1, strips // 2):
            total = total + lax.ppermute(pair[d], "seabed", xor_pairs(strips, 2 * d))
    else:
        spread = partial[0].reshape(2, strips, owned, -1)
        got = lax.all_to_all(spread, "seabed", split_axis=1, concat_axis=1, tiled=True)
        total = got.sum(1)
    return jnp.transpose(total, (1, 0, 2))[:, None]


def solution(mesh):
    placed = (P("freq", None, "seabed", None), P("seabed", None), P("freq", None, None, "seabed"))
    return jax.shard_map(
        shards,
        mesh=mesh,
        in_specs=placed,
        out_specs=P("seabed", "freq", None, None),
        check_vma=False,
    )
```

```python
import functools
import math

import jax
import jax.numpy as jnp
import numpy as np
from jax import lax
from jax.experimental import pallas as pl
from jax.experimental.pallas import tpu as pltpu
from jax.sharding import PartitionSpec as P


FD = 1
PASSES = 3
GROUP = 8
GRANT = 16 * 1024 * 1024


def params():
    return pltpu.CompilerParams(vmem_limit_bytes=GRANT)


def cost(flops, moved):
    return pl.CostEstimate(flops=flops, bytes_accessed=moved, transcendentals=0)


def dft_table(steps_count, freq_count):
    times = np.arange(steps_count)
    freqs = np.arange(freq_count)
    phase = (freqs[:, None] * times[None, :] % steps_count) * (2.0 * math.pi / steps_count)
    scale = 1.0 / math.sqrt(steps_count)
    return (np.stack([np.cos(phase), -np.sin(phase)], 1) * scale).astype(np.float32)


def split_bf16(values):
    high = values.astype(jnp.bfloat16)
    low = (values - high.astype(values.dtype)).astype(jnp.bfloat16)
    return high, low


def transform_operand(steps_count, freq_count, order):
    table = dft_table(steps_count, freq_count)[order]
    eye = np.eye(GROUP, dtype=np.float32)
    high, low = split_bf16(table)
    parts = np.stack([high.astype(np.float32), low.astype(np.float32)], 1)
    full = np.einsum("fpkbt,vw->fpkbvwt", parts, eye)
    return jnp.asarray(full.reshape(full.shape[0], -1, GROUP * steps_count), jnp.bfloat16)


def transform_kernel(slots, edges, table_ref, field_ref, *outs):
    at_table = lax.axis_index("freq") if table_ref.shape[0] > 1 else 0
    group, rows, steps, width = field_ref.shape
    data = jnp.concatenate(
        [field_ref[:, r].reshape(group * steps, width) for r in range(rows)], axis=1
    )
    both = jnp.dot(table_ref[at_table], data, preferred_element_type=jnp.float32)
    half = both.shape[0] // 2
    values = both[:half] + both[half:]
    i = pl.program_id(0)
    for slot in range(slots):
        for b in range(2):
            at = (slot * 2 + b) * group
            for r in range(rows):
                piece = values[at : at + group, r * width : (r + 1) * width]
                outs[slot][b, r] = piece
                if edges:
                    low, high = outs[slots:]
                    if r >= rows - PASSES:
                        low[slot * 2 + b, r - rows + PASSES, i] = piece
                    if r < PASSES:
                        high[slot * 2 + b, r, i] = piece


def transform(field, table, slots, blocks, edges):
    _, rows, steps, width = field.shape
    count = len(blocks)
    first = blocks[0]
    stride = blocks[1] - first if count > 1 else 1
    shape = [jax.ShapeDtypeStruct((2, rows, count * GROUP, width), jnp.float32)] * slots
    spec = [pl.BlockSpec((2, rows, GROUP, width), lambda i: (0, 0, i, 0))] * slots
    if edges:
        rim = (slots * 2, PASSES, count, GROUP, width)
        shape = shape + [jax.ShapeDtypeStruct(rim, jnp.float32)] * 2
        spec = spec + [pl.BlockSpec(rim, lambda i: (0, 0, 0, 0, 0))] * 2
    return pl.pallas_call(
        functools.partial(transform_kernel, slots, edges),
        out_shape=shape,
        grid=(count,),
        in_specs=[
            pl.BlockSpec(table.shape, lambda i: (0, 0, 0)),
            pl.BlockSpec((GROUP, rows, steps, width), lambda i: (first + stride * i, 0, 0, 0)),
        ],
        out_specs=spec,
        compiler_params=params(),
        cost_estimate=cost(
            2 * table.shape[1] * table.shape[2] * rows * width * count,
            count * GROUP * rows * width * (2 * steps + 8 * slots),
        ),
        name="transform",
    )(table, field)


def split_kernel(x_ref, high_ref, low_ref):
    high, low = split_bf16(x_ref[...])
    high_ref[...] = high
    low_ref[...] = low


def split_transfer(transfer):
    parts, sensors, cells = transfer.shape
    block = pl.BlockSpec((1, sensors, cells), lambda a: (a, 0, 0))
    return pl.pallas_call(
        split_kernel,
        out_shape=[jax.ShapeDtypeStruct(transfer.shape, jnp.bfloat16)] * 2,
        grid=(parts,),
        in_specs=[block],
        out_specs=[block, block],
        compiler_params=params(),
        cost_estimate=cost(2 * transfer.size, 8 * transfer.size),
        name="split_transfer",
    )(transfer)


def relaxed_rows(rows, coefficients):
    width = rows[0].shape[-1]
    lane = lax.broadcasted_iota(jnp.int32, rows[0].shape, 1)
    first, last = lane == 0, lane == width - 1
    out = []
    for i in range(1, len(rows) - 1):
        centre = rows[i]
        left = jnp.where(first, 0.0, pltpu.roll(centre, 1, 1))
        right = jnp.where(last, 0.0, pltpu.roll(centre, width - 1, 1))
        beside = (rows[i + 1] + rows[i - 1]) + (left + right)
        out.append(centre + coefficients[i - 1] * (beside - 4.0 * centre))
    return out


def smooth_kernel(count, *refs):
    chunks, (low, high, own_c, low_c, high_c) = refs[:count], refs[count : count + 5]
    outs = refs[count + 5 :]
    rows, vectors, width = chunks[0].shape[1:]
    rim = PASSES - 1
    coefficients = [low_c[i : i + 1] for i in range(rim)]
    coefficients += [own_c[i : i + 1] for i in range(rows)]
    coefficients += [high_c[i : i + 1] for i in range(rim)]
    coefficients = [jnp.broadcast_to(c, (vectors, width)) for c in coefficients]
    for index in range(count):
        for b in range(2):
            values = [low[index * 2 + b, r] for r in range(PASSES)]
            values += [chunks[index][b, r] for r in range(rows)]
            values += [high[index * 2 + b, r] for r in range(PASSES)]
            for step in range(PASSES):
                values = relaxed_rows(values, coefficients[step : len(coefficients) - step])
            for r in range(rows):
                outs[index][b, r] = values[r]


def smooth(chunks, low, high, coefficients):
    shape = chunks[0].shape
    size = len(chunks) * math.prod(shape)
    return pl.pallas_call(
        functools.partial(smooth_kernel, len(chunks)),
        out_shape=[jax.ShapeDtypeStruct(shape, jnp.float32)] * len(chunks),
        compiler_params=params(),
        cost_estimate=cost(30 * size, 10 * size),
        name="smooth",
    )(*chunks, low, high, *coefficients)


def combine_kernel(chunks_in, owners_in, paired, *refs):
    refs = list(refs)
    phases = [[refs.pop(0) for _ in range(count)] for count in chunks_in]
    t_high, t_low = refs.pop(0), refs.pop(0)
    outs, held = refs[:-1], refs[-1]
    rows, vectors, width = phases[0][0].shape[1:]
    each = vectors // owners_in
    for phase, chunks in enumerate(phases):
        inner = slice(phase * each, (phase + 1) * each)
        for index, ref in enumerate(chunks):
            for o in range(owners_in):
                if paired:
                    owner = (lax.axis_index("freq") ^ index) * owners_in + o
                    apart = owner ^ lax.axis_index("seabed")
                    place = (apart & 1) * (held.shape[1] // 2) + (apart >> 1)
                else:
                    place = index * owners_in + o
                for b in range(2):
                    for r in range(rows):
                        held[b, place, inner, r * width : (r + 1) * width] = ref[
                            b, r, o * each : (o + 1) * each
                        ]
    places, owned, cells = held.shape[1:]
    lhs_high, lhs_low = split_bf16(held[...].reshape(2 * places * owned, cells))

    def times(a):
        def dot(x, w):
            return lax.dot_general(
                x, w, (((1,), (1,)), ((), ())), preferred_element_type=jnp.float32
            )

        return (dot(lhs_low, t_high[a]) + dot(lhs_high, t_low[a])) + dot(lhs_high, t_high[a])

    half = places * owned
    by_real, by_imag = times(0), times(1)
    real = by_real[:half] - by_imag[half:]
    imag = by_imag[:half] + by_real[half:]
    sensors = real.shape[-1]
    share = places // len(outs)
    for e, out in enumerate(outs):
        at = slice(e * share * owned, (e + 1) * share * owned)
        out[:, 0] = real[at].reshape(share, owned, sensors)
        out[:, 1] = imag[at].reshape(share, owned, sensors)


def combine(phases, split, owners_in, paired):
    t_high, t_low = split
    sensors, cells = t_high.shape[1:]
    places = len(phases[0]) * owners_in
    owned = sum(p[0].shape[2] for p in phases) // owners_in
    vectors = places * owned
    outs = 2 if paired else 1
    return pl.pallas_call(
        functools.partial(combine_kernel, [len(p) for p in phases], owners_in, paired),
        out_shape=[jax.ShapeDtypeStruct((places // outs, 2, owned, sensors), jnp.float32)] * outs,
        scratch_shapes=[pltpu.VMEM((2, places, owned, cells), jnp.float32)],
        compiler_params=params(),
        cost_estimate=cost(
            24 * vectors * sensors * cells,
            8 * sensors * cells + 8 * vectors * cells + 16 * vectors * sensors,
        ),
        name="combine",
    )(*[c for p in phases for c in p], t_high, t_low)


def chain(count):
    up = [(i, i + 1) for i in range(count - 1)]
    return up, [(b, a) for a, b in up]


def xor_pairs(count, apart):
    return [(i, i ^ apart) for i in range(count)]


def halo_of(chunks):
    rows, vectors, width = chunks[0].shape[1:]
    last = jnp.stack([c[:, rows - PASSES :] for c in chunks])
    first = jnp.stack([c[:, :PASSES] for c in chunks])
    return [x.reshape(-1, PASSES, vectors, width) for x in (last, first)]


def paired_shards(field, coefficient, split_of, table, freq_count, strips, owned):
    vectors, rows, _, width = field.shape
    rim = PASSES - 1
    up, down = chain(strips)
    blocks = np.arange(vectors // GROUP).reshape(2, 2).T.tolist()

    def exchange(chunks):
        moved = {
            m: lax.ppermute(chunks[m], "freq", xor_pairs(freq_count, m))
            for m in reversed(range(1, freq_count))
        }
        return [chunks[0]] + [moved[m] for m in range(1, freq_count)]

    first = transform(field, table, freq_count, blocks[0], False)
    first = exchange(first)
    *second, last_rows, first_rows = transform(field, table, freq_count, blocks[1], True)
    pad = ((0, GROUP - rim), (0, 0))

    def with_rim(edge, rim_rows):
        flat = edge.reshape(-1, width)
        return jnp.concatenate([flat, jnp.pad(rim_rows, pad)], 0)

    def without_rim(moved):
        edge = moved[:-GROUP].reshape(2 * freq_count, PASSES, -1, width)
        return edge, moved[-GROUP : -GROUP + rim]

    last_rows = with_rim(last_rows, coefficient[rows - rim :])
    first_rows = with_rim(first_rows, coefficient[:rim])
    low = lax.ppermute(last_rows, "seabed", up)
    high = lax.ppermute(first_rows, "seabed", down)
    low, low_c = without_rim(low)
    high, high_c = without_rim(high)
    coefficients = (coefficient, low_c, high_c)
    split = split_of()
    second = smooth(second, low, high, coefficients)
    second = exchange(second)
    last_rows, first_rows = halo_of(first)
    low = lax.ppermute(last_rows, "seabed", up)
    high = lax.ppermute(first_rows, "seabed", down)
    first = smooth(first, low, high, coefficients)
    keep, send = combine([first, second], split, 2, True)
    pair = keep + lax.ppermute(send, "seabed", xor_pairs(strips, 1))
    total = pair[0]
    for d in range(1, strips // 2):
        total = total + lax.ppermute(pair[d], "seabed", xor_pairs(strips, 2 * d))
    return total


def plain_shards(field, coefficient, split_of, table, freq_count, strips, owned):
    vectors, rows, _, _ = field.shape
    rim = PASSES - 1
    up, down = chain(strips)
    blocks = list(range(vectors // GROUP))
    spectrum = jnp.stack(transform(field, table, freq_count, blocks, False))
    spectrum = lax.all_to_all(spectrum, "freq", split_axis=0, concat_axis=0, tiled=True)
    chunks = list(spectrum)
    last_rows, first_rows = halo_of(chunks)
    low = lax.ppermute(last_rows, "seabed", up)
    high = lax.ppermute(first_rows, "seabed", down)
    low_c = lax.ppermute(coefficient[rows - rim :], "seabed", up)
    high_c = lax.ppermute(coefficient[:rim], "seabed", down)
    chunks = smooth(chunks, low, high, (coefficient, low_c, high_c))
    (partial,) = combine([chunks], split_of(), vectors // owned, False)
    got = lax.all_to_all(partial, "seabed", split_axis=0, concat_axis=0, tiled=True)
    return got.sum(0)


def shards(uplift, coefficient, transfer):
    vectors, steps, _, _ = uplift.shape
    freq_count, strips = FD * lax.axis_size("freq"), lax.axis_size("seabed")
    owned = vectors * freq_count // strips
    paired = (
        strips == 2 * freq_count
        and strips & (strips - 1) == 0
        and vectors == 2 * owned
        and owned == 2 * GROUP
    )
    slots = np.arange(freq_count)
    order = slots[:, None] ^ slots[None, :] if paired else slots[None, :]
    table = transform_operand(steps, freq_count, order)
    field = jnp.transpose(uplift, (0, 2, 1, 3))
    run = paired_shards if paired else plain_shards
    total = run(
        field,
        coefficient,
        lambda: split_transfer(transfer[0]),
        table,
        freq_count,
        strips,
        owned,
    )
    return jnp.transpose(total, (1, 0, 2))[:, None]


def solution(mesh):
    placed = (P("freq", None, "seabed", None), P("seabed", None), P("freq", None, None, "seabed"))
    return jax.shard_map(
        shards,
        mesh=mesh,
        in_specs=placed,
        out_specs=P("seabed", "freq", None, None),
        check_vma=False,
    )
```

```python
import functools
import math

import jax
import jax.numpy as jnp
import numpy as np
from jax import lax
from jax.experimental import pallas as pl
from jax.experimental.pallas import tpu as pltpu
from jax.sharding import PartitionSpec as P


FD = 1
PASSES = 3
GROUP = 8
GRANT = 16 * 1024 * 1024


def params():
    return pltpu.CompilerParams(vmem_limit_bytes=GRANT)


def cost(flops, moved):
    return pl.CostEstimate(flops=flops, bytes_accessed=moved, transcendentals=0)


def dft_table(steps_count, freq_count):
    times = np.arange(steps_count)
    freqs = np.arange(freq_count)
    phase = (freqs[:, None] * times[None, :] % steps_count) * (2.0 * math.pi / steps_count)
    scale = 1.0 / math.sqrt(steps_count)
    return (np.stack([np.cos(phase), -np.sin(phase)], 1) * scale).astype(np.float32)


def split_bf16(values):
    high = values.astype(jnp.bfloat16)
    low = (values - high.astype(values.dtype)).astype(jnp.bfloat16)
    return high, low


def transform_operand(steps_count, freq_count, order):
    table = dft_table(steps_count, freq_count)[order]
    parts = np.stack([x.astype(np.float32) for x in split_bf16(table)], 1)
    sources = parts.shape[0]
    wide = np.broadcast_to(parts[..., None, :], (*parts.shape[:-1], GROUP, steps_count))
    return jnp.asarray(wide.reshape(sources, -1, GROUP * steps_count), jnp.float32)


def edge_base(slot, b, r, vectors):
    return ((slot * 2 + b) * PASSES + r) * vectors


def transform_kernel(slots, edged, field_hbm, table_hbm, own_hbm, *refs):
    outs, (low, high) = refs[:slots], refs[slots : slots + 2]
    field, table, own_c, field_sem, table_sem, own_sem = refs[slots + 2 :]
    vectors, rows, steps, width = field.shape
    blocks = vectors // GROUP
    source = lax.axis_index("freq") if table_hbm.shape[0] > 1 else 0
    get_table = pltpu.make_async_copy(table_hbm.at[source], table, table_sem)
    get_table.start()
    get_own = pltpu.make_async_copy(own_hbm, own_c, own_sem)
    get_own.start()

    def get(i):
        at = pl.ds(i * GROUP, GROUP)
        return pltpu.make_async_copy(field_hbm.at[at], field.at[at], field_sem.at[i])

    for i in range(blocks):
        get(i).start()
    get_own.wait()
    rim = PASSES - 1
    base = edge_base(edged, 0, 0, vectors)
    low[base : base + rim] = own_c[rows - rim :]
    high[base : base + rim] = own_c[:rim]
    low[base + rim :] = jnp.zeros((low.shape[0] - base - rim, width), jnp.float32)
    high[base + rim :] = jnp.zeros((low.shape[0] - base - rim, width), jnp.float32)
    get_table.wait()
    short = table[...]
    shape = (short.shape[0], GROUP, short.shape[1])
    mine = lax.broadcasted_iota(jnp.int32, shape, 1)
    column = lax.broadcasted_iota(jnp.int32, shape, 2)
    full = jnp.where(
        (column >= mine * steps) & (column < (mine + 1) * steps), short[:, None], 0.0
    )
    full = full.reshape(-1, short.shape[1]).astype(jnp.bfloat16)
    for i in range(blocks):
        get(i).wait()
        span = slice(i * GROUP, (i + 1) * GROUP)
        data = jnp.concatenate(
            [field[span, r].reshape(GROUP * steps, width) for r in range(rows)], axis=1
        )
        both = jnp.dot(full, data, preferred_element_type=jnp.float32)
        half = both.shape[0] // 2
        values = both[:half] + both[half:]
        for slot in range(slots):
            for b in range(2):
                at = (slot * 2 + b) * GROUP
                for r in range(rows):
                    piece = values[at : at + GROUP, r * width : (r + 1) * width]
                    outs[slot][b, r, span] = piece
                    if slot >= edged:
                        continue
                    if r >= rows - PASSES:
                        to = edge_base(slot, b, r - rows + PASSES, vectors) + i * GROUP
                        low[to : to + GROUP] = piece
                    if r < PASSES:
                        to = edge_base(slot, b, r, vectors) + i * GROUP
                        high[to : to + GROUP] = piece


def transform(field, table, coefficient, slots, edged):
    vectors, rows, steps, width = field.shape
    chunk = jax.ShapeDtypeStruct((2, rows, vectors, width), jnp.float32)
    edge = jax.ShapeDtypeStruct((edge_base(edged, 0, 0, vectors) + GROUP, width), jnp.float32)
    hbm = pl.BlockSpec(memory_space=pltpu.HBM)
    vmem = pl.BlockSpec(memory_space=pltpu.VMEM)
    *chunks, low, high = pl.pallas_call(
        functools.partial(transform_kernel, slots, edged),
        out_shape=[chunk] * slots + [edge] * 2,
        in_specs=[hbm, hbm, hbm],
        out_specs=[vmem] * (slots + 2),
        scratch_shapes=[
            pltpu.VMEM(field.shape, field.dtype),
            pltpu.VMEM(table.shape[1:], table.dtype),
            pltpu.VMEM(coefficient.shape, coefficient.dtype),
            pltpu.SemaphoreType.DMA((vectors // GROUP,)),
            pltpu.SemaphoreType.DMA(()),
            pltpu.SemaphoreType.DMA(()),
        ],
        compiler_params=params(),
        cost_estimate=cost(
            2 * table.shape[1] * table.shape[2] * rows * width * vectors,
            vectors * rows * width * (2 * steps + 8 * slots),
        ),
        name="transform",
    )(*(pltpu.with_memory_space_constraint(x, pltpu.HBM) for x in (field, table, coefficient)))
    return chunks, low, high


def split_kernel(x_ref, high_ref, low_ref):
    high, low = split_bf16(x_ref[...])
    high_ref[...] = high
    low_ref[...] = low


def split_transfer(transfer):
    parts, sensors, cells = transfer.shape
    block = pl.BlockSpec((1, sensors, cells), lambda a: (a, 0, 0))
    return pl.pallas_call(
        split_kernel,
        out_shape=[jax.ShapeDtypeStruct(transfer.shape, jnp.bfloat16)] * 2,
        grid=(parts,),
        in_specs=[block],
        out_specs=[block, block],
        compiler_params=params(),
        cost_estimate=cost(2 * transfer.size, 8 * transfer.size),
        name="split_transfer",
    )(transfer)


def relaxed_rows(rows, coefficients):
    width = rows[0].shape[-1]
    lane = lax.broadcasted_iota(jnp.int32, rows[0].shape, 1)
    first, last = lane == 0, lane == width - 1
    out = []
    for i in range(1, len(rows) - 1):
        centre = rows[i]
        left = jnp.where(first, 0.0, pltpu.roll(centre, 1, 1))
        right = jnp.where(last, 0.0, pltpu.roll(centre, width - 1, 1))
        beside = (rows[i + 1] + rows[i - 1]) + (left + right)
        out.append(centre + coefficients[i - 1] * (beside - 4.0 * centre))
    return out


def smooth_kernel(base, rim_base, chunk, low, high, own_c, low_c, high_c, out):
    _, rows, vectors, width = chunk.shape
    rim = PASSES - 1
    coefficients = [low_c[rim_base + i : rim_base + i + 1] for i in range(rim)]
    coefficients += [own_c[i : i + 1] for i in range(rows)]
    coefficients += [high_c[rim_base + i : rim_base + i + 1] for i in range(rim)]
    part = math.gcd(vectors, 2 * GROUP)
    coefficients = [jnp.broadcast_to(c, (part, width)) for c in coefficients]
    for b in range(2):
        for start in range(0, vectors, part):
            span = slice(start, start + part)

            def edge(ref, r):
                at = base + edge_base(0, b, r, vectors) + start
                return ref[at : at + part]

            values = [edge(low, r) for r in range(PASSES)]
            values += [chunk[b, r, span] for r in range(rows)]
            values += [edge(high, r) for r in range(PASSES)]
            for step in range(PASSES):
                values = relaxed_rows(values, coefficients[step : len(coefficients) - step])
            for r in range(rows):
                out[b, r, span] = values[r]


def smooth(chunk, low, high, slot, coefficients, rim_base):
    base = edge_base(slot, 0, 0, chunk.shape[2])
    return pl.pallas_call(
        functools.partial(smooth_kernel, base, rim_base),
        out_shape=jax.ShapeDtypeStruct(chunk.shape, jnp.float32),
        compiler_params=params(),
        cost_estimate=cost(30 * chunk.size, 10 * chunk.size),
        name="smooth",
    )(chunk, low, high, *coefficients)


def combine_kernel(chunks_in, owners_in, paired, *refs):
    refs = list(refs)
    phases = [[refs.pop(0) for _ in range(count)] for count in chunks_in]
    t_high, t_low = refs.pop(0), refs.pop(0)
    outs, held = refs[:-1], refs[-1]
    rows, vectors, width = phases[0][0].shape[1:]
    each = vectors // owners_in
    for phase, chunks in enumerate(phases):
        inner = slice(phase * each, (phase + 1) * each)
        for index, ref in enumerate(chunks):
            for o in range(owners_in):
                if paired:
                    owner = (lax.axis_index("freq") ^ index) * owners_in + o
                    apart = owner ^ lax.axis_index("seabed")
                    place = (apart & 1) * (held.shape[1] // 2) + (apart >> 1)
                else:
                    place = index * owners_in + o
                for b in range(2):
                    for r in range(rows):
                        held[b, place, inner, r * width : (r + 1) * width] = ref[
                            b, r, o * each : (o + 1) * each
                        ]
    places, owned, cells = held.shape[1:]
    lhs_high, lhs_low = split_bf16(held[...].reshape(2 * places * owned, cells))

    def times(a):
        def dot(x, w):
            return lax.dot_general(
                x, w, (((1,), (1,)), ((), ())), preferred_element_type=jnp.float32
            )

        return (dot(lhs_low, t_high[a]) + dot(lhs_high, t_low[a])) + dot(lhs_high, t_high[a])

    half = places * owned
    by_real, by_imag = times(0), times(1)
    real = by_real[:half] - by_imag[half:]
    imag = by_imag[:half] + by_real[half:]
    sensors = real.shape[-1]
    share = places // len(outs)
    for e, out in enumerate(outs):
        at = slice(e * share * owned, (e + 1) * share * owned)
        out[:, 0] = real[at].reshape(share, owned, sensors)
        out[:, 1] = imag[at].reshape(share, owned, sensors)


def combine(phases, split, owners_in, paired):
    t_high, t_low = split
    sensors, cells = t_high.shape[1:]
    places = len(phases[0]) * owners_in
    owned = sum(p[0].shape[2] for p in phases) // owners_in
    vectors = places * owned
    outs = 2 if paired else 1
    return pl.pallas_call(
        functools.partial(combine_kernel, [len(p) for p in phases], owners_in, paired),
        out_shape=[jax.ShapeDtypeStruct((places // outs, 2, owned, sensors), jnp.float32)] * outs,
        scratch_shapes=[pltpu.VMEM((2, places, owned, cells), jnp.float32)],
        compiler_params=params(),
        cost_estimate=cost(
            24 * vectors * sensors * cells,
            8 * sensors * cells + 8 * vectors * cells + 16 * vectors * sensors,
        ),
        name="combine",
    )(*[c for p in phases for c in p], t_high, t_low)


def chain(count):
    up = [(i, i + 1) for i in range(count - 1)]
    return up, [(b, a) for a, b in up]


def xor_pairs(count, apart):
    return [(i, i ^ apart) for i in range(count)]


def edges_of(chunk):
    _, rows, _, width = chunk.shape
    return [x.reshape(-1, width) for x in (chunk[:, rows - PASSES :], chunk[:, :PASSES])]


def shifted(low, high, strips):
    up, down = chain(strips)
    return lax.ppermute(low, "seabed", up), lax.ppermute(high, "seabed", down)


def paired_shards(field, coefficient, split_of, table, freq_count, strips, owned):
    vectors = field.shape[0]
    last = freq_count - 1
    chunks, low, high = transform(field, table, coefficient, freq_count, last)
    low, high = shifted(low, high, strips)

    def exchange(m, chunk):
        return lax.ppermute(chunk, "freq", xor_pairs(freq_count, m))

    moved = {last: exchange(last, chunks[last])}
    split = split_of()
    coefficients = (coefficient, low, high)
    rim_base = edge_base(last, 0, 0, vectors)
    for m in reversed(range(last)):
        chunk = smooth(chunks[m], low, high, m, coefficients, rim_base)
        moved[m] = exchange(m, chunk) if m else chunk
    low, high = shifted(*edges_of(moved[last]), strips)
    moved[last] = smooth(moved[last], low, high, 0, coefficients, rim_base)
    keep, send = combine([[moved[m] for m in range(freq_count)]], split, 2, True)
    pair = keep + lax.ppermute(send, "seabed", xor_pairs(strips, 1))
    total = pair[0]
    for d in reversed(range(1, strips // 2)):
        total = total + lax.ppermute(pair[d], "seabed", xor_pairs(strips, 2 * d))
    return total


def plain_shards(field, coefficient, split_of, table, freq_count, strips, owned):
    vectors, rows = field.shape[:2]
    spectrum, _, _ = transform(field, table, coefficient, freq_count, 0)
    spectrum = jnp.stack(spectrum)
    spectrum = lax.all_to_all(spectrum, "freq", split_axis=0, concat_axis=0, tiled=True)
    chunks = list(spectrum)
    edges = [jnp.concatenate(e) for e in zip(*[edges_of(c) for c in chunks])]
    low, high = shifted(*edges, strips)
    rim = PASSES - 1
    coefficients = (
        coefficient,
        *shifted(coefficient[rows - rim :], coefficient[:rim], strips),
    )
    chunks = [smooth(c, low, high, i, coefficients, 0) for i, c in enumerate(chunks)]
    (partial,) = combine([chunks], split_of(), vectors // owned, False)
    got = lax.all_to_all(partial, "seabed", split_axis=0, concat_axis=0, tiled=True)
    return got.sum(0)


def shards(uplift, coefficient, transfer):
    vectors, steps, _, _ = uplift.shape
    freq_count, strips = FD * lax.axis_size("freq"), lax.axis_size("seabed")
    owned = vectors * freq_count // strips
    paired = (
        strips == 2 * freq_count
        and strips & (strips - 1) == 0
        and vectors == 2 * owned
        and owned == 2 * GROUP
    )
    slots = np.arange(freq_count)
    order = slots[:, None] ^ slots[None, :] if paired else slots[None, :]
    table = transform_operand(steps, freq_count, order)
    field = jnp.transpose(uplift, (0, 2, 1, 3))
    run = paired_shards if paired else plain_shards
    total = run(
        field,
        coefficient,
        lambda: split_transfer(transfer[0]),
        table,
        freq_count,
        strips,
        owned,
    )
    return jnp.transpose(total, (1, 0, 2))[:, None]


def solution(mesh):
    placed = (P("freq", None, "seabed", None), P("seabed", None), P("freq", None, None, "seabed"))
    return jax.shard_map(
        shards,
        mesh=mesh,
        in_specs=placed,
        out_specs=P("seabed", "freq", None, None),
        check_vma=False,
    )
```

```python
import functools
import math

import jax
import jax.numpy as jnp
import numpy as np
from jax import lax
from jax.experimental import pallas as pl
from jax.experimental.pallas import tpu as pltpu
from jax.sharding import PartitionSpec as P


FD = 1
PASSES = 3
GROUP = 8
GRANT = 16 * 1024 * 1024


def params():
    return pltpu.CompilerParams(vmem_limit_bytes=GRANT)


def cost(flops, moved):
    return pl.CostEstimate(flops=flops, bytes_accessed=moved, transcendentals=0)


def in_hbm(array):
    return pltpu.with_memory_space_constraint(array, pltpu.HBM)


def even_strip():
    return lax.rem(lax.axis_index("seabed"), 2) == 0


def pick(flag, one, other):
    return jnp.where(jnp.full(one.shape, flag), one, other)


def dft_table(steps_count, freq_count):
    times = np.arange(steps_count)
    freqs = np.arange(freq_count)
    phase = (freqs[:, None] * times[None, :] % steps_count) * (2.0 * math.pi / steps_count)
    scale = 1.0 / math.sqrt(steps_count)
    return (np.stack([np.cos(phase), -np.sin(phase)], 1) * scale).astype(np.float32)


def split_bf16(values):
    high = values.astype(jnp.bfloat16)
    low = (values - high.astype(values.dtype)).astype(jnp.bfloat16)
    return high, low


def transform_operand(steps_count, freq_count, order):
    table = dft_table(steps_count, freq_count)[order]
    parts = np.stack([x.astype(np.float32) for x in split_bf16(table)], 1)
    sources = parts.shape[0]
    wide = np.broadcast_to(parts[..., None, :], (*parts.shape[:-1], GROUP, steps_count))
    return jnp.asarray(wide.reshape(sources, -1, GROUP * steps_count), jnp.float32)


def edge_base(slot, b, r, vectors):
    return ((slot * 2 + b) * PASSES + r) * vectors


def transform_kernel(slots, edged, field_hbm, table_hbm, own_hbm, *refs):
    outs, (pair, cross) = refs[:slots], refs[slots : slots + 2]
    field, table, own_c, field_sem, table_sem, own_sem = refs[slots + 2 :]
    vectors, rows, steps, width = field.shape
    blocks = vectors // GROUP
    even = even_strip()
    source = lax.axis_index("freq") if table_hbm.shape[0] > 1 else 0
    get_table = pltpu.make_async_copy(table_hbm.at[source], table, table_sem)
    get_table.start()
    get_own = pltpu.make_async_copy(own_hbm, own_c, own_sem)
    get_own.start()

    def get(i):
        at = pl.ds(i * GROUP, GROUP)
        return pltpu.make_async_copy(field_hbm.at[at], field.at[at], field_sem.at[i])

    for i in range(blocks):
        get(i).start()
    get_own.wait()
    rim = PASSES - 1
    base = edge_base(len(edged), 0, 0, vectors)
    last_c, first_c = own_c[rows - rim :], own_c[:rim]
    pad = jnp.zeros((pair.shape[0] - base - rim, width), jnp.float32)
    for ref, one, other in ((pair, last_c, first_c), (cross, first_c, last_c)):
        ref[base : base + rim] = pick(even, one, other)
        ref[base + rim :] = pad
    get_table.wait()
    short = table[...]
    shape = (short.shape[0], GROUP, short.shape[1])
    mine = lax.broadcasted_iota(jnp.int32, shape, 1)
    column = lax.broadcasted_iota(jnp.int32, shape, 2)
    full = jnp.where(
        (column >= mine * steps) & (column < (mine + 1) * steps), short[:, None], 0.0
    )
    full = full.reshape(-1, short.shape[1]).astype(jnp.bfloat16)
    for i in range(blocks):
        get(i).wait()
        span = slice(i * GROUP, (i + 1) * GROUP)
        data = jnp.concatenate(
            [field[span, r].reshape(GROUP * steps, width) for r in range(rows)], axis=1
        )
        both = jnp.dot(full, data, preferred_element_type=jnp.float32)
        half = both.shape[0] // 2
        values = both[:half] + both[half:]
        for slot in range(slots):
            for b in range(2):
                at = (slot * 2 + b) * GROUP
                for r in range(rows):
                    piece = values[at : at + GROUP, r * width : (r + 1) * width]
                    outs[slot][b, r, span] = piece
                if slot not in edged:
                    continue
                for r in range(PASSES):
                    row = (rows - PASSES + r) * width
                    last = values[at : at + GROUP, row : row + width]
                    first = values[at : at + GROUP, r * width : (r + 1) * width]
                    to = edge_base(edged.index(slot), b, r, vectors) + i * GROUP
                    pair[to : to + GROUP] = pick(even, last, first)
                    cross[to : to + GROUP] = pick(even, first, last)


def transform(field, table, coefficient, slots, edged):
    vectors, rows, steps, width = field.shape
    chunk = jax.ShapeDtypeStruct((2, rows, vectors, width), jnp.float32)
    edge = jax.ShapeDtypeStruct((edge_base(len(edged), 0, 0, vectors) + GROUP, width), jnp.float32)
    hbm = pl.BlockSpec(memory_space=pltpu.HBM)
    vmem = pl.BlockSpec(memory_space=pltpu.VMEM)
    *chunks, pair, cross = pl.pallas_call(
        functools.partial(transform_kernel, slots, edged),
        out_shape=[chunk] * slots + [edge] * 2,
        in_specs=[hbm, hbm, hbm],
        out_specs=[vmem] * (slots + 2),
        scratch_shapes=[
            pltpu.VMEM(field.shape, field.dtype),
            pltpu.VMEM(table.shape[1:], table.dtype),
            pltpu.VMEM(coefficient.shape, coefficient.dtype),
            pltpu.SemaphoreType.DMA((vectors // GROUP,)),
            pltpu.SemaphoreType.DMA(()),
            pltpu.SemaphoreType.DMA(()),
        ],
        compiler_params=params(),
        cost_estimate=cost(
            2 * table.shape[1] * table.shape[2] * rows * width * vectors,
            vectors * rows * width * (2 * steps + 8 * slots),
        ),
        name="transform",
    )(*map(in_hbm, (field, table, coefficient)))
    return chunks, pair, cross


def split_kernel(x_ref, high_ref, low_ref):
    high, low = split_bf16(x_ref[...])
    high_ref[...] = high
    low_ref[...] = low


def split_transfer(transfer):
    parts, sensors, cells = transfer.shape
    block = pl.BlockSpec((1, sensors, cells), lambda a: (a, 0, 0))
    return pl.pallas_call(
        split_kernel,
        out_shape=[jax.ShapeDtypeStruct(transfer.shape, jnp.bfloat16)] * 2,
        grid=(parts,),
        in_specs=[block],
        out_specs=[block, block],
        compiler_params=params(),
        cost_estimate=cost(2 * transfer.size, 8 * transfer.size),
        name="split_transfer",
    )(in_hbm(transfer))


def relaxed_rows(rows, coefficients):
    width = rows[0].shape[-1]
    lane = lax.broadcasted_iota(jnp.int32, rows[0].shape, 1)
    first, last = lane == 0, lane == width - 1
    out = []
    for i in range(1, len(rows) - 1):
        centre = rows[i]
        left = jnp.where(first, 0.0, pltpu.roll(centre, 1, 1))
        right = jnp.where(last, 0.0, pltpu.roll(centre, width - 1, 1))
        beside = (rows[i + 1] + rows[i - 1]) + (left + right)
        out.append(centre + coefficients[i - 1] * (beside - 4.0 * centre))
    return out


def edges_kernel(count, *refs):
    chunks, (pair, cross) = refs[:count], refs[count:]
    _, rows, vectors, _ = chunks[0].shape
    even = even_strip().astype(jnp.int32)
    for index, chunk in enumerate(chunks):
        for ref, start in ((pair, even), (cross, 1 - even)):
            for b in range(2):
                for r in range(PASSES):
                    at = edge_base(index, b, r, vectors)
                    ref[at : at + vectors] = chunk[b, start * (rows - PASSES) + r]


def edges(chunks):
    _, _, vectors, width = chunks[0].shape
    shape = (edge_base(len(chunks), 0, 0, vectors), width)
    return pl.pallas_call(
        functools.partial(edges_kernel, len(chunks)),
        out_shape=[jax.ShapeDtypeStruct(shape, jnp.float32)] * 2,
        compiler_params=params(),
        cost_estimate=cost(0, 16 * shape[0] * width),
        name="edges",
    )(*chunks)


def smooth_kernel(base, rim_base, chunk, pair, cross, own_c, pair_c, cross_c, out):
    _, rows, vectors, width = chunk.shape
    rim = PASSES - 1
    even = even_strip()
    part = math.gcd(vectors, 2 * GROUP)

    def rims(one, other):
        return pick(even, one, other), pick(even, other, one)

    at_c = slice(rim_base, rim_base + rim)
    high_c, low_c = rims(pair_c[at_c], cross_c[at_c])
    coefficients = [low_c[i : i + 1] for i in range(rim)]
    coefficients += [own_c[i : i + 1] for i in range(rows)]
    coefficients += [high_c[i : i + 1] for i in range(rim)]
    coefficients = [jnp.broadcast_to(c, (part, width)) for c in coefficients]
    for b in range(2):
        for start in range(0, vectors, part):
            span = slice(start, start + part)
            low, high = [], []
            for r in range(PASSES):
                at = base + edge_base(0, b, r, vectors) + start
                above, below = rims(pair[at : at + part], cross[at : at + part])
                high.append(above)
                low.append(below)
            values = low + [chunk[b, r, span] for r in range(rows)] + high
            for step in range(PASSES):
                values = relaxed_rows(values, coefficients[step : len(coefficients) - step])
            for r in range(rows):
                out[b, r, span] = values[r]


def smooth(chunk, pair, cross, slot, coefficients, rim_base):
    base = edge_base(slot, 0, 0, chunk.shape[2])
    return pl.pallas_call(
        functools.partial(smooth_kernel, base, rim_base),
        out_shape=jax.ShapeDtypeStruct(chunk.shape, jnp.float32),
        compiler_params=params(),
        cost_estimate=cost(30 * chunk.size, 10 * chunk.size),
        name="smooth",
    )(chunk, pair, cross, *coefficients)


def combine_kernel(chunks_in, owners_in, paired, *refs):
    refs = list(refs)
    phases = [[refs.pop(0) for _ in range(count)] for count in chunks_in]
    t_high, t_low = refs.pop(0), refs.pop(0)
    outs, held = refs[:-1], refs[-1]
    rows, vectors, width = phases[0][0].shape[1:]
    each = vectors // owners_in
    for phase, chunks in enumerate(phases):
        inner = slice(phase * each, (phase + 1) * each)
        for index, ref in enumerate(chunks):
            for o in range(owners_in):
                if paired:
                    owner = (lax.axis_index("freq") ^ index) * owners_in + o
                    apart = owner ^ lax.axis_index("seabed")
                    x, y = (apart >> 1) & 1, apart >> 2
                    early, late = jnp.where(owner % 2 == 0, x, y), jnp.where(owner % 2 == 0, y, x)
                    place = (apart & 1) * 4 + early * 2 + late
                else:
                    place = index * owners_in + o
                for b in range(2):
                    for r in range(rows):
                        held[b, place, inner, r * width : (r + 1) * width] = ref[
                            b, r, o * each : (o + 1) * each
                        ]
    places, owned, cells = held.shape[1:]
    lhs_high, lhs_low = split_bf16(held[...].reshape(2 * places * owned, cells))

    def times(a):
        def dot(x, w):
            return lax.dot_general(
                x, w, (((1,), (1,)), ((), ())), preferred_element_type=jnp.float32
            )

        return (dot(lhs_low, t_high[a]) + dot(lhs_high, t_low[a])) + dot(lhs_high, t_high[a])

    half = places * owned
    by_real, by_imag = times(0), times(1)
    real = by_real[:half] - by_imag[half:]
    imag = by_imag[:half] + by_real[half:]
    sensors = real.shape[-1]
    share = places // len(outs)
    for e, out in enumerate(outs):
        at = slice(e * share * owned, (e + 1) * share * owned)
        out[:, 0] = real[at].reshape(share, owned, sensors)
        out[:, 1] = imag[at].reshape(share, owned, sensors)


def combine(phases, split, owners_in, paired):
    t_high, t_low = split
    sensors, cells = t_high.shape[1:]
    places = len(phases[0]) * owners_in
    owned = sum(p[0].shape[2] for p in phases) // owners_in
    vectors = places * owned
    outs = 2 if paired else 1
    return pl.pallas_call(
        functools.partial(combine_kernel, [len(p) for p in phases], owners_in, paired),
        out_shape=[jax.ShapeDtypeStruct((places // outs, 2, owned, sensors), jnp.float32)] * outs,
        scratch_shapes=[pltpu.VMEM((2, places, owned, cells), jnp.float32)],
        compiler_params=params(),
        cost_estimate=cost(
            24 * vectors * sensors * cells,
            8 * sensors * cells + 8 * vectors * cells + 16 * vectors * sensors,
        ),
        name="combine",
    )(*[c for p in phases for c in p], t_high, t_low)


def xor_pairs(count, apart):
    return [(i, i ^ apart) for i in range(count)]


def neighbours(pair, cross, strips):
    inner = [(i, i + 1) for i in range(1, strips - 1, 2)]
    inner = inner + [(b, a) for a, b in inner]
    cross = lax.ppermute(cross, "seabed", inner)
    pair = lax.ppermute(pair, "seabed", xor_pairs(strips, 1))
    return pair, cross


def paired_shards(field, coefficient, split_of, table, freq_count, strips):
    vectors = field.shape[0]
    chunks, pair, cross = transform(field, table, coefficient, freq_count, (2, 0))

    def swap(m, chunk):
        return lax.ppermute(chunk, "freq", xor_pairs(freq_count, m))

    def relax(chunk, edge, slot):
        return smooth(chunk, *edge, slot, coefficients, rim_base)

    third = swap(3, chunks[3])
    edge = neighbours(pair, cross, strips)
    first = swap(1, chunks[1])
    split = split_of()
    coefficients = (coefficient, *edge)
    rim_base = edge_base(2, 0, 0, vectors)
    second = swap(2, relax(chunks[2], edge, 0))
    own = relax(chunks[0], edge, 1)
    edge = neighbours(*edges([third, first]), strips)
    third = relax(third, edge, 0)
    first = relax(first, edge, 1)
    keep, send = combine([[own, first, second, third]], split, 2, True)
    total = keep + lax.ppermute(send, "seabed", xor_pairs(strips, 1))
    for hop in range(2):
        half = total.shape[0] // 2
        apart = [(i, i ^ (2 if i % 2 == hop else 4)) for i in range(strips)]
        total = total[:half] + lax.ppermute(total[half:], "seabed", apart)
    return total[0]


def plain_shards(field, coefficient, split_of, table, freq_count, strips):
    vectors, rows = field.shape[:2]
    spectrum, _, _ = transform(field, table, coefficient, freq_count, ())
    spectrum = jnp.stack(spectrum)
    spectrum = lax.all_to_all(spectrum, "freq", split_axis=0, concat_axis=0, tiled=True)
    chunks = list(spectrum)
    rim = PASSES - 1
    even = even_strip()
    first_c, last_c = coefficient[:rim], coefficient[rows - rim :]
    pair_c, cross_c = pick(even, last_c, first_c), pick(even, first_c, last_c)
    coefficients = (coefficient, *neighbours(pair_c, cross_c, strips))
    edge = neighbours(*edges(chunks), strips)
    chunks = [smooth(c, *edge, i, coefficients, 0) for i, c in enumerate(chunks)]
    owners_in = vectors * freq_count // strips
    (partial,) = combine([chunks], split_of(), vectors // owners_in, False)
    got = lax.all_to_all(partial, "seabed", split_axis=0, concat_axis=0, tiled=True)
    return got.sum(0)


def shards(uplift, coefficient, transfer):
    vectors, steps, _, _ = uplift.shape
    freq_count, strips = FD * lax.axis_size("freq"), lax.axis_size("seabed")
    owned = vectors * freq_count // strips
    paired = (
        strips == 8
        and freq_count == 4
        and vectors == 2 * owned
        and owned == 2 * GROUP
    )
    slots = np.arange(freq_count)
    order = slots[:, None] ^ slots[None, :] if paired else slots[None, :]
    table = transform_operand(steps, freq_count, order)
    field = jnp.transpose(uplift, (0, 2, 1, 3))
    run = paired_shards if paired else plain_shards
    total = run(
        field,
        coefficient,
        lambda: split_transfer(transfer[0]),
        table,
        freq_count,
        strips,
    )
    return jnp.transpose(total, (1, 0, 2))[:, None]


def solution(mesh):
    placed = (P("freq", None, "seabed", None), P("seabed", None), P("freq", None, None, "seabed"))
    return jax.shard_map(
        shards,
        mesh=mesh,
        in_specs=placed,
        out_specs=P("seabed", "freq", None, None),
        check_vma=False,
    )
```

```python
import functools
import math

import jax
import jax.numpy as jnp
import numpy as np
from jax import lax
from jax.experimental import pallas as pl
from jax.experimental.pallas import tpu as pltpu
from jax.sharding import PartitionSpec as P


FD = 1
PASSES = 3
GROUP = 8
GRANT = 16 * 1024 * 1024


def params():
    return pltpu.CompilerParams(vmem_limit_bytes=GRANT)


def cost(flops, moved):
    return pl.CostEstimate(flops=flops, bytes_accessed=moved, transcendentals=0)


def in_hbm(array):
    return pltpu.with_memory_space_constraint(array, pltpu.HBM)


def even_strip():
    return lax.rem(lax.axis_index("seabed"), 2) == 0


def pick(flag, one, other):
    return jnp.where(jnp.full(one.shape, flag), one, other)


def dft_table(steps_count, freq_count):
    times = np.arange(steps_count)
    freqs = np.arange(freq_count)
    phase = (freqs[:, None] * times[None, :] % steps_count) * (2.0 * math.pi / steps_count)
    scale = 1.0 / math.sqrt(steps_count)
    return (np.stack([np.cos(phase), -np.sin(phase)], 1) * scale).astype(np.float32)


def split_bf16(values):
    high = values.astype(jnp.bfloat16)
    low = (values - high.astype(values.dtype)).astype(jnp.bfloat16)
    return high, low


def transform_operand(steps_count, freq_count, order):
    table = dft_table(steps_count, freq_count)[order]
    parts = np.stack([x.astype(np.float32) for x in split_bf16(table)], 1)
    sources = parts.shape[0]
    wide = np.broadcast_to(parts[..., None, :], (*parts.shape[:-1], GROUP, steps_count))
    return jnp.asarray(wide.reshape(sources, -1, GROUP * steps_count), jnp.float32)


def edge_base(slot, b, r, vectors):
    return ((slot * 2 + b) * PASSES + r) * vectors


def transform_kernel(slots, edged, field_hbm, table_hbm, own_hbm, *refs):
    outs, (pair, cross) = refs[:slots], refs[slots : slots + 2]
    field, table, own_c, field_sem, table_sem, own_sem = refs[slots + 2 :]
    vectors, rows, steps, width = field.shape
    blocks = vectors // GROUP
    even = even_strip()
    source = lax.axis_index("freq") if table_hbm.shape[0] > 1 else 0
    get_table = pltpu.make_async_copy(table_hbm.at[source], table, table_sem)
    get_table.start()
    get_own = pltpu.make_async_copy(own_hbm, own_c, own_sem)
    get_own.start()

    def get(i):
        at = pl.ds(i * GROUP, GROUP)
        return pltpu.make_async_copy(field_hbm.at[at], field.at[at], field_sem.at[i])

    for i in range(blocks):
        get(i).start()
    get_own.wait()
    rim = PASSES - 1
    base = edge_base(len(edged), 0, 0, vectors)
    last_c, first_c = own_c[rows - rim :], own_c[:rim]
    pad = jnp.zeros((pair.shape[0] - base - rim, width), jnp.float32)
    for ref, one, other in ((pair, last_c, first_c), (cross, first_c, last_c)):
        ref[base : base + rim] = pick(even, one, other)
        ref[base + rim :] = pad
    get_table.wait()
    short = table[...]
    shape = (short.shape[0], GROUP, short.shape[1])
    mine = lax.broadcasted_iota(jnp.int32, shape, 1)
    column = lax.broadcasted_iota(jnp.int32, shape, 2)
    full = jnp.where(
        (column >= mine * steps) & (column < (mine + 1) * steps), short[:, None], 0.0
    )
    full = full.reshape(-1, short.shape[1]).astype(jnp.bfloat16)
    for i in range(blocks):
        get(i).wait()
        span = slice(i * GROUP, (i + 1) * GROUP)
        data = jnp.concatenate(
            [field[span, r].reshape(GROUP * steps, width) for r in range(rows)], axis=1
        )
        both = jnp.dot(full, data, preferred_element_type=jnp.float32)
        half = both.shape[0] // 2
        values = both[:half] + both[half:]
        for slot in range(slots):
            for b in range(2):
                at = (slot * 2 + b) * GROUP
                for r in range(rows):
                    piece = values[at : at + GROUP, r * width : (r + 1) * width]
                    outs[slot][b, r, span] = piece
                if slot not in edged:
                    continue
                for r in range(PASSES):
                    row = (rows - PASSES + r) * width
                    last = values[at : at + GROUP, row : row + width]
                    first = values[at : at + GROUP, r * width : (r + 1) * width]
                    to = edge_base(edged.index(slot), b, r, vectors) + i * GROUP
                    pair[to : to + GROUP] = pick(even, last, first)
                    cross[to : to + GROUP] = pick(even, first, last)


def transform(field, table, coefficient, slots, edged):
    vectors, rows, steps, width = field.shape
    chunk = jax.ShapeDtypeStruct((2, rows, vectors, width), jnp.float32)
    edge = jax.ShapeDtypeStruct((edge_base(len(edged), 0, 0, vectors) + GROUP, width), jnp.float32)
    hbm = pl.BlockSpec(memory_space=pltpu.HBM)
    vmem = pl.BlockSpec(memory_space=pltpu.VMEM)
    *chunks, pair, cross = pl.pallas_call(
        functools.partial(transform_kernel, slots, edged),
        out_shape=[chunk] * slots + [edge] * 2,
        in_specs=[hbm, hbm, hbm],
        out_specs=[vmem] * (slots + 2),
        scratch_shapes=[
            pltpu.VMEM(field.shape, field.dtype),
            pltpu.VMEM(table.shape[1:], table.dtype),
            pltpu.VMEM(coefficient.shape, coefficient.dtype),
            pltpu.SemaphoreType.DMA((vectors // GROUP,)),
            pltpu.SemaphoreType.DMA(()),
            pltpu.SemaphoreType.DMA(()),
        ],
        compiler_params=params(),
        cost_estimate=cost(
            2 * table.shape[1] * table.shape[2] * rows * width * vectors,
            vectors * rows * width * (2 * steps + 8 * slots),
        ),
        name="transform",
    )(*map(in_hbm, (field, table, coefficient)))
    return chunks, pair, cross


def split_kernel(x_ref, high_ref, low_ref):
    high, low = split_bf16(x_ref[...])
    high_ref[...] = high
    low_ref[...] = low


def split_transfer(transfer):
    parts, sensors, cells = transfer.shape
    block = pl.BlockSpec((1, sensors, cells), lambda a: (a, 0, 0))
    return pl.pallas_call(
        split_kernel,
        out_shape=[jax.ShapeDtypeStruct(transfer.shape, jnp.bfloat16)] * 2,
        grid=(parts,),
        in_specs=[block],
        out_specs=[block, block],
        compiler_params=params(),
        cost_estimate=cost(2 * transfer.size, 8 * transfer.size),
        name="split_transfer",
    )(in_hbm(transfer))


def relaxed_rows(rows, coefficients):
    width = rows[0].shape[-1]
    lane = lax.broadcasted_iota(jnp.int32, rows[0].shape, 1)
    first, last = lane == 0, lane == width - 1
    out = []
    for i in range(1, len(rows) - 1):
        centre = rows[i]
        left = jnp.where(first, 0.0, pltpu.roll(centre, 1, 1))
        right = jnp.where(last, 0.0, pltpu.roll(centre, width - 1, 1))
        beside = (rows[i + 1] + rows[i - 1]) + (left + right)
        out.append(centre + coefficients[i - 1] * (beside - 4.0 * centre))
    return out


def edges_kernel(count, *refs):
    chunks, (pair, cross) = refs[:count], refs[count:]
    _, rows, vectors, _ = chunks[0].shape
    even = even_strip().astype(jnp.int32)
    for index, chunk in enumerate(chunks):
        for ref, start in ((pair, even), (cross, 1 - even)):
            for b in range(2):
                for r in range(PASSES):
                    at = edge_base(index, b, r, vectors)
                    ref[at : at + vectors] = chunk[b, start * (rows - PASSES) + r]


def edges(chunks):
    _, _, vectors, width = chunks[0].shape
    shape = (edge_base(len(chunks), 0, 0, vectors), width)
    return pl.pallas_call(
        functools.partial(edges_kernel, len(chunks)),
        out_shape=[jax.ShapeDtypeStruct(shape, jnp.float32)] * 2,
        compiler_params=params(),
        cost_estimate=cost(0, 16 * shape[0] * width),
        name="edges",
    )(*chunks)


def smooth_kernel(base, rim_base, chunk, pair, cross, own_c, pair_c, cross_c, out):
    _, rows, vectors, width = chunk.shape
    rim = PASSES - 1
    even = even_strip()
    part = math.gcd(vectors, 2 * GROUP)
    strip = lax.axis_index("seabed")
    inside = (strip > 0) & (strip < lax.axis_size("seabed") - 1)

    def rims(one, other):
        other = pick(inside, other, jnp.zeros_like(other))
        return pick(even, one, other), pick(even, other, one)

    at_c = slice(rim_base, rim_base + rim)
    high_c, low_c = rims(pair_c[at_c], cross_c[at_c])
    coefficients = [low_c[i : i + 1] for i in range(rim)]
    coefficients += [own_c[i : i + 1] for i in range(rows)]
    coefficients += [high_c[i : i + 1] for i in range(rim)]
    coefficients = [jnp.broadcast_to(c, (part, width)) for c in coefficients]
    for b in range(2):
        for start in range(0, vectors, part):
            span = slice(start, start + part)
            low, high = [], []
            for r in range(PASSES):
                at = base + edge_base(0, b, r, vectors) + start
                above, below = rims(pair[at : at + part], cross[at : at + part])
                high.append(above)
                low.append(below)
            values = low + [chunk[b, r, span] for r in range(rows)] + high
            for step in range(PASSES):
                values = relaxed_rows(values, coefficients[step : len(coefficients) - step])
            for r in range(rows):
                out[b, r, span] = values[r]


def smooth(chunk, pair, cross, slot, coefficients, rim_base):
    base = edge_base(slot, 0, 0, chunk.shape[2])
    return pl.pallas_call(
        functools.partial(smooth_kernel, base, rim_base),
        out_shape=jax.ShapeDtypeStruct(chunk.shape, jnp.float32),
        compiler_params=params(),
        cost_estimate=cost(30 * chunk.size, 10 * chunk.size),
        name="smooth",
    )(chunk, pair, cross, *coefficients)


def combine_kernel(chunks_in, owners_in, paired, *refs):
    refs = list(refs)
    phases = [[refs.pop(0) for _ in range(count)] for count in chunks_in]
    t_high, t_low = refs.pop(0), refs.pop(0)
    outs, held = refs[:-1], refs[-1]
    rows, vectors, width = phases[0][0].shape[1:]
    each = vectors // owners_in
    for phase, chunks in enumerate(phases):
        inner = slice(phase * each, (phase + 1) * each)
        for index, ref in enumerate(chunks):
            for o in range(owners_in):
                if paired:
                    owner = (lax.axis_index("freq") ^ index) * owners_in + o
                    apart = owner ^ lax.axis_index("seabed")
                    place = (apart & 1) * (held.shape[1] // 2) + (apart >> 1)
                else:
                    place = index * owners_in + o
                for b in range(2):
                    for r in range(rows):
                        held[b, place, inner, r * width : (r + 1) * width] = ref[
                            b, r, o * each : (o + 1) * each
                        ]
    places, owned, cells = held.shape[1:]
    lhs_high, lhs_low = split_bf16(held[...].reshape(2 * places * owned, cells))

    def times(a):
        def dot(x, w):
            return lax.dot_general(
                x, w, (((1,), (1,)), ((), ())), preferred_element_type=jnp.float32
            )

        return (dot(lhs_low, t_high[a]) + dot(lhs_high, t_low[a])) + dot(lhs_high, t_high[a])

    half = places * owned
    by_real, by_imag = times(0), times(1)
    real = by_real[:half] - by_imag[half:]
    imag = by_imag[:half] + by_real[half:]
    sensors = real.shape[-1]
    share = places // len(outs)
    for e, out in enumerate(outs):
        at = slice(e * share * owned, (e + 1) * share * owned)
        out[:, 0] = real[at].reshape(share, owned, sensors)
        out[:, 1] = imag[at].reshape(share, owned, sensors)


def combine(phases, split, owners_in, paired):
    t_high, t_low = split
    sensors, cells = t_high.shape[1:]
    places = len(phases[0]) * owners_in
    owned = sum(p[0].shape[2] for p in phases) // owners_in
    vectors = places * owned
    outs = 2 if paired else 1
    return pl.pallas_call(
        functools.partial(combine_kernel, [len(p) for p in phases], owners_in, paired),
        out_shape=[jax.ShapeDtypeStruct((places // outs, 2, owned, sensors), jnp.float32)] * outs,
        scratch_shapes=[pltpu.VMEM((2, places, owned, cells), jnp.float32)],
        compiler_params=params(),
        cost_estimate=cost(
            24 * vectors * sensors * cells,
            8 * sensors * cells + 8 * vectors * cells + 16 * vectors * sensors,
        ),
        name="combine",
    )(*[c for p in phases for c in p], t_high, t_low)


def xor_pairs(count, apart):
    return [(i, i ^ apart) for i in range(count)]


def neighbours(pair, cross, strips):
    inner = [(i, (i + 1) % strips) for i in range(1, strips, 2)]
    inner = inner + [(b, a) for a, b in inner]
    cross = lax.ppermute(cross, "seabed", inner)
    pair = lax.ppermute(pair, "seabed", xor_pairs(strips, 1))
    return pair, cross


def paired_shards(field, coefficient, split_of, table, freq_count, strips):
    vectors = field.shape[0]
    chunks, pair, cross = transform(field, table, coefficient, freq_count, (2, 0))

    def swap(m, chunk):
        return lax.ppermute(chunk, "freq", xor_pairs(freq_count, m))

    def relax(chunk, edge, slot):
        return smooth(chunk, *edge, slot, coefficients, rim_base)

    third = swap(3, chunks[3])
    edge = neighbours(pair, cross, strips)
    first = swap(1, chunks[1])
    split = split_of()
    coefficients = (coefficient, *edge)
    rim_base = edge_base(2, 0, 0, vectors)
    second = swap(2, relax(chunks[2], edge, 0))
    own = relax(chunks[0], edge, 1)
    edge = neighbours(*edges([third, first]), strips)
    third = relax(third, edge, 0)
    first = relax(first, edge, 1)
    keep, send = combine([[own, first, second, third]], split, 2, True)
    chips = keep + lax.ppermute(send, "seabed", xor_pairs(strips, 1))
    total = chips[0]
    for d in range(1, strips // 2):
        total = total + lax.ppermute(chips[d], "seabed", xor_pairs(strips, 2 * d))
    return total


def plain_shards(field, coefficient, split_of, table, freq_count, strips):
    _, rows = field.shape[:2]
    spectrum, _, _ = transform(field, table, coefficient, freq_count, ())
    spectrum = jnp.stack(spectrum)
    spectrum = lax.all_to_all(spectrum, "freq", split_axis=0, concat_axis=0, tiled=True)
    chunks = list(spectrum)
    rim = PASSES - 1
    even = even_strip()
    first_c, last_c = coefficient[:rim], coefficient[rows - rim :]
    pair_c, cross_c = pick(even, last_c, first_c), pick(even, first_c, last_c)
    coefficients = (coefficient, *neighbours(pair_c, cross_c, strips))
    edge = neighbours(*edges(chunks), strips)
    chunks = [smooth(c, *edge, i, coefficients, 0) for i, c in enumerate(chunks)]
    owners_in = strips // freq_count
    (partial,) = combine([chunks], split_of(), owners_in, False)
    got = lax.all_to_all(partial, "seabed", split_axis=0, concat_axis=0, tiled=True)
    return got.sum(0)


def shards(uplift, coefficient, transfer):
    vectors, steps, _, _ = uplift.shape
    freq_count, strips = FD * lax.axis_size("freq"), lax.axis_size("seabed")
    owned = vectors * freq_count // strips
    paired = (
        strips == 8
        and freq_count == 4
        and vectors == 2 * owned
        and owned == 2 * GROUP
    )
    slots = np.arange(freq_count)
    order = slots[:, None] ^ slots[None, :] if paired else slots[None, :]
    table = transform_operand(steps, freq_count, order)
    field = jnp.transpose(uplift, (0, 2, 1, 3))
    run = paired_shards if paired else plain_shards
    total = run(
        field,
        coefficient,
        lambda: split_transfer(transfer[0]),
        table,
        freq_count,
        strips,
    )
    return jnp.transpose(total, (1, 0, 2))[:, None]


def solution(mesh):
    placed = (P("freq", None, "seabed", None), P("seabed", None), P("freq", None, None, "seabed"))
    return jax.shard_map(
        shards,
        mesh=mesh,
        in_specs=placed,
        out_specs=P("seabed", "freq", None, None),
        check_vma=False,
    )
```

```python
import functools
import math

import jax
import jax.numpy as jnp
import numpy as np
from jax import lax
from jax.experimental import pallas as pl
from jax.experimental.pallas import tpu as pltpu
from jax.sharding import PartitionSpec as P


FD = 1
PASSES = 3
GROUP = 8
GRANT = 16 * 1024 * 1024


def params():
    return pltpu.CompilerParams(vmem_limit_bytes=GRANT)


def cost(flops, moved):
    return pl.CostEstimate(flops=flops, bytes_accessed=moved, transcendentals=0)


def in_hbm(array):
    return pltpu.with_memory_space_constraint(array, pltpu.HBM)


def even_strip():
    return lax.rem(lax.axis_index("seabed"), 2) == 0


def pick(flag, one, other):
    return jnp.where(jnp.full(one.shape, flag), one, other)


def dft_table(steps_count, freq_count):
    times = np.arange(steps_count)
    freqs = np.arange(freq_count)
    phase = (freqs[:, None] * times[None, :] % steps_count) * (2.0 * math.pi / steps_count)
    scale = 1.0 / math.sqrt(steps_count)
    return (np.stack([np.cos(phase), -np.sin(phase)], 1) * scale).astype(np.float32)


def split_bf16(values):
    high = values.astype(jnp.bfloat16)
    low = (values - high.astype(values.dtype)).astype(jnp.bfloat16)
    return high, low


def transform_operand(steps_count, freq_count, order):
    table = dft_table(steps_count, freq_count)[order]
    parts = np.stack([x.astype(np.float32) for x in split_bf16(table)], 1)
    sources = parts.shape[0]
    wide = np.broadcast_to(parts[..., None, :], (*parts.shape[:-1], GROUP, steps_count))
    return jnp.asarray(wide.reshape(sources, -1, GROUP * steps_count), jnp.float32)


def edge_base(slot, b, r, vectors):
    return ((slot * 2 + b) * PASSES + r) * vectors


def transform_kernel(slots, edged, field_hbm, table_hbm, own_hbm, *refs):
    outs, (pair, cross) = refs[:slots], refs[slots : slots + 2]
    field, table, own_c, field_sem, table_sem, own_sem = refs[slots + 2 :]
    vectors, rows, steps, width = field.shape
    blocks = vectors // GROUP
    even = even_strip()
    source = lax.axis_index("freq") if table_hbm.shape[0] > 1 else 0
    get_table = pltpu.make_async_copy(table_hbm.at[source], table, table_sem)
    get_table.start()
    get_own = pltpu.make_async_copy(own_hbm, own_c, own_sem)
    get_own.start()

    def get(i):
        at = pl.ds(i * GROUP, GROUP)
        return pltpu.make_async_copy(field_hbm.at[at], field.at[at], field_sem.at[i])

    for i in range(blocks):
        get(i).start()
    get_own.wait()
    rim = PASSES - 1
    base = edge_base(len(edged), 0, 0, vectors)
    last_c, first_c = own_c[rows - rim :], own_c[:rim]
    pad = jnp.zeros((pair.shape[0] - base - rim, width), jnp.float32)
    for ref, one, other in ((pair, last_c, first_c), (cross, first_c, last_c)):
        ref[base : base + rim] = pick(even, one, other)
        ref[base + rim :] = pad
    get_table.wait()
    short = table[...]
    shape = (short.shape[0], GROUP, short.shape[1])
    mine = lax.broadcasted_iota(jnp.int32, shape, 1)
    column = lax.broadcasted_iota(jnp.int32, shape, 2)
    full = jnp.where(
        (column >= mine * steps) & (column < (mine + 1) * steps), short[:, None], 0.0
    )
    full = full.reshape(-1, short.shape[1]).astype(jnp.bfloat16)
    for i in range(blocks):
        get(i).wait()
        span = slice(i * GROUP, (i + 1) * GROUP)
        data = jnp.concatenate(
            [field[span, r].reshape(GROUP * steps, width) for r in range(rows)], axis=1
        )
        both = jnp.dot(full, data, preferred_element_type=jnp.float32)
        half = both.shape[0] // 2
        values = both[:half] + both[half:]
        for slot in range(slots):
            for b in range(2):
                at = (slot * 2 + b) * GROUP
                for r in range(rows):
                    piece = values[at : at + GROUP, r * width : (r + 1) * width]
                    outs[slot][b, r, span] = piece
                if slot not in edged:
                    continue
                for r in range(PASSES):
                    row = (rows - PASSES + r) * width
                    last = values[at : at + GROUP, row : row + width]
                    first = values[at : at + GROUP, r * width : (r + 1) * width]
                    to = edge_base(edged.index(slot), b, r, vectors) + i * GROUP
                    pair[to : to + GROUP] = pick(even, last, first)
                    cross[to : to + GROUP] = pick(even, first, last)


def transform(field, table, coefficient, slots, edged):
    vectors, rows, steps, width = field.shape
    chunk = jax.ShapeDtypeStruct((2, rows, vectors, width), jnp.float32)
    edge = jax.ShapeDtypeStruct((edge_base(len(edged), 0, 0, vectors) + GROUP, width), jnp.float32)
    hbm = pl.BlockSpec(memory_space=pltpu.HBM)
    vmem = pl.BlockSpec(memory_space=pltpu.VMEM)
    *chunks, pair, cross = pl.pallas_call(
        functools.partial(transform_kernel, slots, edged),
        out_shape=[chunk] * slots + [edge] * 2,
        in_specs=[hbm, hbm, hbm],
        out_specs=[vmem] * (slots + 2),
        scratch_shapes=[
            pltpu.VMEM(field.shape, field.dtype),
            pltpu.VMEM(table.shape[1:], table.dtype),
            pltpu.VMEM(coefficient.shape, coefficient.dtype),
            pltpu.SemaphoreType.DMA((vectors // GROUP,)),
            pltpu.SemaphoreType.DMA(()),
            pltpu.SemaphoreType.DMA(()),
        ],
        compiler_params=params(),
        cost_estimate=cost(
            2 * table.shape[1] * table.shape[2] * rows * width * vectors,
            vectors * rows * width * (2 * steps + 8 * slots),
        ),
        name="transform",
    )(*map(in_hbm, (field, table, coefficient)))
    return chunks, pair, cross


def split_kernel(x_ref, high_ref, low_ref):
    high, low = split_bf16(x_ref[...])
    high_ref[...] = high
    low_ref[...] = low


def split_transfer(transfer):
    parts, sensors, cells = transfer.shape
    block = pl.BlockSpec((1, sensors, cells), lambda a: (a, 0, 0))
    return pl.pallas_call(
        split_kernel,
        out_shape=[jax.ShapeDtypeStruct(transfer.shape, jnp.bfloat16)] * 2,
        grid=(parts,),
        in_specs=[block],
        out_specs=[block, block],
        compiler_params=params(),
        cost_estimate=cost(2 * transfer.size, 8 * transfer.size),
        name="split_transfer",
    )(in_hbm(transfer))


def relaxed_rows(rows, coefficients):
    width = rows[0].shape[-1]
    lane = lax.broadcasted_iota(jnp.int32, rows[0].shape, 1)
    first, last = lane == 0, lane == width - 1
    out = []
    for i in range(1, len(rows) - 1):
        centre = rows[i]
        left = jnp.where(first, 0.0, pltpu.roll(centre, 1, 1))
        right = jnp.where(last, 0.0, pltpu.roll(centre, width - 1, 1))
        beside = (rows[i + 1] + rows[i - 1]) + (left + right)
        out.append(centre + coefficients[i - 1] * (beside - 4.0 * centre))
    return out


def edges_kernel(count, *refs):
    chunks, (pair, cross) = refs[:count], refs[count:]
    _, rows, vectors, _ = chunks[0].shape
    even = even_strip().astype(jnp.int32)
    for index, chunk in enumerate(chunks):
        for ref, start in ((pair, even), (cross, 1 - even)):
            for b in range(2):
                for r in range(PASSES):
                    at = edge_base(index, b, r, vectors)
                    ref[at : at + vectors] = chunk[b, start * (rows - PASSES) + r]


def edges(chunks):
    _, _, vectors, width = chunks[0].shape
    shape = (edge_base(len(chunks), 0, 0, vectors), width)
    return pl.pallas_call(
        functools.partial(edges_kernel, len(chunks)),
        out_shape=[jax.ShapeDtypeStruct(shape, jnp.float32)] * 2,
        compiler_params=params(),
        cost_estimate=cost(0, 16 * shape[0] * width),
        name="edges",
    )(*chunks)


def smooth_kernel(base, rim_base, chunk, pair, cross, own_c, pair_c, cross_c, out):
    _, rows, vectors, width = chunk.shape
    rim = PASSES - 1
    even = even_strip()
    part = math.gcd(vectors, 2 * GROUP)
    strip = lax.axis_index("seabed")
    inside = (strip > 0) & (strip < lax.axis_size("seabed") - 1)

    def rims(one, other):
        other = pick(inside, other, jnp.zeros_like(other))
        return pick(even, one, other), pick(even, other, one)

    at_c = slice(rim_base, rim_base + rim)
    high_c, low_c = rims(pair_c[at_c], cross_c[at_c])
    coefficients = [low_c[i : i + 1] for i in range(rim)]
    coefficients += [own_c[i : i + 1] for i in range(rows)]
    coefficients += [high_c[i : i + 1] for i in range(rim)]
    coefficients = [jnp.broadcast_to(c, (part, width)) for c in coefficients]
    for b in range(2):
        for start in range(0, vectors, part):
            span = slice(start, start + part)
            low, high = [], []
            for r in range(PASSES):
                at = base + edge_base(0, b, r, vectors) + start
                above, below = rims(pair[at : at + part], cross[at : at + part])
                high.append(above)
                low.append(below)
            values = low + [chunk[b, r, span] for r in range(rows)] + high
            for step in range(PASSES):
                values = relaxed_rows(values, coefficients[step : len(coefficients) - step])
            for r in range(rows):
                out[b, r, span] = values[r]


def smooth(chunk, pair, cross, slot, coefficients, rim_base):
    base = edge_base(slot, 0, 0, chunk.shape[2])
    return pl.pallas_call(
        functools.partial(smooth_kernel, base, rim_base),
        out_shape=jax.ShapeDtypeStruct(chunk.shape, jnp.float32),
        compiler_params=params(),
        cost_estimate=cost(30 * chunk.size, 10 * chunk.size),
        name="smooth",
    )(chunk, pair, cross, *coefficients)


def place_of(index, o, owners_in):
    owner = (lax.axis_index("freq") ^ index) * owners_in + o
    apart = owner ^ lax.axis_index("seabed")
    return apart & 1, apart >> 1


def combine_kernel(indices, owners_in, paired, absent, *refs):
    count = len(indices)
    chunks, (t_high, t_low), (out, held) = refs[:count], refs[count : count + 2], refs[-2:]
    _, rows, vectors, width = chunks[0].shape
    owned = vectors // owners_in
    for at, ref in enumerate(chunks):
        for b in range(2):
            for r in range(rows):
                held[b, at, :, r * width : (r + 1) * width] = ref[b, r]
    half = count * vectors
    lhs_high, lhs_low = split_bf16(held[...].reshape(2 * half, rows * width))

    def times(a):
        def dot(x, w):
            return lax.dot_general(
                x, w, (((1,), (1,)), ((), ())), preferred_element_type=jnp.float32
            )

        return (dot(lhs_low, t_high[a]) + dot(lhs_high, t_low[a])) + dot(lhs_high, t_high[a])

    by_real, by_imag = times(0), times(1)
    real = by_real[:half] - by_imag[half:]
    imag = by_imag[:half] + by_real[half:]

    def place(index, o):
        if not paired:
            return index * owners_in + o
        core, chip = place_of(index, o, owners_in)
        return core * (out.shape[0] // 2) + (chip if out.shape[0] > 2 else 0)

    for at, index in enumerate(indices):
        for o in range(owners_in):
            span = slice((at * owners_in + o) * owned, (at * owners_in + o + 1) * owned)
            out[place(index, o), 0] = real[span]
            out[place(index, o), 1] = imag[span]
    for index in absent:
        for o in range(owners_in):
            out[place(index, o)] = jnp.zeros(out.shape[1:], out.dtype)


def combine(chunks, split, owners_in, places, paired, absent=()):
    t_high, t_low = split
    sensors, cells = t_high.shape[1:]
    indices = sorted(chunks)
    _, _, vectors, _ = chunks[indices[0]].shape
    owned = vectors // owners_in
    whole = len(indices) * vectors
    return pl.pallas_call(
        functools.partial(combine_kernel, indices, owners_in, paired, absent),
        out_shape=jax.ShapeDtypeStruct((places, 2, owned, sensors), jnp.float32),
        scratch_shapes=[pltpu.VMEM((2, len(indices), vectors, cells), jnp.float32)],
        compiler_params=params(),
        cost_estimate=cost(
            24 * whole * sensors * cells,
            8 * sensors * cells + 8 * whole * cells + 16 * whole * sensors,
        ),
        name="combine",
    )(*[chunks[i] for i in indices], t_high, t_low)


def merge_kernel(late, owners_in, most, most_moved, tail, tail_moved, *outs):
    _, chip = place_of(late, 0, owners_in)
    final = tail[0] + tail_moved[0]
    for d, out in enumerate(outs):
        here = pick(chip == d, final, jnp.zeros_like(final))
        out[...] = (most[d] + most_moved[d]) + here


def merge(late, owners_in, most, most_moved, tail, tail_moved):
    shape = jax.ShapeDtypeStruct(most.shape[1:], jnp.float32)
    return pl.pallas_call(
        functools.partial(merge_kernel, late, owners_in),
        out_shape=[shape] * most_moved.shape[0],
        compiler_params=params(),
        cost_estimate=cost(4 * most.size, 12 * most.size),
        name="merge",
    )(most, most_moved, tail, tail_moved)


def xor_pairs(count, apart):
    return [(i, i ^ apart) for i in range(count)]


def neighbours(pair, cross, strips):
    inner = [(i, (i + 1) % strips) for i in range(1, strips, 2)]
    inner = inner + [(b, a) for a, b in inner]
    cross = lax.ppermute(cross, "seabed", inner)
    pair = lax.ppermute(pair, "seabed", xor_pairs(strips, 1))
    return pair, cross


def paired_shards(field, coefficient, split_of, table, freq_count, strips):
    vectors = field.shape[0]
    chunks, pair, cross = transform(field, table, coefficient, freq_count, (2, 0))

    def swap(m, chunk):
        return lax.ppermute(chunk, "freq", xor_pairs(freq_count, m))

    def relax(chunk, edge, slot):
        return smooth(chunk, *edge, slot, coefficients, rim_base)

    first = swap(1, chunks[1])
    third = swap(3, chunks[3])
    edge = neighbours(pair, cross, strips)
    split = split_of()
    coefficients = (coefficient, *edge)
    rim_base = edge_base(2, 0, 0, vectors)
    first_edge = neighbours(*edges([first]), strips)
    second = swap(2, relax(chunks[2], edge, 0))
    own = relax(chunks[0], edge, 1)
    third_edge = neighbours(*edges([third]), strips)
    first = relax(first, first_edge, 0)
    third = relax(third, third_edge, 0)
    most = combine({0: own, 1: first, 3: third}, split, 2, strips, True, (2,))

    def to_core(partial):
        send = partial[partial.shape[0] // 2 :]
        return lax.ppermute(send, "seabed", xor_pairs(strips, 1))

    most_moved = to_core(most)
    tail = combine({2: second}, split, 2, 2, True)
    chips = merge(2, 2, most, most_moved, tail, to_core(tail))
    total = chips[0]
    for d in range(1, strips // 2):
        total = total + lax.ppermute(chips[d], "seabed", xor_pairs(strips, 2 * d))
    return total


def plain_shards(field, coefficient, split_of, table, freq_count, strips):
    _, rows = field.shape[:2]
    spectrum, _, _ = transform(field, table, coefficient, freq_count, ())
    spectrum = jnp.stack(spectrum)
    spectrum = lax.all_to_all(spectrum, "freq", split_axis=0, concat_axis=0, tiled=True)
    chunks = list(spectrum)
    rim = PASSES - 1
    even = even_strip()
    first_c, last_c = coefficient[:rim], coefficient[rows - rim :]
    pair_c, cross_c = pick(even, last_c, first_c), pick(even, first_c, last_c)
    coefficients = (coefficient, *neighbours(pair_c, cross_c, strips))
    edge = neighbours(*edges(chunks), strips)
    chunks = [smooth(c, *edge, i, coefficients, 0) for i, c in enumerate(chunks)]
    owners_in = strips // freq_count
    partial = combine(dict(enumerate(chunks)), split_of(), owners_in, strips, False)
    got = lax.all_to_all(partial, "seabed", split_axis=0, concat_axis=0, tiled=True)
    return got.sum(0)


def shards(uplift, coefficient, transfer):
    vectors, steps, _, _ = uplift.shape
    freq_count, strips = FD * lax.axis_size("freq"), lax.axis_size("seabed")
    owned = vectors * freq_count // strips
    paired = (
        strips == 8
        and freq_count == 4
        and vectors == 2 * owned
        and owned == 2 * GROUP
    )
    slots = np.arange(freq_count)
    order = slots[:, None] ^ slots[None, :] if paired else slots[None, :]
    table = transform_operand(steps, freq_count, order)
    field = jnp.transpose(uplift, (0, 2, 1, 3))
    run = paired_shards if paired else plain_shards
    total = run(
        field,
        coefficient,
        lambda: split_transfer(transfer[0]),
        table,
        freq_count,
        strips,
    )
    return jnp.transpose(total, (1, 0, 2))[:, None]


def solution(mesh):
    placed = (P("freq", None, "seabed", None), P("seabed", None), P("freq", None, None, "seabed"))
    return jax.shard_map(
        shards,
        mesh=mesh,
        in_specs=placed,
        out_specs=P("seabed", "freq", None, None),
        check_vma=False,
    )
```

```python
import functools
import math

import jax
import jax.numpy as jnp
import numpy as np
from jax import lax
from jax.experimental import pallas as pl
from jax.experimental.pallas import tpu as pltpu
from jax.sharding import PartitionSpec as P


FD = 1
PASSES = 3
GROUP = 8
GRANT = 16 * 1024 * 1024


def params():
    return pltpu.CompilerParams(vmem_limit_bytes=GRANT)


def cost(flops, moved):
    return pl.CostEstimate(flops=flops, bytes_accessed=moved, transcendentals=0)


def in_hbm(array):
    return pltpu.with_memory_space_constraint(array, pltpu.HBM)


def even_strip():
    return lax.rem(lax.axis_index("seabed"), 2) == 0


def pick(flag, one, other):
    return jnp.where(jnp.full(one.shape, flag), one, other)


def dft_table(steps_count, freq_count):
    times = np.arange(steps_count)
    freqs = np.arange(freq_count)
    phase = (freqs[:, None] * times[None, :] % steps_count) * (2.0 * math.pi / steps_count)
    scale = 1.0 / math.sqrt(steps_count)
    return (np.stack([np.cos(phase), -np.sin(phase)], 1) * scale).astype(np.float32)


def split_bf16(values):
    high = values.astype(jnp.bfloat16)
    low = (values - high.astype(values.dtype)).astype(jnp.bfloat16)
    return high, low


def transform_operand(steps_count, freq_count, order):
    table = dft_table(steps_count, freq_count)[order]
    parts = np.stack([x.astype(np.float32) for x in split_bf16(table)], 1)
    sources = parts.shape[0]
    wide = np.broadcast_to(parts[..., None, :], (*parts.shape[:-1], GROUP, steps_count))
    return jnp.asarray(wide.reshape(sources, -1, GROUP * steps_count), jnp.float32)


def edge_base(slot, b, r, vectors):
    return ((slot * 2 + b) * PASSES + r) * vectors


def transform_kernel(slots, edged, field_hbm, table_hbm, own_hbm, *refs):
    outs, (pair, cross) = refs[:slots], refs[slots : slots + 2]
    field, table, own_c, field_sem, table_sem, own_sem = refs[slots + 2 :]
    vectors, rows, steps, width = field.shape
    blocks = vectors // GROUP
    even = even_strip()
    source = lax.axis_index("freq") if table_hbm.shape[0] > 1 else 0
    get_table = pltpu.make_async_copy(table_hbm.at[source], table, table_sem)
    get_table.start()
    get_own = pltpu.make_async_copy(own_hbm, own_c, own_sem)
    get_own.start()

    def get(i):
        at = pl.ds(i * GROUP, GROUP)
        return pltpu.make_async_copy(field_hbm.at[at], field.at[at], field_sem.at[i])

    for i in range(blocks):
        get(i).start()
    get_own.wait()
    rim = PASSES - 1
    base = edge_base(len(edged), 0, 0, vectors)
    last_c, first_c = own_c[rows - rim :], own_c[:rim]
    pad = jnp.zeros((pair.shape[0] - base - rim, width), jnp.float32)
    for ref, one, other in ((pair, last_c, first_c), (cross, first_c, last_c)):
        ref[base : base + rim] = pick(even, one, other)
        ref[base + rim :] = pad
    get_table.wait()
    short = table[...]
    shape = (short.shape[0], GROUP, short.shape[1])
    mine = lax.broadcasted_iota(jnp.int32, shape, 1)
    column = lax.broadcasted_iota(jnp.int32, shape, 2)
    full = jnp.where(
        (column >= mine * steps) & (column < (mine + 1) * steps), short[:, None], 0.0
    )
    full = full.reshape(-1, short.shape[1]).astype(jnp.bfloat16)
    for i in range(blocks):
        get(i).wait()
        span = slice(i * GROUP, (i + 1) * GROUP)
        data = jnp.concatenate(
            [field[span, r].reshape(GROUP * steps, width) for r in range(rows)], axis=1
        )
        both = jnp.dot(full, data, preferred_element_type=jnp.float32)
        half = both.shape[0] // 2
        values = both[:half] + both[half:]
        for slot in range(slots):
            for b in range(2):
                at = (slot * 2 + b) * GROUP
                for r in range(rows):
                    piece = values[at : at + GROUP, r * width : (r + 1) * width]
                    outs[slot][b, r, span] = piece
                if slot not in edged:
                    continue
                for r in range(PASSES):
                    row = (rows - PASSES + r) * width
                    last = values[at : at + GROUP, row : row + width]
                    first = values[at : at + GROUP, r * width : (r + 1) * width]
                    to = edge_base(edged.index(slot), b, r, vectors) + i * GROUP
                    pair[to : to + GROUP] = pick(even, last, first)
                    cross[to : to + GROUP] = pick(even, first, last)


def transform(field, table, coefficient, slots, edged):
    vectors, rows, steps, width = field.shape
    chunk = jax.ShapeDtypeStruct((2, rows, vectors, width), jnp.float32)
    edge = jax.ShapeDtypeStruct((edge_base(len(edged), 0, 0, vectors) + GROUP, width), jnp.float32)
    hbm = pl.BlockSpec(memory_space=pltpu.HBM)
    vmem = pl.BlockSpec(memory_space=pltpu.VMEM)
    *chunks, pair, cross = pl.pallas_call(
        functools.partial(transform_kernel, slots, edged),
        out_shape=[chunk] * slots + [edge] * 2,
        in_specs=[hbm, hbm, hbm],
        out_specs=[vmem] * (slots + 2),
        scratch_shapes=[
            pltpu.VMEM(field.shape, field.dtype),
            pltpu.VMEM(table.shape[1:], table.dtype),
            pltpu.VMEM(coefficient.shape, coefficient.dtype),
            pltpu.SemaphoreType.DMA((vectors // GROUP,)),
            pltpu.SemaphoreType.DMA(()),
            pltpu.SemaphoreType.DMA(()),
        ],
        compiler_params=params(),
        cost_estimate=cost(
            2 * table.shape[1] * table.shape[2] * rows * width * vectors,
            vectors * rows * width * (2 * steps + 8 * slots),
        ),
        name="transform",
    )(*map(in_hbm, (field, table, coefficient)))
    return chunks, pair, cross


def split_kernel(x_ref, high_ref, low_ref):
    high_ref[0], low_ref[0] = split_bf16(jnp.transpose(x_ref[0]))


def split_transfer(transfer):
    parts, sensors, cells = transfer.shape
    block = pl.BlockSpec((1, cells, sensors), lambda a: (a, 0, 0))
    return pl.pallas_call(
        split_kernel,
        out_shape=[jax.ShapeDtypeStruct((parts, cells, sensors), jnp.bfloat16)] * 2,
        grid=(parts,),
        in_specs=[pl.BlockSpec((1, sensors, cells), lambda a: (a, 0, 0))],
        out_specs=[block, block],
        compiler_params=params(),
        cost_estimate=cost(2 * transfer.size, 8 * transfer.size),
        name="split_transfer",
    )(in_hbm(transfer))


def relaxed_rows(rows, coefficients):
    width = rows[0].shape[-1]
    lane = lax.broadcasted_iota(jnp.int32, rows[0].shape, 1)
    first, last = lane == 0, lane == width - 1
    out = []
    for i in range(1, len(rows) - 1):
        centre = rows[i]
        left = jnp.where(first, 0.0, pltpu.roll(centre, 1, 1))
        right = jnp.where(last, 0.0, pltpu.roll(centre, width - 1, 1))
        beside = (rows[i + 1] + rows[i - 1]) + (left + right)
        out.append(centre + coefficients[i - 1] * (beside - 4.0 * centre))
    return out


def edges_kernel(count, *refs):
    chunks, (pair, cross) = refs[:count], refs[count:]
    _, rows, vectors, _ = chunks[0].shape
    even = even_strip().astype(jnp.int32)
    for index, chunk in enumerate(chunks):
        for ref, start in ((pair, even), (cross, 1 - even)):
            for b in range(2):
                for r in range(PASSES):
                    at = edge_base(index, b, r, vectors)
                    ref[at : at + vectors] = chunk[b, start * (rows - PASSES) + r]


def edges(chunks):
    _, _, vectors, width = chunks[0].shape
    shape = (edge_base(len(chunks), 0, 0, vectors), width)
    return pl.pallas_call(
        functools.partial(edges_kernel, len(chunks)),
        out_shape=[jax.ShapeDtypeStruct(shape, jnp.float32)] * 2,
        compiler_params=params(),
        cost_estimate=cost(0, 16 * shape[0] * width),
        name="edges",
    )(*chunks)


def smooth_kernel(base, rim_base, chunk, pair, cross, own_c, pair_c, cross_c, out):
    _, rows, vectors, width = chunk.shape
    rim = PASSES - 1
    even = even_strip()
    part = math.gcd(vectors, 2 * GROUP)
    strip = lax.axis_index("seabed")
    inside = (strip > 0) & (strip < lax.axis_size("seabed") - 1)

    def rims(one, other):
        other = pick(inside, other, jnp.zeros_like(other))
        return pick(even, one, other), pick(even, other, one)

    at_c = slice(rim_base, rim_base + rim)
    high_c, low_c = rims(pair_c[at_c], cross_c[at_c])
    coefficients = [low_c[i : i + 1] for i in range(rim)]
    coefficients += [own_c[i : i + 1] for i in range(rows)]
    coefficients += [high_c[i : i + 1] for i in range(rim)]
    coefficients = [jnp.broadcast_to(c, (part, width)) for c in coefficients]
    for b in range(2):
        for start in range(0, vectors, part):
            span = slice(start, start + part)
            low, high = [], []
            for r in range(PASSES):
                at = base + edge_base(0, b, r, vectors) + start
                above, below = rims(pair[at : at + part], cross[at : at + part])
                high.append(above)
                low.append(below)
            values = low + [chunk[b, r, span] for r in range(rows)] + high
            for step in range(PASSES):
                values = relaxed_rows(values, coefficients[step : len(coefficients) - step])
            for r in range(rows):
                out[b, r, span] = values[r]


def smooth(chunk, pair, cross, slot, coefficients, rim_base):
    base = edge_base(slot, 0, 0, chunk.shape[2])
    return pl.pallas_call(
        functools.partial(smooth_kernel, base, rim_base),
        out_shape=jax.ShapeDtypeStruct(chunk.shape, jnp.float32),
        compiler_params=params(),
        cost_estimate=cost(30 * chunk.size, 10 * chunk.size),
        name="smooth",
    )(chunk, pair, cross, *coefficients)


def place_of(index, o, owners_in):
    owner = (lax.axis_index("freq") ^ index) * owners_in + o
    apart = owner ^ lax.axis_index("seabed")
    return apart & 1, apart >> 1


def combine_kernel(indices, owners_in, paired, absent, *refs):
    count = len(indices)
    chunks, (t_high, t_low), (out, held) = refs[:count], refs[count : count + 2], refs[-2:]
    _, rows, vectors, width = chunks[0].shape
    owned = vectors // owners_in
    for at, ref in enumerate(chunks):
        for b in range(2):
            for r in range(rows):
                held[b, at, :, r * width : (r + 1) * width] = ref[b, r]
    half = count * vectors
    lhs_high, lhs_low = split_bf16(held[...].reshape(2 * half, rows * width))

    def times(a):
        def dot(x, w):
            return lax.dot_general(
                x, w, (((1,), (0,)), ((), ())), preferred_element_type=jnp.float32
            )

        return (dot(lhs_low, t_high[a]) + dot(lhs_high, t_low[a])) + dot(lhs_high, t_high[a])

    by_real, by_imag = times(0), times(1)
    real = by_real[:half] - by_imag[half:]
    imag = by_imag[:half] + by_real[half:]

    def place(index, o):
        if not paired:
            return index * owners_in + o
        core, chip = place_of(index, o, owners_in)
        return core * (out.shape[0] // 2) + (chip if out.shape[0] > 2 else 0)

    for at, index in enumerate(indices):
        for o in range(owners_in):
            span = slice((at * owners_in + o) * owned, (at * owners_in + o + 1) * owned)
            out[place(index, o), 0] = real[span]
            out[place(index, o), 1] = imag[span]
    for index in absent:
        for o in range(owners_in):
            out[place(index, o)] = jnp.zeros(out.shape[1:], out.dtype)


def combine(chunks, split, owners_in, places, paired, absent=()):
    t_high, t_low = split
    cells, sensors = t_high.shape[1:]
    indices = sorted(chunks)
    _, _, vectors, _ = chunks[indices[0]].shape
    owned = vectors // owners_in
    whole = len(indices) * vectors
    return pl.pallas_call(
        functools.partial(combine_kernel, indices, owners_in, paired, absent),
        out_shape=jax.ShapeDtypeStruct((places, 2, owned, sensors), jnp.float32),
        scratch_shapes=[pltpu.VMEM((2, len(indices), vectors, cells), jnp.float32)],
        compiler_params=params(),
        cost_estimate=cost(
            24 * whole * sensors * cells,
            8 * sensors * cells + 8 * whole * cells + 16 * whole * sensors,
        ),
        name="combine",
    )(*[chunks[i] for i in indices], t_high, t_low)


def merge_kernel(late, owners_in, most, most_moved, tail, tail_moved, *outs):
    _, chip = place_of(late, 0, owners_in)
    final = tail[0] + tail_moved[0]
    for d, out in enumerate(outs):
        here = pick(chip == d, final, jnp.zeros_like(final))
        out[...] = (most[d] + most_moved[d]) + here


def merge(late, owners_in, most, most_moved, tail, tail_moved):
    shape = jax.ShapeDtypeStruct(most.shape[1:], jnp.float32)
    return pl.pallas_call(
        functools.partial(merge_kernel, late, owners_in),
        out_shape=[shape] * most_moved.shape[0],
        compiler_params=params(),
        cost_estimate=cost(4 * most.size, 12 * most.size),
        name="merge",
    )(most, most_moved, tail, tail_moved)


def xor_pairs(count, apart):
    return [(i, i ^ apart) for i in range(count)]


def neighbours(pair, cross, strips):
    inner = [(i, (i + 1) % strips) for i in range(1, strips, 2)]
    inner = inner + [(b, a) for a, b in inner]
    cross = lax.ppermute(cross, "seabed", inner)
    pair = lax.ppermute(pair, "seabed", xor_pairs(strips, 1))
    return pair, cross


def paired_shards(field, coefficient, split_of, table, freq_count, strips):
    vectors = field.shape[0]
    chunks, pair, cross = transform(field, table, coefficient, freq_count, (2,))

    def swap(m, chunk):
        return lax.ppermute(chunk, "freq", xor_pairs(freq_count, m))

    def relax(chunk, edge, slot):
        return smooth(chunk, *edge, slot, coefficients, rim_base)

    first = swap(1, chunks[1])
    third = swap(3, chunks[3])
    edge = neighbours(pair, cross, strips)
    split = split_of()
    coefficients = (coefficient, *edge)
    rim_base = edge_base(1, 0, 0, vectors)
    mid_edge = neighbours(*edges([chunks[0], first]), strips)
    second = swap(2, relax(chunks[2], edge, 0))
    own = relax(chunks[0], mid_edge, 0)
    third_edge = neighbours(*edges([third]), strips)
    first = relax(first, mid_edge, 1)
    third = relax(third, third_edge, 0)
    most = combine({0: own, 1: first, 3: third}, split, 2, strips, True, (2,))

    def to_core(partial):
        send = partial[partial.shape[0] // 2 :]
        return lax.ppermute(send, "seabed", xor_pairs(strips, 1))

    most_moved = to_core(most)
    tail = combine({2: second}, split, 2, 2, True)
    chips = merge(2, 2, most, most_moved, tail, to_core(tail))
    total = chips[0]
    for d in range(1, strips // 2):
        total = total + lax.ppermute(chips[d], "seabed", xor_pairs(strips, 2 * d))
    return total


def plain_shards(field, coefficient, split_of, table, freq_count, strips):
    _, rows = field.shape[:2]
    spectrum, _, _ = transform(field, table, coefficient, freq_count, ())
    spectrum = jnp.stack(spectrum)
    spectrum = lax.all_to_all(spectrum, "freq", split_axis=0, concat_axis=0, tiled=True)
    chunks = list(spectrum)
    rim = PASSES - 1
    even = even_strip()
    first_c, last_c = coefficient[:rim], coefficient[rows - rim :]
    pair_c, cross_c = pick(even, last_c, first_c), pick(even, first_c, last_c)
    coefficients = (coefficient, *neighbours(pair_c, cross_c, strips))
    edge = neighbours(*edges(chunks), strips)
    chunks = [smooth(c, *edge, i, coefficients, 0) for i, c in enumerate(chunks)]
    owners_in = strips // freq_count
    partial = combine(dict(enumerate(chunks)), split_of(), owners_in, strips, False)
    got = lax.all_to_all(partial, "seabed", split_axis=0, concat_axis=0, tiled=True)
    return got.sum(0)


def shards(uplift, coefficient, transfer):
    vectors, steps, _, _ = uplift.shape
    freq_count, strips = FD * lax.axis_size("freq"), lax.axis_size("seabed")
    owned = vectors * freq_count // strips
    paired = (
        strips == 8
        and freq_count == 4
        and vectors == 2 * owned
        and owned == 2 * GROUP
    )
    slots = np.arange(freq_count)
    order = slots[:, None] ^ slots[None, :] if paired else slots[None, :]
    table = transform_operand(steps, freq_count, order)
    field = jnp.transpose(uplift, (0, 2, 1, 3))
    run = paired_shards if paired else plain_shards
    total = run(
        field,
        coefficient,
        lambda: split_transfer(transfer[0]),
        table,
        freq_count,
        strips,
    )
    return jnp.transpose(total, (1, 0, 2))[:, None]


def solution(mesh):
    placed = (P("freq", None, "seabed", None), P("seabed", None), P("freq", None, None, "seabed"))
    return jax.shard_map(
        shards,
        mesh=mesh,
        in_specs=placed,
        out_specs=P("seabed", "freq", None, None),
        check_vma=False,
    )
```

```python
import functools
import math

import jax
import jax.numpy as jnp
import numpy as np
from jax import lax
from jax.experimental import pallas as pl
from jax.experimental.pallas import tpu as pltpu
from jax.sharding import PartitionSpec as P


FD = 1
PASSES = 3
GROUP = 8
GRANT = 16 * 1024 * 1024


def params():
    return pltpu.CompilerParams(vmem_limit_bytes=GRANT)


def cost(flops, moved):
    return pl.CostEstimate(flops=flops, bytes_accessed=moved, transcendentals=0)


def in_hbm(array):
    return pltpu.with_memory_space_constraint(array, pltpu.HBM)


def even_strip():
    return lax.rem(lax.axis_index("seabed"), 2) == 0


def pick(flag, one, other):
    return jnp.where(jnp.full(one.shape, flag), one, other)


def dft_table(steps_count, freq_count):
    times = np.arange(steps_count)
    freqs = np.arange(freq_count)
    phase = (freqs[:, None] * times[None, :] % steps_count) * (2.0 * math.pi / steps_count)
    scale = 1.0 / math.sqrt(steps_count)
    return (np.stack([np.cos(phase), -np.sin(phase)], 1) * scale).astype(np.float32)


def split_bf16(values):
    high = values.astype(jnp.bfloat16)
    low = (values - high.astype(values.dtype)).astype(jnp.bfloat16)
    return high, low


def transform_operand(steps_count, freq_count, order):
    table = dft_table(steps_count, freq_count)[order]
    parts = np.stack([x.astype(np.float32) for x in split_bf16(table)], 1)
    sources = parts.shape[0]
    wide = np.broadcast_to(parts[..., None, :], (*parts.shape[:-1], GROUP, steps_count))
    return jnp.asarray(wide.reshape(sources, -1, GROUP * steps_count), jnp.float32)


def edge_base(slot, b, r, vectors):
    return ((slot * 2 + b) * PASSES + r) * vectors


def transform_kernel(slots, edged, field_hbm, table_hbm, own_hbm, *refs):
    outs, (pair, cross) = refs[:slots], refs[slots : slots + 2]
    field, table, own_c, field_sem, table_sem, own_sem = refs[slots + 2 :]
    vectors, rows, steps, width = field.shape
    blocks = vectors // GROUP
    even = even_strip()
    source = lax.axis_index("freq") if table_hbm.shape[0] > 1 else 0
    get_table = pltpu.make_async_copy(table_hbm.at[source], table, table_sem)
    get_table.start()
    get_own = pltpu.make_async_copy(own_hbm, own_c, own_sem)
    get_own.start()

    def get(i):
        at = pl.ds(i * GROUP, GROUP)
        return pltpu.make_async_copy(field_hbm.at[at], field.at[at], field_sem.at[i])

    for i in range(blocks):
        get(i).start()
    get_own.wait()
    rim = PASSES - 1
    base = edge_base(len(edged), 0, 0, vectors)
    last_c, first_c = own_c[rows - rim :], own_c[:rim]
    pad = jnp.zeros((pair.shape[0] - base - rim, width), jnp.float32)
    for ref, one, other in ((pair, last_c, first_c), (cross, first_c, last_c)):
        ref[base : base + rim] = pick(even, one, other)
        ref[base + rim :] = pad
    get_table.wait()
    short = table[...]
    shape = (short.shape[0], GROUP, short.shape[1])
    mine = lax.broadcasted_iota(jnp.int32, shape, 1)
    column = lax.broadcasted_iota(jnp.int32, shape, 2)
    full = jnp.where(
        (column >= mine * steps) & (column < (mine + 1) * steps), short[:, None], 0.0
    )
    full = full.reshape(-1, short.shape[1]).astype(jnp.bfloat16)
    for i in range(blocks):
        get(i).wait()
        span = slice(i * GROUP, (i + 1) * GROUP)
        data = jnp.concatenate(
            [field[span, r].reshape(GROUP * steps, width) for r in range(rows)], axis=1
        )
        both = jnp.dot(full, data, preferred_element_type=jnp.float32)
        half = both.shape[0] // 2
        values = both[:half] + both[half:]
        for slot in range(slots):
            for b in range(2):
                at = (slot * 2 + b) * GROUP
                for r in range(rows):
                    piece = values[at : at + GROUP, r * width : (r + 1) * width]
                    outs[slot][b, r, span] = piece
                if slot not in edged:
                    continue
                for r in range(PASSES):
                    row = (rows - PASSES + r) * width
                    last = values[at : at + GROUP, row : row + width]
                    first = values[at : at + GROUP, r * width : (r + 1) * width]
                    to = edge_base(edged.index(slot), b, r, vectors) + i * GROUP
                    pair[to : to + GROUP] = pick(even, last, first)
                    cross[to : to + GROUP] = pick(even, first, last)


def transform(field, table, coefficient, slots, edged):
    vectors, rows, steps, width = field.shape
    chunk = jax.ShapeDtypeStruct((2, rows, vectors, width), jnp.float32)
    edge = jax.ShapeDtypeStruct((edge_base(len(edged), 0, 0, vectors) + GROUP, width), jnp.float32)
    hbm = pl.BlockSpec(memory_space=pltpu.HBM)
    vmem = pl.BlockSpec(memory_space=pltpu.VMEM)
    *chunks, pair, cross = pl.pallas_call(
        functools.partial(transform_kernel, slots, edged),
        out_shape=[chunk] * slots + [edge] * 2,
        in_specs=[hbm, hbm, hbm],
        out_specs=[vmem] * (slots + 2),
        scratch_shapes=[
            pltpu.VMEM(field.shape, field.dtype),
            pltpu.VMEM(table.shape[1:], table.dtype),
            pltpu.VMEM(coefficient.shape, coefficient.dtype),
            pltpu.SemaphoreType.DMA((vectors // GROUP,)),
            pltpu.SemaphoreType.DMA(()),
            pltpu.SemaphoreType.DMA(()),
        ],
        compiler_params=params(),
        cost_estimate=cost(
            2 * table.shape[1] * table.shape[2] * rows * width * vectors,
            vectors * rows * width * (2 * steps + 8 * slots),
        ),
        name="transform",
    )(*map(in_hbm, (field, table, coefficient)))
    return chunks, pair, cross


def split_kernel(x_ref, high_ref, low_ref):
    high_ref[0], low_ref[0] = split_bf16(jnp.transpose(x_ref[0]))


def split_transfer(transfer):
    parts, sensors, cells = transfer.shape
    block = pl.BlockSpec((1, cells, sensors), lambda a: (a, 0, 0))
    return pl.pallas_call(
        split_kernel,
        out_shape=[jax.ShapeDtypeStruct((parts, cells, sensors), jnp.bfloat16)] * 2,
        grid=(parts,),
        in_specs=[pl.BlockSpec((1, sensors, cells), lambda a: (a, 0, 0))],
        out_specs=[block, block],
        compiler_params=params(),
        cost_estimate=cost(2 * transfer.size, 8 * transfer.size),
        name="split_transfer",
    )(in_hbm(transfer))


def relaxed_rows(rows, coefficients):
    width = rows[0].shape[-1]
    lane = lax.broadcasted_iota(jnp.int32, rows[0].shape, 1)
    first, last = lane == 0, lane == width - 1
    out = []
    for i in range(1, len(rows) - 1):
        centre = rows[i]
        left = jnp.where(first, 0.0, pltpu.roll(centre, 1, 1))
        right = jnp.where(last, 0.0, pltpu.roll(centre, width - 1, 1))
        beside = (rows[i + 1] + rows[i - 1]) + (left + right)
        out.append(centre + coefficients[i - 1] * (beside - 4.0 * centre))
    return out


def edges_kernel(count, *refs):
    chunks, (pair, cross) = refs[:count], refs[count:]
    _, rows, vectors, _ = chunks[0].shape
    even = even_strip().astype(jnp.int32)
    for index, chunk in enumerate(chunks):
        for ref, start in ((pair, even), (cross, 1 - even)):
            for b in range(2):
                for r in range(PASSES):
                    at = edge_base(index, b, r, vectors)
                    ref[at : at + vectors] = chunk[b, start * (rows - PASSES) + r]


def edges(chunks):
    _, _, vectors, width = chunks[0].shape
    shape = (edge_base(len(chunks), 0, 0, vectors), width)
    return pl.pallas_call(
        functools.partial(edges_kernel, len(chunks)),
        out_shape=[jax.ShapeDtypeStruct(shape, jnp.float32)] * 2,
        compiler_params=params(),
        cost_estimate=cost(0, 16 * shape[0] * width),
        name="edges",
    )(*chunks)


def smooth_kernel(base, rim_base, chunk, pair, cross, own_c, pair_c, cross_c, out):
    _, rows, vectors, width = chunk.shape
    rim = PASSES - 1
    even = even_strip()
    part = math.gcd(vectors, 2 * GROUP)
    strip = lax.axis_index("seabed")
    inside = (strip > 0) & (strip < lax.axis_size("seabed") - 1)

    def rims(one, other):
        other = pick(inside, other, jnp.zeros_like(other))
        return pick(even, one, other), pick(even, other, one)

    at_c = slice(rim_base, rim_base + rim)
    high_c, low_c = rims(pair_c[at_c], cross_c[at_c])
    coefficients = [low_c[i : i + 1] for i in range(rim)]
    coefficients += [own_c[i : i + 1] for i in range(rows)]
    coefficients += [high_c[i : i + 1] for i in range(rim)]
    coefficients = [jnp.broadcast_to(c, (part, width)) for c in coefficients]
    for b in range(2):
        for start in range(0, vectors, part):
            span = slice(start, start + part)
            low, high = [], []
            for r in range(PASSES):
                at = base + edge_base(0, b, r, vectors) + start
                above, below = rims(pair[at : at + part], cross[at : at + part])
                high.append(above)
                low.append(below)
            values = low + [chunk[b, r, span] for r in range(rows)] + high
            for step in range(PASSES):
                values = relaxed_rows(values, coefficients[step : len(coefficients) - step])
            for r in range(rows):
                out[b, r, span] = values[r]


def smooth(chunk, pair, cross, slot, coefficients, rim_base):
    base = edge_base(slot, 0, 0, chunk.shape[2])
    return pl.pallas_call(
        functools.partial(smooth_kernel, base, rim_base),
        out_shape=jax.ShapeDtypeStruct(chunk.shape, jnp.float32),
        compiler_params=params(),
        cost_estimate=cost(30 * chunk.size, 10 * chunk.size),
        name="smooth",
    )(chunk, pair, cross, *coefficients)


def place_of(index, o, owners_in):
    owner = (lax.axis_index("freq") ^ index) * owners_in + o
    apart = owner ^ lax.axis_index("seabed")
    return apart & 1, apart >> 1


def combine_kernel(indices, owners_in, paired, absent, *refs):
    count = len(indices)
    chunks, (t_high, t_low), (out, held) = refs[:count], refs[count : count + 2], refs[-2:]
    _, rows, vectors, width = chunks[0].shape
    owned = vectors // owners_in
    for at, ref in enumerate(chunks):
        for b in range(2):
            for r in range(rows):
                held[b, at, :, r * width : (r + 1) * width] = ref[b, r]
    half = count * vectors
    lhs_high, lhs_low = split_bf16(held[...].reshape(2 * half, rows * width))

    def times(a):
        def dot(x, w):
            return lax.dot_general(
                x, w, (((1,), (0,)), ((), ())), preferred_element_type=jnp.float32
            )

        return (dot(lhs_low, t_high[a]) + dot(lhs_high, t_low[a])) + dot(lhs_high, t_high[a])

    by_real, by_imag = times(0), times(1)
    real = by_real[:half] - by_imag[half:]
    imag = by_imag[:half] + by_real[half:]

    def place(index, o):
        if not paired:
            return index * owners_in + o
        core, chip = place_of(index, o, owners_in)
        return core * (out.shape[0] // 2) + (chip if absent else indices.index(index))

    for at, index in enumerate(indices):
        for o in range(owners_in):
            span = slice((at * owners_in + o) * owned, (at * owners_in + o + 1) * owned)
            out[place(index, o), 0] = real[span]
            out[place(index, o), 1] = imag[span]
    for index in absent:
        for o in range(owners_in):
            out[place(index, o)] = jnp.zeros(out.shape[1:], out.dtype)


def combine(chunks, split, owners_in, places, paired, absent=()):
    t_high, t_low = split
    cells, sensors = t_high.shape[1:]
    indices = sorted(chunks)
    _, _, vectors, _ = chunks[indices[0]].shape
    owned = vectors // owners_in
    whole = len(indices) * vectors
    return pl.pallas_call(
        functools.partial(combine_kernel, indices, owners_in, paired, absent),
        out_shape=jax.ShapeDtypeStruct((places, 2, owned, sensors), jnp.float32),
        scratch_shapes=[pltpu.VMEM((2, len(indices), vectors, cells), jnp.float32)],
        compiler_params=params(),
        cost_estimate=cost(
            24 * whole * sensors * cells,
            8 * sensors * cells + 8 * whole * cells + 16 * whole * sensors,
        ),
        name="combine",
    )(*[chunks[i] for i in indices], t_high, t_low)


def merge_kernel(late, owners_in, most, most_moved, tail, tail_moved, *outs):
    chips = [place_of(index, 0, owners_in)[1] for index in late]
    final = [tail[i] + tail_moved[i] for i in range(len(late))]
    for d, out in enumerate(outs):
        value = most[d] + most_moved[d]
        for chip, add in zip(chips, final):
            value = value + pick(chip == d, add, jnp.zeros_like(add))
        out[...] = value


def merge(late, owners_in, most, most_moved, tail, tail_moved):
    shape = jax.ShapeDtypeStruct(most.shape[1:], jnp.float32)
    return pl.pallas_call(
        functools.partial(merge_kernel, late, owners_in),
        out_shape=[shape] * most_moved.shape[0],
        compiler_params=params(),
        cost_estimate=cost(4 * most.size, 12 * most.size),
        name="merge",
    )(most, most_moved, tail, tail_moved)


def xor_pairs(count, apart):
    return [(i, i ^ apart) for i in range(count)]


def neighbours(pair, cross, strips):
    inner = [(i, (i + 1) % strips) for i in range(1, strips, 2)]
    inner = inner + [(b, a) for a, b in inner]
    cross = lax.ppermute(cross, "seabed", inner)
    pair = lax.ppermute(pair, "seabed", xor_pairs(strips, 1))
    return pair, cross


def paired_shards(field, coefficient, split_of, table, freq_count, strips):
    vectors = field.shape[0]
    chunks, pair, cross = transform(field, table, coefficient, freq_count, (2,))

    def swap(m, chunk):
        return lax.ppermute(chunk, "freq", xor_pairs(freq_count, m))

    def relax(chunk, edge, slot):
        return smooth(chunk, *edge, slot, coefficients, rim_base)

    first = swap(1, chunks[1])
    third = swap(3, chunks[3])
    edge = neighbours(pair, cross, strips)
    split = split_of()
    coefficients = (coefficient, *edge)
    rim_base = edge_base(1, 0, 0, vectors)
    second = swap(2, relax(chunks[2], edge, 0))
    mid_edge = neighbours(*edges([chunks[0], first]), strips)
    own = relax(chunks[0], mid_edge, 0)
    third_edge = neighbours(*edges([third]), strips)
    first = relax(first, mid_edge, 1)
    third = relax(third, third_edge, 0)
    most = combine({0: own, 1: first}, split, 2, strips, True, (2, 3))

    def to_core(partial):
        send = partial[partial.shape[0] // 2 :]
        return lax.ppermute(send, "seabed", xor_pairs(strips, 1))

    most_moved = to_core(most)
    tail = combine({2: second, 3: third}, split, 2, strips // 2, True)
    chips = merge((2, 3), 2, most, most_moved, tail, to_core(tail))
    total = chips[0]
    for d in range(1, strips // 2):
        total = total + lax.ppermute(chips[d], "seabed", xor_pairs(strips, 2 * d))
    return total


def plain_shards(field, coefficient, split_of, table, freq_count, strips):
    _, rows = field.shape[:2]
    spectrum, _, _ = transform(field, table, coefficient, freq_count, ())
    spectrum = jnp.stack(spectrum)
    spectrum = lax.all_to_all(spectrum, "freq", split_axis=0, concat_axis=0, tiled=True)
    chunks = list(spectrum)
    rim = PASSES - 1
    even = even_strip()
    first_c, last_c = coefficient[:rim], coefficient[rows - rim :]
    pair_c, cross_c = pick(even, last_c, first_c), pick(even, first_c, last_c)
    coefficients = (coefficient, *neighbours(pair_c, cross_c, strips))
    edge = neighbours(*edges(chunks), strips)
    chunks = [smooth(c, *edge, i, coefficients, 0) for i, c in enumerate(chunks)]
    owners_in = strips // freq_count
    partial = combine(dict(enumerate(chunks)), split_of(), owners_in, strips, False)
    got = lax.all_to_all(partial, "seabed", split_axis=0, concat_axis=0, tiled=True)
    return got.sum(0)


def shards(uplift, coefficient, transfer):
    vectors, steps, _, _ = uplift.shape
    freq_count, strips = FD * lax.axis_size("freq"), lax.axis_size("seabed")
    owned = vectors * freq_count // strips
    paired = (
        strips == 8
        and freq_count == 4
        and vectors == 2 * owned
        and owned == 2 * GROUP
    )
    slots = np.arange(freq_count)
    order = slots[:, None] ^ slots[None, :] if paired else slots[None, :]
    table = transform_operand(steps, freq_count, order)
    field = jnp.transpose(uplift, (0, 2, 1, 3))
    run = paired_shards if paired else plain_shards
    total = run(
        field,
        coefficient,
        lambda: split_transfer(transfer[0]),
        table,
        freq_count,
        strips,
    )
    return jnp.transpose(total, (1, 0, 2))[:, None]


def solution(mesh):
    placed = (P("freq", None, "seabed", None), P("seabed", None), P("freq", None, None, "seabed"))
    return jax.shard_map(
        shards,
        mesh=mesh,
        in_specs=placed,
        out_specs=P("seabed", "freq", None, None),
        check_vma=False,
    )
```

```python
import functools
import math

import jax
import jax.numpy as jnp
import numpy as np
from jax import lax
from jax.experimental import pallas as pl
from jax.experimental.pallas import tpu as pltpu
from jax.sharding import PartitionSpec as P


FD = 1
PASSES = 3
GROUP = 8
GRANT = 16 * 1024 * 1024


def params():
    return pltpu.CompilerParams(vmem_limit_bytes=GRANT)


def cost(flops, moved):
    return pl.CostEstimate(flops=flops, bytes_accessed=moved, transcendentals=0)


def in_hbm(array):
    return pltpu.with_memory_space_constraint(array, pltpu.HBM)


def even_strip():
    return lax.rem(lax.axis_index("seabed"), 2) == 0


def pick(flag, one, other):
    return jnp.where(jnp.full(one.shape, flag), one, other)


def dft_table(steps_count, freq_count):
    times = np.arange(steps_count)
    freqs = np.arange(freq_count)
    phase = (freqs[:, None] * times[None, :] % steps_count) * (2.0 * math.pi / steps_count)
    scale = 1.0 / math.sqrt(steps_count)
    return (np.stack([np.cos(phase), -np.sin(phase)], 1) * scale).astype(np.float32)


def split_bf16(values):
    high = values.astype(jnp.bfloat16)
    low = (values - high.astype(values.dtype)).astype(jnp.bfloat16)
    return high, low


def transform_operand(steps_count, freq_count, order):
    table = dft_table(steps_count, freq_count)[order]
    parts = np.stack([x.astype(np.float32) for x in split_bf16(table)], 1)
    sources = parts.shape[0]
    wide = np.broadcast_to(parts[..., None, :], (*parts.shape[:-1], GROUP, steps_count))
    return jnp.asarray(wide.reshape(sources, -1, GROUP * steps_count), jnp.float32)


def edge_base(slot, b, r, vectors):
    return ((slot * 2 + b) * PASSES + r) * vectors


def transform_kernel(slots, edged, field_hbm, table_hbm, own_hbm, *refs):
    outs, pair, crosses = refs[:slots], refs[slots], refs[slots + 1 : -6]
    field, table, own_c, field_sem, table_sem, own_sem = refs[-6:]
    vectors, rows, steps, width = field.shape
    blocks = vectors // GROUP
    even = even_strip()
    source = lax.axis_index("freq") if table_hbm.shape[0] > 1 else 0
    get_table = pltpu.make_async_copy(table_hbm.at[source], table, table_sem)
    get_table.start()
    get_own = pltpu.make_async_copy(own_hbm, own_c, own_sem)
    get_own.start()

    def get(i):
        at = pl.ds(i * GROUP, GROUP)
        return pltpu.make_async_copy(field_hbm.at[at], field.at[at], field_sem.at[i])

    for i in range(blocks):
        get(i).start()
    get_own.wait()
    rim = PASSES - 1
    last_c, first_c = own_c[rows - rim :], own_c[:rim]
    for ref, one, other in ((pair, last_c, first_c), (crosses[0], first_c, last_c)):
        base = ref.shape[0] - GROUP
        ref[base : base + rim] = pick(even, one, other)
        ref[base + rim :] = jnp.zeros((GROUP - rim, width), jnp.float32)
    get_table.wait()
    short = table[...]
    shape = (short.shape[0], GROUP, short.shape[1])
    mine = lax.broadcasted_iota(jnp.int32, shape, 1)
    column = lax.broadcasted_iota(jnp.int32, shape, 2)
    full = jnp.where(
        (column >= mine * steps) & (column < (mine + 1) * steps), short[:, None], 0.0
    )
    full = full.reshape(-1, short.shape[1]).astype(jnp.bfloat16)
    for i in range(blocks):
        get(i).wait()
        span = slice(i * GROUP, (i + 1) * GROUP)
        data = jnp.concatenate(
            [field[span, r].reshape(GROUP * steps, width) for r in range(rows)], axis=1
        )
        both = jnp.dot(full, data, preferred_element_type=jnp.float32)
        half = both.shape[0] // 2
        values = both[:half] + both[half:]
        for slot in range(slots):
            for b in range(2):
                at = (slot * 2 + b) * GROUP
                for r in range(rows):
                    piece = values[at : at + GROUP, r * width : (r + 1) * width]
                    outs[slot][b, r, span] = piece
                if slot not in edged:
                    continue
                for r in range(PASSES):
                    row = (rows - PASSES + r) * width
                    last = values[at : at + GROUP, row : row + width]
                    first = values[at : at + GROUP, r * width : (r + 1) * width]
                    to = edge_base(edged.index(slot), b, r, vectors) + i * GROUP
                    pair[to : to + GROUP] = pick(even, last, first)
                    to = edge_base(0, b, r, vectors) + i * GROUP
                    crosses[edged.index(slot)][to : to + GROUP] = pick(even, first, last)


def transform(field, table, coefficient, slots, edged):
    vectors, rows, steps, width = field.shape
    chunk = jax.ShapeDtypeStruct((2, rows, vectors, width), jnp.float32)
    size = edge_base(1, 0, 0, vectors)
    pair = (len(edged) * size + GROUP, width)
    crosses = [(size * bool(edged) + GROUP, width)] + [(size, width)] * (len(edged) - 1)
    edges = [jax.ShapeDtypeStruct(shape, jnp.float32) for shape in (pair, *crosses)]
    hbm = pl.BlockSpec(memory_space=pltpu.HBM)
    vmem = pl.BlockSpec(memory_space=pltpu.VMEM)
    outs = pl.pallas_call(
        functools.partial(transform_kernel, slots, edged),
        out_shape=[chunk] * slots + edges,
        in_specs=[hbm, hbm, hbm],
        out_specs=[vmem] * (slots + len(edges)),
        scratch_shapes=[
            pltpu.VMEM(field.shape, field.dtype),
            pltpu.VMEM(table.shape[1:], table.dtype),
            pltpu.VMEM(coefficient.shape, coefficient.dtype),
            pltpu.SemaphoreType.DMA((vectors // GROUP,)),
            pltpu.SemaphoreType.DMA(()),
            pltpu.SemaphoreType.DMA(()),
        ],
        compiler_params=params(),
        cost_estimate=cost(
            2 * table.shape[1] * table.shape[2] * rows * width * vectors,
            vectors * rows * width * (2 * steps + 8 * slots),
        ),
        name="transform",
    )(*map(in_hbm, (field, table, coefficient)))
    return outs[:slots], outs[slots], outs[slots + 1 :]


def split_kernel(x_ref, high_ref, low_ref):
    high_ref[0], low_ref[0] = split_bf16(jnp.transpose(x_ref[0]))


def split_transfer(transfer):
    parts, sensors, cells = transfer.shape
    block = pl.BlockSpec((1, cells, sensors), lambda a: (a, 0, 0))
    return pl.pallas_call(
        split_kernel,
        out_shape=[jax.ShapeDtypeStruct((parts, cells, sensors), jnp.bfloat16)] * 2,
        grid=(parts,),
        in_specs=[pl.BlockSpec((1, sensors, cells), lambda a: (a, 0, 0))],
        out_specs=[block, block],
        compiler_params=params(),
        cost_estimate=cost(2 * transfer.size, 8 * transfer.size),
        name="split_transfer",
    )(in_hbm(transfer))


def relaxed_rows(rows, coefficients):
    width = rows[0].shape[-1]
    lane = lax.broadcasted_iota(jnp.int32, rows[0].shape, 1)
    first, last = lane == 0, lane == width - 1
    out = []
    for i in range(1, len(rows) - 1):
        centre = rows[i]
        left = jnp.where(first, 0.0, pltpu.roll(centre, 1, 1))
        right = jnp.where(last, 0.0, pltpu.roll(centre, width - 1, 1))
        beside = (rows[i + 1] + rows[i - 1]) + (left + right)
        out.append(centre + coefficients[i - 1] * (beside - 4.0 * centre))
    return out


def edges_kernel(count, crossing, *refs):
    chunks, outs = refs[:count], refs[count:]
    _, rows, vectors, _ = chunks[0].shape
    even = even_strip().astype(jnp.int32)

    def put(ref, slot, chunk, last):
        for b in range(2):
            for r in range(PASSES):
                at = edge_base(slot, b, r, vectors)
                ref[at : at + vectors] = chunk[b, last * (rows - PASSES) + r]

    if crossing:
        for slot, index in enumerate(crossing):
            put(outs[-1], slot, chunks[index], 1 - even)
    if len(outs) > 1 or not crossing:
        for index, chunk in enumerate(chunks):
            put(outs[0], index, chunk, even)


def edges(chunks, crossing, pair=True):
    _, _, vectors, width = chunks[0].shape
    counts = [len(chunks)] * pair + [len(crossing)] * bool(crossing)
    shapes = [(edge_base(n, 0, 0, vectors), width) for n in counts]
    return pl.pallas_call(
        functools.partial(edges_kernel, len(chunks), crossing),
        out_shape=[jax.ShapeDtypeStruct(shape, jnp.float32) for shape in shapes],
        compiler_params=params(),
        cost_estimate=cost(0, 16 * shapes[0][0] * width),
        name="edges",
    )(*chunks)


def smooth_kernel(pair_slot, cross_slot, chunk, pair, cross, own_c, pair_c, cross_c, out):
    _, rows, vectors, width = chunk.shape
    rim = PASSES - 1
    even = even_strip()
    part = math.gcd(vectors, 2 * GROUP)
    strip = lax.axis_index("seabed")
    inside = (strip > 0) & (strip < lax.axis_size("seabed") - 1)

    def rims(one, other):
        other = pick(inside, other, jnp.zeros_like(other))
        return pick(even, one, other), pick(even, other, one)

    def rim_of(ref):
        base = ref.shape[0] - GROUP
        return ref[base : base + rim]

    high_c, low_c = rims(rim_of(pair_c), rim_of(cross_c))
    coefficients = [low_c[i : i + 1] for i in range(rim)]
    coefficients += [own_c[i : i + 1] for i in range(rows)]
    coefficients += [high_c[i : i + 1] for i in range(rim)]
    coefficients = [jnp.broadcast_to(c, (part, width)) for c in coefficients]
    for b in range(2):
        for start in range(0, vectors, part):
            span = slice(start, start + part)
            low, high = [], []
            for r in range(PASSES):
                at = edge_base(pair_slot, b, r, vectors) + start
                to = edge_base(cross_slot, b, r, vectors) + start
                above, below = rims(pair[at : at + part], cross[to : to + part])
                high.append(above)
                low.append(below)
            values = low + [chunk[b, r, span] for r in range(rows)] + high
            for step in range(PASSES):
                values = relaxed_rows(values, coefficients[step : len(coefficients) - step])
            for r in range(rows):
                out[b, r, span] = values[r]


def smooth(chunk, pair, pair_slot, cross, cross_slot, coefficients):
    return pl.pallas_call(
        functools.partial(smooth_kernel, pair_slot, cross_slot),
        out_shape=jax.ShapeDtypeStruct(chunk.shape, jnp.float32),
        compiler_params=params(),
        cost_estimate=cost(30 * chunk.size, 10 * chunk.size),
        name="smooth",
    )(chunk, pair, cross, *coefficients)


def place_of(index, o, owners_in):
    owner = (lax.axis_index("freq") ^ index) * owners_in + o
    apart = owner ^ lax.axis_index("seabed")
    return apart & 1, apart >> 1


def combine_kernel(indices, owners_in, paired, absent, *refs):
    count = len(indices)
    chunks, (t_high, t_low), (out, held) = refs[:count], refs[count : count + 2], refs[-2:]
    _, rows, vectors, width = chunks[0].shape
    owned = vectors // owners_in
    for at, ref in enumerate(chunks):
        for b in range(2):
            for r in range(rows):
                held[b, at, :, r * width : (r + 1) * width] = ref[b, r]
    half = count * vectors
    lhs_high, lhs_low = split_bf16(held[...].reshape(2 * half, rows * width))

    def times(a):
        def dot(x, w):
            return lax.dot_general(
                x, w, (((1,), (0,)), ((), ())), preferred_element_type=jnp.float32
            )

        return (dot(lhs_low, t_high[a]) + dot(lhs_high, t_low[a])) + dot(lhs_high, t_high[a])

    by_real, by_imag = times(0), times(1)
    real = by_real[:half] - by_imag[half:]
    imag = by_imag[:half] + by_real[half:]

    def place(index, o):
        if not paired:
            return index * owners_in + o
        core, chip = place_of(index, o, owners_in)
        return core * (out.shape[0] // 2) + (chip if absent else indices.index(index))

    for at, index in enumerate(indices):
        for o in range(owners_in):
            span = slice((at * owners_in + o) * owned, (at * owners_in + o + 1) * owned)
            out[place(index, o), 0] = real[span]
            out[place(index, o), 1] = imag[span]
    for index in absent:
        for o in range(owners_in):
            out[place(index, o)] = jnp.zeros(out.shape[1:], out.dtype)


def combine(chunks, split, owners_in, places, paired, absent=()):
    t_high, t_low = split
    cells, sensors = t_high.shape[1:]
    indices = sorted(chunks)
    _, _, vectors, _ = chunks[indices[0]].shape
    owned = vectors // owners_in
    whole = len(indices) * vectors
    return pl.pallas_call(
        functools.partial(combine_kernel, indices, owners_in, paired, absent),
        out_shape=jax.ShapeDtypeStruct((places, 2, owned, sensors), jnp.float32),
        scratch_shapes=[pltpu.VMEM((2, len(indices), vectors, cells), jnp.float32)],
        compiler_params=params(),
        cost_estimate=cost(
            24 * whole * sensors * cells,
            8 * sensors * cells + 8 * whole * cells + 16 * whole * sensors,
        ),
        name="combine",
    )(*[chunks[i] for i in indices], t_high, t_low)


def merge_kernel(late, owners_in, most, most_moved, tail, tail_moved, *outs):
    chips = [place_of(index, 0, owners_in)[1] for index in late]
    final = [tail[i] + tail_moved[i] for i in range(len(late))]
    for d, out in enumerate(outs):
        value = most[d] + most_moved[d]
        for chip, add in zip(chips, final):
            value = value + pick(chip == d, add, jnp.zeros_like(add))
        out[...] = value


def merge(late, owners_in, most, most_moved, tail, tail_moved):
    shape = jax.ShapeDtypeStruct(most.shape[1:], jnp.float32)
    return pl.pallas_call(
        functools.partial(merge_kernel, late, owners_in),
        out_shape=[shape] * most_moved.shape[0],
        compiler_params=params(),
        cost_estimate=cost(4 * most.size, 12 * most.size),
        name="merge",
    )(most, most_moved, tail, tail_moved)


def xor_pairs(count, apart):
    return [(i, i ^ apart) for i in range(count)]


def to_pair(edge, strips):
    return lax.ppermute(edge, "seabed", xor_pairs(strips, 1))


def to_cross(edge, strips):
    inner = [(i, (i + 1) % strips) for i in range(1, strips, 2)]
    return lax.ppermute(edge, "seabed", inner + [(b, a) for a, b in inner])


def paired_shards(field, coefficient, split_of, table, freq_count, strips):
    chunks, pair, crosses = transform(field, table, coefficient, freq_count, (2, 0))

    def swap(m, chunk):
        return lax.ppermute(chunk, "freq", xor_pairs(freq_count, m))

    def relax(chunk, pair, pair_slot, cross):
        return smooth(chunk, pair, pair_slot, cross, 0, coefficients)

    first = swap(1, chunks[1])
    third = swap(3, chunks[3])
    cross2 = to_cross(crosses[0], strips)
    pair = to_pair(pair, strips)
    cross0 = to_cross(crosses[1], strips)
    coefficients = (coefficient, pair, cross2)
    split = split_of()
    second = swap(2, relax(chunks[2], pair, 0, cross2))
    own = relax(chunks[0], pair, 1, cross0)
    (cross1,) = edges([first], (0,), False)
    cross1 = to_cross(cross1, strips)
    pair, cross3 = edges([first, third], (1,))
    cross3 = to_cross(cross3, strips)
    pair = to_pair(pair, strips)
    first = relax(first, pair, 0, cross1)
    third = relax(third, pair, 1, cross3)
    most = combine({0: own, 1: first}, split, 2, strips, True, (2, 3))

    def to_core(partial):
        send = partial[partial.shape[0] // 2 :]
        return lax.ppermute(send, "seabed", xor_pairs(strips, 1))

    most_moved = to_core(most)
    tail = combine({2: second, 3: third}, split, 2, strips // 2, True)
    chips = merge((2, 3), 2, most, most_moved, tail, to_core(tail))
    total = chips[0]
    for d in range(1, strips // 2):
        total = total + lax.ppermute(chips[d], "seabed", xor_pairs(strips, 2 * d))
    return total


def plain_shards(field, coefficient, split_of, table, freq_count, strips):
    spectrum, pair_c, (cross_c,) = transform(field, table, coefficient, freq_count, ())
    spectrum = jnp.stack(spectrum)
    spectrum = lax.all_to_all(spectrum, "freq", split_axis=0, concat_axis=0, tiled=True)
    chunks = list(spectrum)
    pair_c = to_pair(pair_c, strips)
    cross_c = to_cross(cross_c, strips)
    coefficients = (coefficient, pair_c, cross_c)
    pair, cross = edges(chunks, tuple(range(len(chunks))))
    pair, cross = to_pair(pair, strips), to_cross(cross, strips)
    chunks = [smooth(c, pair, i, cross, i, coefficients) for i, c in enumerate(chunks)]
    owners_in = strips // freq_count
    partial = combine(dict(enumerate(chunks)), split_of(), owners_in, strips, False)
    got = lax.all_to_all(partial, "seabed", split_axis=0, concat_axis=0, tiled=True)
    return got.sum(0)


def shards(uplift, coefficient, transfer):
    vectors, steps, _, _ = uplift.shape
    freq_count, strips = FD * lax.axis_size("freq"), lax.axis_size("seabed")
    owned = vectors * freq_count // strips
    paired = (
        strips == 8
        and freq_count == 4
        and vectors == 2 * owned
        and owned == 2 * GROUP
    )
    slots = np.arange(freq_count)
    order = slots[:, None] ^ slots[None, :] if paired else slots[None, :]
    table = transform_operand(steps, freq_count, order)
    field = jnp.transpose(uplift, (0, 2, 1, 3))
    run = paired_shards if paired else plain_shards
    total = run(
        field,
        coefficient,
        lambda: split_transfer(transfer[0]),
        table,
        freq_count,
        strips,
    )
    return jnp.transpose(total, (1, 0, 2))[:, None]


def solution(mesh):
    placed = (P("freq", None, "seabed", None), P("seabed", None), P("freq", None, None, "seabed"))
    return jax.shard_map(
        shards,
        mesh=mesh,
        in_specs=placed,
        out_specs=P("seabed", "freq", None, None),
        check_vma=False,
    )
```

```python
import functools
import math

import jax
import jax.numpy as jnp
import numpy as np
from jax import lax
from jax.experimental import pallas as pl
from jax.experimental.pallas import tpu as pltpu
from jax.sharding import PartitionSpec as P


FD = 1
PASSES = 3
GROUP = 8
GRANT = 16 * 1024 * 1024


def params():
    return pltpu.CompilerParams(vmem_limit_bytes=GRANT)


def cost(flops, moved):
    return pl.CostEstimate(flops=flops, bytes_accessed=moved, transcendentals=0)


def in_hbm(array):
    return pltpu.with_memory_space_constraint(array, pltpu.HBM)


def even_strip():
    return lax.rem(lax.axis_index("seabed"), 2) == 0


def pick(flag, one, other):
    return jnp.where(jnp.full(one.shape, flag), one, other)


def dft_table(steps_count, freq_count):
    times = np.arange(steps_count)
    freqs = np.arange(freq_count)
    phase = (freqs[:, None] * times[None, :] % steps_count) * (2.0 * math.pi / steps_count)
    scale = 1.0 / math.sqrt(steps_count)
    return (np.stack([np.cos(phase), -np.sin(phase)], 1) * scale).astype(np.float32)


def split_bf16(values):
    high = values.astype(jnp.bfloat16)
    low = (values - high.astype(values.dtype)).astype(jnp.bfloat16)
    return high, low


def transform_operand(steps_count, freq_count, order):
    table = dft_table(steps_count, freq_count)[order]
    parts = np.stack([x.astype(np.float32) for x in split_bf16(table)], 1)
    sources = parts.shape[0]
    wide = np.broadcast_to(parts[..., None, :], (*parts.shape[:-1], GROUP, steps_count))
    return jnp.asarray(wide.reshape(sources, -1, GROUP * steps_count), jnp.float32)


def edge_base(slot, b, r, vectors):
    return ((slot * 2 + b) * PASSES + r) * vectors


def transform_kernel(slots, edged, field_hbm, table_hbm, own_hbm, *refs):
    outs, pair, crosses = refs[:slots], refs[slots], refs[slots + 1 : -6]
    field, table, own_c, field_sem, table_sem, own_sem = refs[-6:]
    vectors, rows, steps, width = field.shape
    blocks = vectors // GROUP
    even = even_strip()
    source = lax.axis_index("freq") if table_hbm.shape[0] > 1 else 0
    get_table = pltpu.make_async_copy(table_hbm.at[source], table, table_sem)
    get_table.start()
    get_own = pltpu.make_async_copy(own_hbm, own_c, own_sem)
    get_own.start()

    def get(i):
        at = pl.ds(i * GROUP, GROUP)
        return pltpu.make_async_copy(field_hbm.at[at], field.at[at], field_sem.at[i])

    for i in range(blocks):
        get(i).start()
    get_own.wait()
    rim = PASSES - 1
    last_c, first_c = own_c[rows - rim :], own_c[:rim]
    for ref, one, other in ((pair, last_c, first_c), (crosses[0], first_c, last_c)):
        base = ref.shape[0] - GROUP
        ref[base : base + rim] = pick(even, one, other)
        ref[base + rim :] = jnp.zeros((GROUP - rim, width), jnp.float32)
    get_table.wait()
    short = table[...]
    shape = (short.shape[0], GROUP, short.shape[1])
    mine = lax.broadcasted_iota(jnp.int32, shape, 1)
    column = lax.broadcasted_iota(jnp.int32, shape, 2)
    full = jnp.where(
        (column >= mine * steps) & (column < (mine + 1) * steps), short[:, None], 0.0
    )
    full = full.reshape(-1, short.shape[1]).astype(jnp.bfloat16)
    for i in range(blocks):
        get(i).wait()
        span = slice(i * GROUP, (i + 1) * GROUP)
        data = jnp.concatenate(
            [field[span, r].reshape(GROUP * steps, width) for r in range(rows)], axis=1
        )
        both = jnp.dot(full, data, preferred_element_type=jnp.float32)
        half = both.shape[0] // 2
        values = both[:half] + both[half:]
        for slot in range(slots):
            for b in range(2):
                at = (slot * 2 + b) * GROUP
                for r in range(rows):
                    piece = values[at : at + GROUP, r * width : (r + 1) * width]
                    outs[slot][b, r, span] = piece
                if slot not in sum(edged, ()):
                    continue
                group = [slot in g for g in edged].index(True)
                for r in range(PASSES):
                    row = (rows - PASSES + r) * width
                    last = values[at : at + GROUP, row : row + width]
                    first = values[at : at + GROUP, r * width : (r + 1) * width]
                    to = edge_base(sum(edged, ()).index(slot), b, r, vectors) + i * GROUP
                    pair[to : to + GROUP] = pick(even, last, first)
                    to = edge_base(edged[group].index(slot), b, r, vectors) + i * GROUP
                    crosses[group][to : to + GROUP] = pick(even, first, last)


def transform(field, table, coefficient, slots, edged):
    vectors, rows, steps, width = field.shape
    chunk = jax.ShapeDtypeStruct((2, rows, vectors, width), jnp.float32)
    size = edge_base(1, 0, 0, vectors)
    pair = (sum(map(len, edged)) * size + GROUP, width)
    crosses = [(len(g) * size + GROUP * (i == 0), width) for i, g in enumerate(edged)]
    edges = [jax.ShapeDtypeStruct(shape, jnp.float32) for shape in (pair, *crosses)]
    hbm = pl.BlockSpec(memory_space=pltpu.HBM)
    vmem = pl.BlockSpec(memory_space=pltpu.VMEM)
    outs = pl.pallas_call(
        functools.partial(transform_kernel, slots, edged),
        out_shape=[chunk] * slots + edges,
        in_specs=[hbm, hbm, hbm],
        out_specs=[vmem] * (slots + len(edges)),
        scratch_shapes=[
            pltpu.VMEM(field.shape, field.dtype),
            pltpu.VMEM(table.shape[1:], table.dtype),
            pltpu.VMEM(coefficient.shape, coefficient.dtype),
            pltpu.SemaphoreType.DMA((vectors // GROUP,)),
            pltpu.SemaphoreType.DMA(()),
            pltpu.SemaphoreType.DMA(()),
        ],
        compiler_params=params(),
        cost_estimate=cost(
            2 * table.shape[1] * table.shape[2] * rows * width * vectors,
            vectors * rows * width * (2 * steps + 8 * slots),
        ),
        name="transform",
    )(*map(in_hbm, (field, table, coefficient)))
    return outs[:slots], outs[slots], outs[slots + 1 :]


def split_kernel(x_ref, high_ref, low_ref):
    high_ref[0], low_ref[0] = split_bf16(jnp.transpose(x_ref[0]))


def split_transfer(transfer):
    parts, sensors, cells = transfer.shape
    block = pl.BlockSpec((1, cells, sensors), lambda a: (a, 0, 0))
    return pl.pallas_call(
        split_kernel,
        out_shape=[jax.ShapeDtypeStruct((parts, cells, sensors), jnp.bfloat16)] * 2,
        grid=(parts,),
        in_specs=[pl.BlockSpec((1, sensors, cells), lambda a: (a, 0, 0))],
        out_specs=[block, block],
        compiler_params=params(),
        cost_estimate=cost(2 * transfer.size, 8 * transfer.size),
        name="split_transfer",
    )(in_hbm(transfer))


def relaxed_rows(rows, coefficients):
    width = rows[0].shape[-1]
    lane = lax.broadcasted_iota(jnp.int32, rows[0].shape, 1)
    first, last = lane == 0, lane == width - 1
    out = []
    for i in range(1, len(rows) - 1):
        centre = rows[i]
        left = jnp.where(first, 0.0, pltpu.roll(centre, 1, 1))
        right = jnp.where(last, 0.0, pltpu.roll(centre, width - 1, 1))
        beside = (rows[i + 1] + rows[i - 1]) + (left + right)
        out.append(centre + coefficients[i - 1] * (beside - 4.0 * centre))
    return out


def edges_kernel(count, crossing, *refs):
    chunks, outs = refs[:count], refs[count:]
    _, rows, vectors, _ = chunks[0].shape
    even = even_strip().astype(jnp.int32)

    def put(ref, slot, chunk, last):
        for b in range(2):
            for r in range(PASSES):
                at = edge_base(slot, b, r, vectors)
                ref[at : at + vectors] = chunk[b, last * (rows - PASSES) + r]

    if crossing:
        for slot, index in enumerate(crossing):
            put(outs[-1], slot, chunks[index], 1 - even)
    if len(outs) > 1 or not crossing:
        for index, chunk in enumerate(chunks):
            put(outs[0], index, chunk, even)


def edges(chunks, crossing, pair=True):
    _, _, vectors, width = chunks[0].shape
    counts = [len(chunks)] * pair + [len(crossing)] * bool(crossing)
    shapes = [(edge_base(n, 0, 0, vectors), width) for n in counts]
    return pl.pallas_call(
        functools.partial(edges_kernel, len(chunks), crossing),
        out_shape=[jax.ShapeDtypeStruct(shape, jnp.float32) for shape in shapes],
        compiler_params=params(),
        cost_estimate=cost(0, 16 * shapes[0][0] * width),
        name="edges",
    )(*chunks)


def smooth_kernel(pair_slot, cross_slot, chunk, pair, cross, own_c, pair_c, cross_c, out):
    _, rows, vectors, width = chunk.shape
    rim = PASSES - 1
    even = even_strip()
    part = math.gcd(vectors, 2 * GROUP)
    strip = lax.axis_index("seabed")
    inside = (strip > 0) & (strip < lax.axis_size("seabed") - 1)

    def rims(one, other):
        other = pick(inside, other, jnp.zeros_like(other))
        return pick(even, one, other), pick(even, other, one)

    def rim_of(ref):
        base = ref.shape[0] - GROUP
        return ref[base : base + rim]

    high_c, low_c = rims(rim_of(pair_c), rim_of(cross_c))
    coefficients = [low_c[i : i + 1] for i in range(rim)]
    coefficients += [own_c[i : i + 1] for i in range(rows)]
    coefficients += [high_c[i : i + 1] for i in range(rim)]
    coefficients = [jnp.broadcast_to(c, (part, width)) for c in coefficients]
    for b in range(2):
        for start in range(0, vectors, part):
            span = slice(start, start + part)
            low, high = [], []
            for r in range(PASSES):
                at = edge_base(pair_slot, b, r, vectors) + start
                to = edge_base(cross_slot, b, r, vectors) + start
                above, below = rims(pair[at : at + part], cross[to : to + part])
                high.append(above)
                low.append(below)
            values = low + [chunk[b, r, span] for r in range(rows)] + high
            for step in range(PASSES):
                values = relaxed_rows(values, coefficients[step : len(coefficients) - step])
            for r in range(rows):
                out[b, r, span] = values[r]


def smooth(chunk, pair, pair_slot, cross, cross_slot, coefficients):
    return pl.pallas_call(
        functools.partial(smooth_kernel, pair_slot, cross_slot),
        out_shape=jax.ShapeDtypeStruct(chunk.shape, jnp.float32),
        compiler_params=params(),
        cost_estimate=cost(30 * chunk.size, 10 * chunk.size),
        name="smooth",
    )(chunk, pair, cross, *coefficients)


def place_of(index, o, owners_in):
    owner = (lax.axis_index("freq") ^ index) * owners_in + o
    apart = owner ^ lax.axis_index("seabed")
    return apart & 1, apart >> 1


def combine_kernel(indices, owners_in, paired, absent, *refs):
    count = len(indices)
    chunks, (t_high, t_low), (out, held) = refs[:count], refs[count : count + 2], refs[-2:]
    _, rows, vectors, width = chunks[0].shape
    owned = vectors // owners_in
    for at, ref in enumerate(chunks):
        for b in range(2):
            for r in range(rows):
                held[b, at, :, r * width : (r + 1) * width] = ref[b, r]
    half = count * vectors
    lhs_high, lhs_low = split_bf16(held[...].reshape(2 * half, rows * width))

    def times(a):
        def dot(x, w):
            return lax.dot_general(
                x, w, (((1,), (0,)), ((), ())), preferred_element_type=jnp.float32
            )

        return (dot(lhs_low, t_high[a]) + dot(lhs_high, t_low[a])) + dot(lhs_high, t_high[a])

    by_real, by_imag = times(0), times(1)
    real = by_real[:half] - by_imag[half:]
    imag = by_imag[:half] + by_real[half:]

    def place(index, o):
        if not paired:
            return index * owners_in + o
        core, chip = place_of(index, o, owners_in)
        return core * (out.shape[0] // 2) + (chip if absent else indices.index(index))

    for at, index in enumerate(indices):
        for o in range(owners_in):
            span = slice((at * owners_in + o) * owned, (at * owners_in + o + 1) * owned)
            out[place(index, o), 0] = real[span]
            out[place(index, o), 1] = imag[span]
    for index in absent:
        for o in range(owners_in):
            out[place(index, o)] = jnp.zeros(out.shape[1:], out.dtype)


def combine(chunks, split, owners_in, places, paired, absent=()):
    t_high, t_low = split
    cells, sensors = t_high.shape[1:]
    indices = sorted(chunks)
    _, _, vectors, _ = chunks[indices[0]].shape
    owned = vectors // owners_in
    whole = len(indices) * vectors
    return pl.pallas_call(
        functools.partial(combine_kernel, indices, owners_in, paired, absent),
        out_shape=jax.ShapeDtypeStruct((places, 2, owned, sensors), jnp.float32),
        scratch_shapes=[pltpu.VMEM((2, len(indices), vectors, cells), jnp.float32)],
        compiler_params=params(),
        cost_estimate=cost(
            24 * whole * sensors * cells,
            8 * sensors * cells + 8 * whole * cells + 16 * whole * sensors,
        ),
        name="combine",
    )(*[chunks[i] for i in indices], t_high, t_low)


def merge_kernel(late, owners_in, most, most_moved, tail, tail_moved, *outs):
    chips = [place_of(index, 0, owners_in)[1] for index in late]
    final = [tail[i] + tail_moved[i] for i in range(len(late))]
    for d, out in enumerate(outs):
        value = most[d] + most_moved[d]
        for chip, add in zip(chips, final):
            value = value + pick(chip == d, add, jnp.zeros_like(add))
        out[...] = value


def merge(late, owners_in, most, most_moved, tail, tail_moved):
    shape = jax.ShapeDtypeStruct(most.shape[1:], jnp.float32)
    return pl.pallas_call(
        functools.partial(merge_kernel, late, owners_in),
        out_shape=[shape] * most_moved.shape[0],
        compiler_params=params(),
        cost_estimate=cost(4 * most.size, 12 * most.size),
        name="merge",
    )(most, most_moved, tail, tail_moved)


def xor_pairs(count, apart):
    return [(i, i ^ apart) for i in range(count)]


def to_pair(edge, strips):
    return lax.ppermute(edge, "seabed", xor_pairs(strips, 1))


def to_cross(edge, strips):
    inner = [(i, (i + 1) % strips) for i in range(1, strips, 2)]
    return lax.ppermute(edge, "seabed", inner + [(b, a) for a, b in inner])


def paired_shards(field, coefficient, split_of, table, freq_count, strips):
    chunks, pair, crosses = transform(field, table, coefficient, freq_count, ((2,), (0, 1)))

    def swap(m, chunk):
        return lax.ppermute(chunk, "freq", xor_pairs(freq_count, m))

    def relax(chunk, pair, pair_slot, cross, cross_slot):
        return smooth(chunk, pair, pair_slot, cross, cross_slot, coefficients)

    third = swap(3, chunks[3])
    cross2 = to_cross(crosses[0], strips)
    pair = to_pair(pair, strips)
    cross01 = to_cross(crosses[1], strips)
    coefficients = (coefficient, pair, cross2)
    split = split_of()
    second = swap(2, relax(chunks[2], pair, 0, cross2, 0))
    pair3, cross3 = edges([third], (0,))
    cross3 = to_cross(cross3, strips)
    pair3 = to_pair(pair3, strips)
    first = swap(1, relax(chunks[1], pair, 2, cross01, 1))
    own = relax(chunks[0], pair, 1, cross01, 0)
    third = relax(third, pair3, 0, cross3, 0)
    most = combine({0: own, 3: third}, split, 2, strips, True, (1, 2))

    def to_core(partial):
        send = partial[partial.shape[0] // 2 :]
        return lax.ppermute(send, "seabed", xor_pairs(strips, 1))

    most_moved = to_core(most)
    tail = combine({1: first, 2: second}, split, 2, strips // 2, True)
    chips = merge((1, 2), 2, most, most_moved, tail, to_core(tail))
    total = chips[0]
    for d in range(1, strips // 2):
        total = total + lax.ppermute(chips[d], "seabed", xor_pairs(strips, 2 * d))
    return total


def plain_shards(field, coefficient, split_of, table, freq_count, strips):
    spectrum, pair_c, (cross_c,) = transform(field, table, coefficient, freq_count, ((),))
    spectrum = jnp.stack(spectrum)
    spectrum = lax.all_to_all(spectrum, "freq", split_axis=0, concat_axis=0, tiled=True)
    chunks = list(spectrum)
    pair_c = to_pair(pair_c, strips)
    cross_c = to_cross(cross_c, strips)
    coefficients = (coefficient, pair_c, cross_c)
    pair, cross = edges(chunks, tuple(range(len(chunks))))
    pair, cross = to_pair(pair, strips), to_cross(cross, strips)
    chunks = [smooth(c, pair, i, cross, i, coefficients) for i, c in enumerate(chunks)]
    owners_in = strips // freq_count
    partial = combine(dict(enumerate(chunks)), split_of(), owners_in, strips, False)
    got = lax.all_to_all(partial, "seabed", split_axis=0, concat_axis=0, tiled=True)
    return got.sum(0)


def shards(uplift, coefficient, transfer):
    vectors, steps, _, _ = uplift.shape
    freq_count, strips = FD * lax.axis_size("freq"), lax.axis_size("seabed")
    owned = vectors * freq_count // strips
    paired = (
        strips == 8
        and freq_count == 4
        and vectors == 2 * owned
        and owned == 2 * GROUP
    )
    slots = np.arange(freq_count)
    order = slots[:, None] ^ slots[None, :] if paired else slots[None, :]
    table = transform_operand(steps, freq_count, order)
    field = jnp.transpose(uplift, (0, 2, 1, 3))
    run = paired_shards if paired else plain_shards
    total = run(field, coefficient, lambda: split_transfer(transfer[0]), table, freq_count, strips)
    return jnp.transpose(total, (1, 0, 2))[:, None]


def solution(mesh):
    placed = (P("freq", None, "seabed", None), P("seabed", None), P("freq", None, None, "seabed"))
    return jax.shard_map(
        shards,
        mesh=mesh,
        in_specs=placed,
        out_specs=P("seabed", "freq", None, None),
        check_vma=False,
    )
```

```python
import functools
import math

import jax
import jax.numpy as jnp
import numpy as np
from jax import lax
from jax.experimental import pallas as pl
from jax.experimental.pallas import tpu as pltpu
from jax.sharding import PartitionSpec as P


FD = 1
PASSES = 3
GROUP = 8
GRANT = 16 * 1024 * 1024


def params():
    return pltpu.CompilerParams(vmem_limit_bytes=GRANT)


def cost(flops, moved):
    return pl.CostEstimate(flops=flops, bytes_accessed=moved, transcendentals=0)


def in_hbm(array):
    return pltpu.with_memory_space_constraint(array, pltpu.HBM)


def even_strip():
    return lax.rem(lax.axis_index("seabed"), 2) == 0


def pick(flag, one, other):
    return jnp.where(jnp.full(one.shape, flag), one, other)


def dft_table(steps_count, freq_count):
    times = np.arange(steps_count)
    freqs = np.arange(freq_count)
    phase = (freqs[:, None] * times[None, :] % steps_count) * (2.0 * math.pi / steps_count)
    scale = 1.0 / math.sqrt(steps_count)
    return (np.stack([np.cos(phase), -np.sin(phase)], 1) * scale).astype(np.float32)


def split_bf16(values):
    high = values.astype(jnp.bfloat16)
    low = (values - high.astype(values.dtype)).astype(jnp.bfloat16)
    return high, low


def transform_operand(steps_count, freq_count, order):
    table = dft_table(steps_count, freq_count)[order]
    parts = np.stack([x.astype(np.float32) for x in split_bf16(table)], 1)
    sources = parts.shape[0]
    wide = np.broadcast_to(parts[..., None, :], (*parts.shape[:-1], GROUP, steps_count))
    return jnp.asarray(wide.reshape(sources, -1, GROUP * steps_count), jnp.float32)


def edge_base(slot, b, r, vectors):
    return ((slot * 2 + b) * PASSES + r) * vectors


def transform_kernel(slots, edged, field_hbm, table_hbm, own_hbm, *refs):
    outs, pair, crosses = refs[:slots], refs[slots], refs[slots + 1 : -6]
    own_c, field, table, field_sem, table_sem, own_sem = refs[-6:]
    vectors, rows, steps, width = field.shape
    blocks = vectors // GROUP
    even = even_strip()
    source = lax.axis_index("freq") if table_hbm.shape[0] > 1 else 0
    get_field = pltpu.make_async_copy(field_hbm, field, field_sem)
    get_field.start()
    get_table = pltpu.make_async_copy(table_hbm.at[source], table, table_sem)
    get_table.start()
    get_own = pltpu.make_async_copy(own_hbm, own_c, own_sem)
    get_own.start()
    get_own.wait()
    rim = PASSES - 1
    last_c, first_c = own_c[rows - rim :], own_c[:rim]
    for ref, one, other in ((pair, last_c, first_c), (crosses[0], first_c, last_c)):
        base = ref.shape[0] - GROUP
        ref[base : base + rim] = pick(even, one, other)
        ref[base + rim :] = jnp.zeros((GROUP - rim, width), jnp.float32)
    get_table.wait()
    short = table[...]
    shape = (short.shape[0], GROUP, short.shape[1])
    mine = lax.broadcasted_iota(jnp.int32, shape, 1)
    column = lax.broadcasted_iota(jnp.int32, shape, 2)
    full = jnp.where(
        (column >= mine * steps) & (column < (mine + 1) * steps), short[:, None], 0.0
    )
    full = full.reshape(-1, short.shape[1]).astype(jnp.bfloat16)
    get_field.wait()
    for i in range(blocks):
        span = slice(i * GROUP, (i + 1) * GROUP)
        data = jnp.concatenate(
            [field[span, r].reshape(GROUP * steps, width) for r in range(rows)], axis=1
        )
        both = jnp.dot(full, data, preferred_element_type=jnp.float32)
        half = both.shape[0] // 2
        values = both[:half] + both[half:]
        for slot in range(slots):
            for b in range(2):
                at = (slot * 2 + b) * GROUP
                for r in range(rows):
                    piece = values[at : at + GROUP, r * width : (r + 1) * width]
                    outs[slot][b, r, span] = piece
                if slot not in sum(edged, ()):
                    continue
                group = [slot in g for g in edged].index(True)
                for r in range(PASSES):
                    row = (rows - PASSES + r) * width
                    last = values[at : at + GROUP, row : row + width]
                    first = values[at : at + GROUP, r * width : (r + 1) * width]
                    to = edge_base(sum(edged, ()).index(slot), b, r, vectors) + i * GROUP
                    pair[to : to + GROUP] = pick(even, last, first)
                    to = edge_base(edged[group].index(slot), b, r, vectors) + i * GROUP
                    crosses[group][to : to + GROUP] = pick(even, first, last)


def transform(field, table, coefficient, slots, edged):
    vectors, rows, steps, width = field.shape
    chunk = jax.ShapeDtypeStruct((2, rows, vectors, width), jnp.float32)
    size = edge_base(1, 0, 0, vectors)
    pair = (sum(map(len, edged)) * size + GROUP, width)
    crosses = [(len(g) * size + GROUP * (i == 0), width) for i, g in enumerate(edged)]
    edges = [jax.ShapeDtypeStruct(shape, jnp.float32) for shape in (pair, *crosses, coefficient.shape)]
    hbm = pl.BlockSpec(memory_space=pltpu.HBM)
    vmem = pl.BlockSpec(memory_space=pltpu.VMEM)
    outs = pl.pallas_call(
        functools.partial(transform_kernel, slots, edged),
        out_shape=[chunk] * slots + edges,
        in_specs=[hbm, hbm, hbm],
        out_specs=[vmem] * (slots + len(edges)),
        scratch_shapes=[
            pltpu.VMEM(field.shape, field.dtype),
            pltpu.VMEM(table.shape[1:], table.dtype),
            pltpu.SemaphoreType.DMA(()),
            pltpu.SemaphoreType.DMA(()),
            pltpu.SemaphoreType.DMA(()),
        ],
        compiler_params=params(),
        cost_estimate=cost(
            2 * table.shape[1] * table.shape[2] * rows * width * vectors,
            vectors * rows * width * (2 * steps + 8 * slots),
        ),
        name="transform",
    )(*map(in_hbm, (field, table, coefficient)))
    return outs[:slots], outs[slots], outs[slots + 1 : -1], outs[-1]


def split_kernel(x_ref, high_ref, low_ref):
    high_ref[0], low_ref[0] = split_bf16(jnp.transpose(x_ref[0]))


def split_transfer(transfer):
    parts, sensors, cells = transfer.shape
    block = pl.BlockSpec((1, cells, sensors), lambda a: (a, 0, 0))
    return pl.pallas_call(
        split_kernel,
        out_shape=[jax.ShapeDtypeStruct((parts, cells, sensors), jnp.bfloat16)] * 2,
        grid=(parts,),
        in_specs=[pl.BlockSpec((1, sensors, cells), lambda a: (a, 0, 0))],
        out_specs=[block, block],
        compiler_params=params(),
        cost_estimate=cost(2 * transfer.size, 8 * transfer.size),
        name="split_transfer",
    )(in_hbm(transfer))


def relaxed_rows(rows, coefficients):
    width = rows[0].shape[-1]
    lane = lax.broadcasted_iota(jnp.int32, rows[0].shape, 1)
    first, last = lane == 0, lane == width - 1
    out = []
    for i in range(1, len(rows) - 1):
        centre = rows[i]
        left = jnp.where(first, 0.0, pltpu.roll(centre, 1, 1))
        right = jnp.where(last, 0.0, pltpu.roll(centre, width - 1, 1))
        beside = (rows[i + 1] + rows[i - 1]) + (left + right)
        out.append(centre + coefficients[i - 1] * (beside - 4.0 * centre))
    return out


def edges_kernel(count, crossing, *refs):
    chunks, outs = refs[:count], refs[count:]
    _, rows, vectors, _ = chunks[0].shape
    even = even_strip().astype(jnp.int32)

    def put(ref, slot, chunk, last):
        for b in range(2):
            for r in range(PASSES):
                at = edge_base(slot, b, r, vectors)
                ref[at : at + vectors] = chunk[b, last * (rows - PASSES) + r]

    if crossing:
        for slot, index in enumerate(crossing):
            put(outs[-1], slot, chunks[index], 1 - even)
    if len(outs) > 1 or not crossing:
        for index, chunk in enumerate(chunks):
            put(outs[0], index, chunk, even)


def edges(chunks, crossing, pair=True):
    _, _, vectors, width = chunks[0].shape
    counts = [len(chunks)] * pair + [len(crossing)] * bool(crossing)
    shapes = [(edge_base(n, 0, 0, vectors), width) for n in counts]
    return pl.pallas_call(
        functools.partial(edges_kernel, len(chunks), crossing),
        out_shape=[jax.ShapeDtypeStruct(shape, jnp.float32) for shape in shapes],
        compiler_params=params(),
        cost_estimate=cost(0, 16 * shapes[0][0] * width),
        name="edges",
    )(*chunks)


def smooth_kernel(pair_slot, cross_slot, chunk, pair, cross, own_c, pair_c, cross_c, out):
    _, rows, vectors, width = chunk.shape
    rim = PASSES - 1
    even = even_strip()
    part = math.gcd(vectors, 2 * GROUP)
    strip = lax.axis_index("seabed")
    inside = (strip > 0) & (strip < lax.axis_size("seabed") - 1)

    def rims(one, other):
        other = pick(inside, other, jnp.zeros_like(other))
        return pick(even, one, other), pick(even, other, one)

    def rim_of(ref):
        base = ref.shape[0] - GROUP
        return ref[base : base + rim]

    high_c, low_c = rims(rim_of(pair_c), rim_of(cross_c))
    coefficients = [low_c[i : i + 1] for i in range(rim)]
    coefficients += [own_c[i : i + 1] for i in range(rows)]
    coefficients += [high_c[i : i + 1] for i in range(rim)]
    coefficients = [jnp.broadcast_to(c, (part, width)) for c in coefficients]
    for b in range(2):
        for start in range(0, vectors, part):
            span = slice(start, start + part)
            low, high = [], []
            for r in range(PASSES):
                at = edge_base(pair_slot, b, r, vectors) + start
                to = edge_base(cross_slot, b, r, vectors) + start
                above, below = rims(pair[at : at + part], cross[to : to + part])
                high.append(above)
                low.append(below)
            values = low + [chunk[b, r, span] for r in range(rows)] + high
            for step in range(PASSES):
                values = relaxed_rows(values, coefficients[step : len(coefficients) - step])
            for r in range(rows):
                out[b, r, span] = values[r]


def smooth(chunk, pair, pair_slot, cross, cross_slot, coefficients):
    return pl.pallas_call(
        functools.partial(smooth_kernel, pair_slot, cross_slot),
        out_shape=jax.ShapeDtypeStruct(chunk.shape, jnp.float32),
        compiler_params=params(),
        cost_estimate=cost(30 * chunk.size, 10 * chunk.size),
        name="smooth",
    )(chunk, pair, cross, *coefficients)


def place_of(index, o, owners_in):
    owner = (lax.axis_index("freq") ^ index) * owners_in + o
    apart = owner ^ lax.axis_index("seabed")
    return apart & 1, apart >> 1


def combine_kernel(indices, owners_in, paired, absent, *refs):
    count = len(indices)
    chunks, (t_high, t_low), (out, held) = refs[:count], refs[count : count + 2], refs[-2:]
    _, rows, vectors, width = chunks[0].shape
    owned = vectors // owners_in
    for at, ref in enumerate(chunks):
        for b in range(2):
            for r in range(rows):
                held[b, at, :, r * width : (r + 1) * width] = ref[b, r]
    half = count * vectors
    lhs_high, lhs_low = split_bf16(held[...].reshape(2 * half, rows * width))

    def times(a):
        def dot(x, w):
            return lax.dot_general(
                x, w, (((1,), (0,)), ((), ())), preferred_element_type=jnp.float32
            )

        return (dot(lhs_low, t_high[a]) + dot(lhs_high, t_low[a])) + dot(lhs_high, t_high[a])

    by_real, by_imag = times(0), times(1)
    real = by_real[:half] - by_imag[half:]
    imag = by_imag[:half] + by_real[half:]

    def place(index, o):
        if not paired:
            return index * owners_in + o
        core, chip = place_of(index, o, owners_in)
        return core * (out.shape[0] // 2) + (chip if absent else indices.index(index))

    for at, index in enumerate(indices):
        for o in range(owners_in):
            span = slice((at * owners_in + o) * owned, (at * owners_in + o + 1) * owned)
            out[place(index, o), 0] = real[span]
            out[place(index, o), 1] = imag[span]
    for index in absent:
        for o in range(owners_in):
            out[place(index, o)] = jnp.zeros(out.shape[1:], out.dtype)


def combine(chunks, split, owners_in, places, paired, absent=()):
    t_high, t_low = split
    cells, sensors = t_high.shape[1:]
    indices = sorted(chunks)
    _, _, vectors, _ = chunks[indices[0]].shape
    owned = vectors // owners_in
    whole = len(indices) * vectors
    return pl.pallas_call(
        functools.partial(combine_kernel, indices, owners_in, paired, absent),
        out_shape=jax.ShapeDtypeStruct((places, 2, owned, sensors), jnp.float32),
        scratch_shapes=[pltpu.VMEM((2, len(indices), vectors, cells), jnp.float32)],
        compiler_params=params(),
        cost_estimate=cost(
            24 * whole * sensors * cells,
            8 * sensors * cells + 8 * whole * cells + 16 * whole * sensors,
        ),
        name="combine",
    )(*[chunks[i] for i in indices], t_high, t_low)


def merge_kernel(late, owners_in, most, most_moved, tail, tail_moved, *outs):
    chips = [place_of(index, 0, owners_in)[1] for index in late]
    final = [tail[i] + tail_moved[i] for i in range(len(late))]
    for d, out in enumerate(outs):
        value = most[d] + most_moved[d]
        for chip, add in zip(chips, final):
            value = value + pick(chip == d, add, jnp.zeros_like(add))
        out[...] = value


def merge(late, owners_in, most, most_moved, tail, tail_moved):
    shape = jax.ShapeDtypeStruct(most.shape[1:], jnp.float32)
    return pl.pallas_call(
        functools.partial(merge_kernel, late, owners_in),
        out_shape=[shape] * most_moved.shape[0],
        compiler_params=params(),
        cost_estimate=cost(4 * most.size, 12 * most.size),
        name="merge",
    )(most, most_moved, tail, tail_moved)


def xor_pairs(count, apart):
    return [(i, i ^ apart) for i in range(count)]


def to_pair(edge, strips):
    return lax.ppermute(edge, "seabed", xor_pairs(strips, 1))


def to_cross(edge, strips):
    inner = [(i, (i + 1) % strips) for i in range(1, strips, 2)]
    return lax.ppermute(edge, "seabed", inner + [(b, a) for a, b in inner])


def paired_shards(field, coefficient, split_of, table, freq_count, strips):
    chunks, pair, crosses, coefficient = transform(field, table, coefficient, freq_count, ((2,), (1,), (0,)))

    def swap(m, chunk):
        return lax.ppermute(chunk, "freq", xor_pairs(freq_count, m))

    def relax(chunk, pair, pair_slot, cross, cross_slot):
        return smooth(chunk, pair, pair_slot, cross, cross_slot, coefficients)

    third = swap(3, chunks[3])
    cross2 = to_cross(crosses[0], strips)
    pair = to_pair(pair, strips)
    cross1 = to_cross(crosses[1], strips)
    cross0 = to_cross(crosses[2], strips)
    coefficients = (coefficient, pair, cross2)
    split = split_of()
    second = swap(2, relax(chunks[2], pair, 0, cross2, 0))
    pair3, cross3 = edges([third], (0,))
    cross3 = to_cross(cross3, strips)
    pair3 = to_pair(pair3, strips)
    first = swap(1, relax(chunks[1], pair, 1, cross1, 0))
    own = relax(chunks[0], pair, 2, cross0, 0)
    third = relax(third, pair3, 0, cross3, 0)
    most = combine({0: own, 3: third}, split, 2, strips, True, (1, 2))

    def to_core(partial):
        send = partial[partial.shape[0] // 2 :]
        return lax.ppermute(send, "seabed", xor_pairs(strips, 1))

    most_moved = to_core(most)
    tail = combine({1: first, 2: second}, split, 2, strips // 2, True)
    chips = merge((1, 2), 2, most, most_moved, tail, to_core(tail))
    total = chips[0]
    for d in range(1, strips // 2):
        total = total + lax.ppermute(chips[d], "seabed", xor_pairs(strips, 2 * d))
    return total


def plain_shards(field, coefficient, split_of, table, freq_count, strips):
    spectrum, pair_c, (cross_c,), coefficient = transform(field, table, coefficient, freq_count, ((),))
    spectrum = jnp.stack(spectrum)
    spectrum = lax.all_to_all(spectrum, "freq", split_axis=0, concat_axis=0, tiled=True)
    chunks = list(spectrum)
    pair_c = to_pair(pair_c, strips)
    cross_c = to_cross(cross_c, strips)
    coefficients = (coefficient, pair_c, cross_c)
    pair, cross = edges(chunks, tuple(range(len(chunks))))
    pair, cross = to_pair(pair, strips), to_cross(cross, strips)
    chunks = [smooth(c, pair, i, cross, i, coefficients) for i, c in enumerate(chunks)]
    owners_in = strips // freq_count
    partial = combine(dict(enumerate(chunks)), split_of(), owners_in, strips, False)
    got = lax.all_to_all(partial, "seabed", split_axis=0, concat_axis=0, tiled=True)
    return got.sum(0)


def shards(uplift, coefficient, transfer):
    vectors, steps, _, _ = uplift.shape
    freq_count, strips = FD * lax.axis_size("freq"), lax.axis_size("seabed")
    owned = vectors * freq_count // strips
    paired = (
        strips == 8
        and freq_count == 4
        and vectors == 2 * owned
        and owned == 2 * GROUP
    )
    slots = np.arange(freq_count)
    order = slots[:, None] ^ slots[None, :] if paired else slots[None, :]
    table = transform_operand(steps, freq_count, order)
    field = jnp.transpose(uplift, (0, 2, 1, 3))
    run = paired_shards if paired else plain_shards
    total = run(field, coefficient, lambda: split_transfer(transfer[0]), table, freq_count, strips)
    return jnp.transpose(total, (1, 0, 2))[:, None]


def solution(mesh):
    placed = (P("freq", None, "seabed", None), P("seabed", None), P("freq", None, None, "seabed"))
    return jax.shard_map(
        shards,
        mesh=mesh,
        in_specs=placed,
        out_specs=P("seabed", "freq", None, None),
        check_vma=False,
    )
```

```python
import functools
import math

import jax
import jax.numpy as jnp
import numpy as np
from jax import lax
from jax.experimental import pallas as pl
from jax.experimental.pallas import tpu as pltpu
from jax.sharding import PartitionSpec as P


FD = 1
PASSES = 3
GROUP = 8
GRANT = 16 * 1024 * 1024


def params():
    return pltpu.CompilerParams(vmem_limit_bytes=GRANT)


def cost(flops, moved):
    return pl.CostEstimate(flops=flops, bytes_accessed=moved, transcendentals=0)


def in_hbm(array):
    return pltpu.with_memory_space_constraint(array, pltpu.HBM)


def even_strip():
    return lax.rem(lax.axis_index("seabed"), 2) == 0


def pick(flag, one, other):
    return jnp.where(jnp.full(one.shape, flag), one, other)


def dft_table(steps_count, freq_count):
    times = np.arange(steps_count)
    freqs = np.arange(freq_count)
    phase = (freqs[:, None] * times[None, :] % steps_count) * (2.0 * math.pi / steps_count)
    scale = 1.0 / math.sqrt(steps_count)
    return (np.stack([np.cos(phase), -np.sin(phase)], 1) * scale).astype(np.float32)


def split_bf16(values):
    high = values.astype(jnp.bfloat16)
    low = (values - high.astype(values.dtype)).astype(jnp.bfloat16)
    return high, low


def transform_operand(steps_count, freq_count, order):
    table = dft_table(steps_count, freq_count)[order]
    parts = np.stack([x.astype(np.float32) for x in split_bf16(table)], 1)
    sources = parts.shape[0]
    wide = np.broadcast_to(parts[..., None, :], (*parts.shape[:-1], GROUP, steps_count))
    return jnp.asarray(wide.reshape(sources, -1, GROUP * steps_count), jnp.float32)


def edge_base(slot, b, r, vectors):
    return ((slot * 2 + b) * PASSES + r) * vectors


def transform_kernel(slots, edged, field_hbm, table_hbm, own_hbm, *refs):
    outs, pair, crosses = refs[:slots], refs[slots], refs[slots + 1 : -6]
    own_c, field, table, field_sem, table_sem, own_sem = refs[-6:]
    vectors, rows, steps, width = field.shape
    blocks = vectors // GROUP
    even = even_strip()
    source = lax.axis_index("freq") if table_hbm.shape[0] > 1 else 0
    get_field = pltpu.make_async_copy(field_hbm, field, field_sem)
    get_field.start()
    get_table = pltpu.make_async_copy(table_hbm.at[source], table, table_sem)
    get_table.start()
    get_own = pltpu.make_async_copy(own_hbm, own_c, own_sem)
    get_own.start()
    get_own.wait()
    rim = PASSES - 1
    last_c, first_c = own_c[rows - rim :], own_c[:rim]
    for ref, one, other in ((pair, last_c, first_c), (crosses[0], first_c, last_c)):
        base = ref.shape[0] - GROUP
        ref[base : base + rim] = pick(even, one, other)
        ref[base + rim :] = jnp.zeros((GROUP - rim, width), jnp.float32)
    get_table.wait()
    short = table[...]
    shape = (short.shape[0], GROUP, short.shape[1])
    mine = lax.broadcasted_iota(jnp.int32, shape, 1)
    column = lax.broadcasted_iota(jnp.int32, shape, 2)
    full = jnp.where(
        (column >= mine * steps) & (column < (mine + 1) * steps), short[:, None], 0.0
    )
    full = full.reshape(-1, short.shape[1]).astype(jnp.bfloat16)
    get_field.wait()
    for i in range(blocks):
        span = slice(i * GROUP, (i + 1) * GROUP)
        data = jnp.concatenate(
            [field[span, r].reshape(GROUP * steps, width) for r in range(rows)], axis=1
        )
        both = jnp.dot(full, data, preferred_element_type=jnp.float32)
        half = both.shape[0] // 2
        values = both[:half] + both[half:]
        for slot in range(slots):
            for b in range(2):
                at = (slot * 2 + b) * GROUP
                for r in range(rows):
                    piece = values[at : at + GROUP, r * width : (r + 1) * width]
                    outs[slot][b, r, span] = piece
                if slot not in sum(edged, ()):
                    continue
                group = [slot in g for g in edged].index(True)
                for r in range(PASSES):
                    row = (rows - PASSES + r) * width
                    last = values[at : at + GROUP, row : row + width]
                    first = values[at : at + GROUP, r * width : (r + 1) * width]
                    to = edge_base(sum(edged, ()).index(slot), b, r, vectors) + i * GROUP
                    pair[to : to + GROUP] = pick(even, last, first)
                    to = edge_base(edged[group].index(slot), b, r, vectors) + i * GROUP
                    crosses[group][to : to + GROUP] = pick(even, first, last)


def transform(field, table, coefficient, slots, edged):
    vectors, rows, steps, width = field.shape
    chunk = jax.ShapeDtypeStruct((2, rows, vectors, width), jnp.float32)
    size = edge_base(1, 0, 0, vectors)
    pair = (sum(map(len, edged)) * size + GROUP, width)
    crosses = [(len(g) * size + GROUP * (i == 0), width) for i, g in enumerate(edged)]
    edges = [jax.ShapeDtypeStruct(shape, jnp.float32) for shape in (pair, *crosses, coefficient.shape)]
    hbm = pl.BlockSpec(memory_space=pltpu.HBM)
    vmem = pl.BlockSpec(memory_space=pltpu.VMEM)
    outs = pl.pallas_call(
        functools.partial(transform_kernel, slots, edged),
        out_shape=[chunk] * slots + edges,
        in_specs=[hbm, hbm, hbm],
        out_specs=[vmem] * (slots + len(edges)),
        scratch_shapes=[
            pltpu.VMEM(field.shape, field.dtype),
            pltpu.VMEM(table.shape[1:], table.dtype),
            pltpu.SemaphoreType.DMA(()),
            pltpu.SemaphoreType.DMA(()),
            pltpu.SemaphoreType.DMA(()),
        ],
        compiler_params=params(),
        cost_estimate=cost(
            2 * table.shape[1] * table.shape[2] * rows * width * vectors,
            vectors * rows * width * (2 * steps + 8 * slots),
        ),
        name="transform",
    )(*map(in_hbm, (field, table, coefficient)))
    return outs[:slots], outs[slots], outs[slots + 1 : -1], outs[-1]


def split_kernel(x_ref, high_ref, low_ref):
    high_ref[0], low_ref[0] = split_bf16(jnp.transpose(x_ref[0]))


def split_transfer(transfer):
    parts, sensors, cells = transfer.shape
    block = pl.BlockSpec((1, cells, sensors), lambda a: (a, 0, 0))
    return pl.pallas_call(
        split_kernel,
        out_shape=[jax.ShapeDtypeStruct((parts, cells, sensors), jnp.bfloat16)] * 2,
        grid=(parts,),
        in_specs=[pl.BlockSpec((1, sensors, cells), lambda a: (a, 0, 0))],
        out_specs=[block, block],
        compiler_params=params(),
        cost_estimate=cost(2 * transfer.size, 8 * transfer.size),
        name="split_transfer",
    )(in_hbm(transfer))


def relaxed_rows(rows, coefficients):
    width = rows[0].shape[-1]
    lane = lax.broadcasted_iota(jnp.int32, rows[0].shape, 1)
    first, last = lane == 0, lane == width - 1
    out = []
    for i in range(1, len(rows) - 1):
        centre = rows[i]
        left = jnp.where(first, 0.0, pltpu.roll(centre, 1, 1))
        right = jnp.where(last, 0.0, pltpu.roll(centre, width - 1, 1))
        beside = (rows[i + 1] + rows[i - 1]) + (left + right)
        out.append(centre + coefficients[i - 1] * (beside - 4.0 * centre))
    return out


def edges_kernel(count, crossing, *refs):
    chunks, outs = refs[:count], refs[count:]
    _, rows, vectors, _ = chunks[0].shape
    even = even_strip().astype(jnp.int32)

    def put(ref, slot, chunk, last):
        for b in range(2):
            for r in range(PASSES):
                at = edge_base(slot, b, r, vectors)
                ref[at : at + vectors] = chunk[b, last * (rows - PASSES) + r]

    if crossing:
        for slot, index in enumerate(crossing):
            put(outs[-1], slot, chunks[index], 1 - even)
    if len(outs) > 1 or not crossing:
        for index, chunk in enumerate(chunks):
            put(outs[0], index, chunk, even)


def edges(chunks, crossing, pair=True):
    _, _, vectors, width = chunks[0].shape
    counts = [len(chunks)] * pair + [len(crossing)] * bool(crossing)
    shapes = [(edge_base(n, 0, 0, vectors), width) for n in counts]
    return pl.pallas_call(
        functools.partial(edges_kernel, len(chunks), crossing),
        out_shape=[jax.ShapeDtypeStruct(shape, jnp.float32) for shape in shapes],
        compiler_params=params(),
        cost_estimate=cost(0, 16 * shapes[0][0] * width),
        name="edges",
    )(*chunks)


def smooth_kernel(pair_slot, cross_slot, chunk, pair, cross, own_c, pair_c, cross_c, out):
    _, rows, vectors, width = chunk.shape
    rim = PASSES - 1
    even = even_strip()
    part = math.gcd(vectors, 2 * GROUP)
    strip = lax.axis_index("seabed")
    inside = (strip > 0) & (strip < lax.axis_size("seabed") - 1)

    def rims(one, other):
        other = pick(inside, other, jnp.zeros_like(other))
        return pick(even, one, other), pick(even, other, one)

    def rim_of(ref):
        base = ref.shape[0] - GROUP
        return ref[base : base + rim]

    high_c, low_c = rims(rim_of(pair_c), rim_of(cross_c))
    coefficients = [low_c[i : i + 1] for i in range(rim)]
    coefficients += [own_c[i : i + 1] for i in range(rows)]
    coefficients += [high_c[i : i + 1] for i in range(rim)]
    coefficients = [jnp.broadcast_to(c, (part, width)) for c in coefficients]
    for b in range(2):
        for start in range(0, vectors, part):
            span = slice(start, start + part)
            low, high = [], []
            for r in range(PASSES):
                at = edge_base(pair_slot, b, r, vectors) + start
                to = edge_base(cross_slot, b, r, vectors) + start
                above, below = rims(pair[at : at + part], cross[to : to + part])
                high.append(above)
                low.append(below)
            values = low + [chunk[b, r, span] for r in range(rows)] + high
            for step in range(PASSES):
                values = relaxed_rows(values, coefficients[step : len(coefficients) - step])
            for r in range(rows):
                out[b, r, span] = values[r]


def smooth(chunk, pair, pair_slot, cross, cross_slot, coefficients):
    return pl.pallas_call(
        functools.partial(smooth_kernel, pair_slot, cross_slot),
        out_shape=jax.ShapeDtypeStruct(chunk.shape, jnp.float32),
        compiler_params=params(),
        cost_estimate=cost(30 * chunk.size, 10 * chunk.size),
        name="smooth",
    )(chunk, pair, cross, *coefficients)


def place_of(index, o, owners_in):
    owner = (lax.axis_index("freq") ^ index) * owners_in + o
    apart = owner ^ lax.axis_index("seabed")
    return apart & 1, apart >> 1


def combine_kernel(indices, owners_in, paired, absent, *refs):
    count = len(indices)
    chunks, (t_high, t_low), (out, held) = refs[:count], refs[count : count + 2], refs[-2:]
    _, rows, vectors, width = chunks[0].shape
    owned = vectors // owners_in
    for at, ref in enumerate(chunks):
        for b in range(2):
            for r in range(rows):
                held[b, at, :, r * width : (r + 1) * width] = ref[b, r]
    half = count * vectors
    lhs_high, lhs_low = split_bf16(held[...].reshape(2 * half, rows * width))
    lhs_both = jnp.concatenate([lhs_high, lhs_low], axis=0)

    def times(a):
        def dot(x, w):
            return lax.dot_general(
                x, w, (((1,), (0,)), ((), ())), preferred_element_type=jnp.float32
            )

        by_high = dot(lhs_both, t_high[a])
        return (by_high[2 * half :] + dot(lhs_high, t_low[a])) + by_high[: 2 * half]

    by_real, by_imag = times(0), times(1)
    real = by_real[:half] - by_imag[half:]
    imag = by_imag[:half] + by_real[half:]

    def place(index, o):
        if not paired:
            return index * owners_in + o
        core, chip = place_of(index, o, owners_in)
        return core * (out.shape[0] // 2) + (chip if absent else indices.index(index))

    for at, index in enumerate(indices):
        for o in range(owners_in):
            span = slice((at * owners_in + o) * owned, (at * owners_in + o + 1) * owned)
            out[place(index, o), 0] = real[span]
            out[place(index, o), 1] = imag[span]
    for index in absent:
        for o in range(owners_in):
            out[place(index, o)] = jnp.zeros(out.shape[1:], out.dtype)


def combine(chunks, split, owners_in, places, paired, absent=()):
    t_high, t_low = split
    cells, sensors = t_high.shape[1:]
    indices = sorted(chunks)
    _, _, vectors, _ = chunks[indices[0]].shape
    owned = vectors // owners_in
    whole = len(indices) * vectors
    return pl.pallas_call(
        functools.partial(combine_kernel, indices, owners_in, paired, absent),
        out_shape=jax.ShapeDtypeStruct((places, 2, owned, sensors), jnp.float32),
        scratch_shapes=[pltpu.VMEM((2, len(indices), vectors, cells), jnp.float32)],
        compiler_params=params(),
        cost_estimate=cost(
            24 * whole * sensors * cells,
            8 * sensors * cells + 8 * whole * cells + 16 * whole * sensors,
        ),
        name="combine",
    )(*[chunks[i] for i in indices], t_high, t_low)


def merge_kernel(late, owners_in, most, most_moved, tail, tail_moved, *outs):
    chips = [place_of(index, 0, owners_in)[1] for index in late]
    final = [tail[i] + tail_moved[i] for i in range(len(late))]
    for d, out in enumerate(outs):
        value = most[d] + most_moved[d]
        for chip, add in zip(chips, final):
            value = value + pick(chip == d, add, jnp.zeros_like(add))
        out[...] = value


def merge(late, owners_in, most, most_moved, tail, tail_moved):
    shape = jax.ShapeDtypeStruct(most.shape[1:], jnp.float32)
    return pl.pallas_call(
        functools.partial(merge_kernel, late, owners_in),
        out_shape=[shape] * most_moved.shape[0],
        compiler_params=params(),
        cost_estimate=cost(4 * most.size, 12 * most.size),
        name="merge",
    )(most, most_moved, tail, tail_moved)


def xor_pairs(count, apart):
    return [(i, i ^ apart) for i in range(count)]


def to_pair(edge, strips):
    return lax.ppermute(edge, "seabed", xor_pairs(strips, 1))


def to_cross(edge, strips):
    inner = [(i, (i + 1) % strips) for i in range(1, strips, 2)]
    return lax.ppermute(edge, "seabed", inner + [(b, a) for a, b in inner])


def paired_shards(field, coefficient, split_of, table, freq_count, strips):
    chunks, pair, crosses, coefficient = transform(
        field, table, coefficient, freq_count, ((2,), (0,))
    )

    def swap(m, chunk):
        return lax.ppermute(chunk, "freq", xor_pairs(freq_count, m))

    def relax(chunk, pair, pair_slot, cross):
        return smooth(chunk, pair, pair_slot, cross, 0, coefficients)

    first = swap(1, chunks[1])
    third = swap(3, chunks[3])
    cross2 = to_cross(crosses[0], strips)
    pair = to_pair(pair, strips)
    cross0 = to_cross(crosses[1], strips)
    coefficients = (coefficient, pair, cross2)
    split = split_of()
    second = swap(2, relax(chunks[2], pair, 0, cross2))
    own = relax(chunks[0], pair, 1, cross0)
    (cross1,) = edges([first], (0,), False)
    cross1 = to_cross(cross1, strips)
    pair, cross3 = edges([first, third], (1,))
    cross3 = to_cross(cross3, strips)
    pair = to_pair(pair, strips)
    first = relax(first, pair, 0, cross1)
    third = relax(third, pair, 1, cross3)
    most = combine({0: own, 1: first}, split, 2, strips, True, (2, 3))

    def to_core(partial):
        send = partial[partial.shape[0] // 2 :]
        return lax.ppermute(send, "seabed", xor_pairs(strips, 1))

    most_moved = to_core(most)
    tail = combine({2: second, 3: third}, split, 2, strips // 2, True)
    chips = merge((2, 3), 2, most, most_moved, tail, to_core(tail))
    total = chips[0]
    for d in range(1, strips // 2):
        total = total + lax.ppermute(chips[d], "seabed", xor_pairs(strips, 2 * d))
    return total


def plain_shards(field, coefficient, split_of, table, freq_count, strips):
    spectrum, pair_c, (cross_c,), coefficient = transform(
        field, table, coefficient, freq_count, ((),)
    )
    spectrum = jnp.stack(spectrum)
    spectrum = lax.all_to_all(spectrum, "freq", split_axis=0, concat_axis=0, tiled=True)
    chunks = list(spectrum)
    pair_c = to_pair(pair_c, strips)
    cross_c = to_cross(cross_c, strips)
    coefficients = (coefficient, pair_c, cross_c)
    pair, cross = edges(chunks, tuple(range(len(chunks))))
    pair, cross = to_pair(pair, strips), to_cross(cross, strips)
    chunks = [smooth(c, pair, i, cross, i, coefficients) for i, c in enumerate(chunks)]
    owners_in = strips // freq_count
    partial = combine(dict(enumerate(chunks)), split_of(), owners_in, strips, False)
    got = lax.all_to_all(partial, "seabed", split_axis=0, concat_axis=0, tiled=True)
    return got.sum(0)


def shards(uplift, coefficient, transfer):
    vectors, steps, _, _ = uplift.shape
    freq_count, strips = FD * lax.axis_size("freq"), lax.axis_size("seabed")
    owned = vectors * freq_count // strips
    paired = (
        strips == 8
        and freq_count == 4
        and vectors == 2 * owned
        and owned == 2 * GROUP
    )
    slots = np.arange(freq_count)
    order = slots[:, None] ^ slots[None, :] if paired else slots[None, :]
    table = transform_operand(steps, freq_count, order)
    field = jnp.transpose(uplift, (0, 2, 1, 3))
    run = paired_shards if paired else plain_shards
    total = run(
        field,
        coefficient,
        lambda: split_transfer(transfer[0]),
        table,
        freq_count,
        strips,
    )
    return jnp.transpose(total, (1, 0, 2))[:, None]


def solution(mesh):
    placed = (P("freq", None, "seabed", None), P("seabed", None), P("freq", None, None, "seabed"))
    return jax.shard_map(
        shards,
        mesh=mesh,
        in_specs=placed,
        out_specs=P("seabed", "freq", None, None),
        check_vma=False,
    )
```

```python
import functools
import math

import jax
import jax.numpy as jnp
import numpy as np
from jax import lax
from jax.experimental import pallas as pl
from jax.experimental.pallas import tpu as pltpu
from jax.sharding import PartitionSpec as P


FD = 1
PASSES = 3
GROUP = 8
GRANT = 16 * 1024 * 1024


def params():
    return pltpu.CompilerParams(vmem_limit_bytes=GRANT)


def cost(flops, moved):
    return pl.CostEstimate(flops=flops, bytes_accessed=moved, transcendentals=0)


def in_hbm(array):
    return pltpu.with_memory_space_constraint(array, pltpu.HBM)


def even_strip():
    return lax.rem(lax.axis_index("seabed"), 2) == 0


def pick(flag, one, other):
    return jnp.where(jnp.full(one.shape, flag), one, other)


def dft_table(steps_count, freq_count):
    times = np.arange(steps_count)
    freqs = np.arange(freq_count)
    phase = (freqs[:, None] * times[None, :] % steps_count) * (2.0 * math.pi / steps_count)
    scale = 1.0 / math.sqrt(steps_count)
    return (np.stack([np.cos(phase), -np.sin(phase)], 1) * scale).astype(np.float32)


def split_bf16(values):
    high = values.astype(jnp.bfloat16)
    low = (values - high.astype(values.dtype)).astype(jnp.bfloat16)
    return high, low


def transform_operand(steps_count, freq_count, order):
    table = dft_table(steps_count, freq_count)[order]
    parts = np.stack([x.astype(np.float32) for x in split_bf16(table)], 1)
    sources = parts.shape[0]
    wide = np.broadcast_to(parts[..., None, :], (*parts.shape[:-1], GROUP, steps_count))
    return jnp.asarray(wide.reshape(sources, -1, GROUP * steps_count), jnp.float32)


def edge_base(slot, b, r, vectors):
    return ((slot * 2 + b) * PASSES + r) * vectors


def transform_kernel(slots, edged, field_hbm, table_hbm, own_hbm, *refs):
    outs, pair, crosses = refs[:slots], refs[slots], refs[slots + 1 : -6]
    own_c, field, table, field_sem, table_sem, own_sem = refs[-6:]
    vectors, rows, steps, width = field.shape
    blocks = vectors // GROUP
    even = even_strip()
    source = lax.axis_index("freq") if table_hbm.shape[0] > 1 else 0
    get_field = pltpu.make_async_copy(field_hbm, field, field_sem)
    get_field.start()
    get_table = pltpu.make_async_copy(table_hbm.at[source], table, table_sem)
    get_table.start()
    get_own = pltpu.make_async_copy(own_hbm, own_c, own_sem)
    get_own.start()
    get_own.wait()
    rim = PASSES - 1
    last_c, first_c = own_c[rows - rim :], own_c[:rim]
    for ref, one, other in ((pair, last_c, first_c), (crosses[0], first_c, last_c)):
        base = ref.shape[0] - GROUP
        ref[base : base + rim] = pick(even, one, other)
        ref[base + rim :] = jnp.zeros((GROUP - rim, width), jnp.float32)
    get_table.wait()
    short = table[...]
    shape = (short.shape[0], GROUP, short.shape[1])
    mine = lax.broadcasted_iota(jnp.int32, shape, 1)
    column = lax.broadcasted_iota(jnp.int32, shape, 2)
    full = jnp.where(
        (column >= mine * steps) & (column < (mine + 1) * steps), short[:, None], 0.0
    )
    full = full.reshape(-1, short.shape[1]).astype(jnp.bfloat16)
    get_field.wait()
    for i in range(blocks):
        span = slice(i * GROUP, (i + 1) * GROUP)
        data = jnp.concatenate(
            [field[span, r].reshape(GROUP * steps, width) for r in range(rows)], axis=1
        )
        both = jnp.dot(full, data, preferred_element_type=jnp.float32)
        half = both.shape[0] // 2
        values = both[:half] + both[half:]
        for slot in range(slots):
            for b in range(2):
                at = (slot * 2 + b) * GROUP
                for r in range(rows):
                    piece = values[at : at + GROUP, r * width : (r + 1) * width]
                    outs[slot][b, r, span] = piece
                if slot not in sum(edged, ()):
                    continue
                group = [slot in g for g in edged].index(True)
                for r in range(PASSES):
                    row = (rows - PASSES + r) * width
                    last = values[at : at + GROUP, row : row + width]
                    first = values[at : at + GROUP, r * width : (r + 1) * width]
                    to = edge_base(sum(edged, ()).index(slot), b, r, vectors) + i * GROUP
                    pair[to : to + GROUP] = pick(even, last, first)
                    to = edge_base(edged[group].index(slot), b, r, vectors) + i * GROUP
                    crosses[group][to : to + GROUP] = pick(even, first, last)


def transform(field, table, coefficient, slots, edged):
    vectors, rows, steps, width = field.shape
    chunk = jax.ShapeDtypeStruct((2, rows, vectors, width), jnp.float32)
    size = edge_base(1, 0, 0, vectors)
    pair = (sum(map(len, edged)) * size + GROUP, width)
    crosses = [(len(g) * size + GROUP * (i == 0), width) for i, g in enumerate(edged)]
    edges = [jax.ShapeDtypeStruct(shape, jnp.float32) for shape in (pair, *crosses, coefficient.shape)]
    hbm = pl.BlockSpec(memory_space=pltpu.HBM)
    vmem = pl.BlockSpec(memory_space=pltpu.VMEM)
    outs = pl.pallas_call(
        functools.partial(transform_kernel, slots, edged),
        out_shape=[chunk] * slots + edges,
        in_specs=[hbm, hbm, hbm],
        out_specs=[vmem] * (slots + len(edges)),
        scratch_shapes=[
            pltpu.VMEM(field.shape, field.dtype),
            pltpu.VMEM(table.shape[1:], table.dtype),
            pltpu.SemaphoreType.DMA(()),
            pltpu.SemaphoreType.DMA(()),
            pltpu.SemaphoreType.DMA(()),
        ],
        compiler_params=params(),
        cost_estimate=cost(
            2 * table.shape[1] * table.shape[2] * rows * width * vectors,
            vectors * rows * width * (2 * steps + 8 * slots),
        ),
        name="transform",
    )(*map(in_hbm, (field, table, coefficient)))
    return outs[:slots], outs[slots], outs[slots + 1 : -1], outs[-1]


def split_kernel(x_ref, high_ref, low_ref):
    high_ref[...], low_ref[...] = split_bf16(jnp.transpose(x_ref[0]))


def split_transfer(transfer, part):
    _, sensors, cells = transfer.shape
    block = pl.BlockSpec((cells, sensors), lambda i: (0, 0))
    return pl.pallas_call(
        split_kernel,
        out_shape=[jax.ShapeDtypeStruct((cells, sensors), jnp.bfloat16)] * 2,
        grid=(1,),
        in_specs=[pl.BlockSpec((1, sensors, cells), lambda i: (part, 0, 0))],
        out_specs=[block, block],
        compiler_params=params(),
        cost_estimate=cost(2 * sensors * cells, 8 * sensors * cells),
        name="split_transfer",
    )(in_hbm(transfer))


def relaxed_rows(rows, coefficients):
    width = rows[0].shape[-1]
    lane = lax.broadcasted_iota(jnp.int32, rows[0].shape, 1)
    first, last = lane == 0, lane == width - 1
    out = []
    for i in range(1, len(rows) - 1):
        centre = rows[i]
        left = jnp.where(first, 0.0, pltpu.roll(centre, 1, 1))
        right = jnp.where(last, 0.0, pltpu.roll(centre, width - 1, 1))
        beside = (rows[i + 1] + rows[i - 1]) + (left + right)
        out.append(centre + coefficients[i - 1] * (beside - 4.0 * centre))
    return out


def edges_kernel(count, crossing, *refs):
    chunks, outs = refs[:count], refs[count:]
    _, rows, vectors, _ = chunks[0].shape
    even = even_strip().astype(jnp.int32)

    def put(ref, slot, chunk, last):
        for b in range(2):
            for r in range(PASSES):
                at = edge_base(slot, b, r, vectors)
                ref[at : at + vectors] = chunk[b, last * (rows - PASSES) + r]

    if crossing:
        for slot, index in enumerate(crossing):
            put(outs[-1], slot, chunks[index], 1 - even)
    if len(outs) > 1 or not crossing:
        for index, chunk in enumerate(chunks):
            put(outs[0], index, chunk, even)


def edges(chunks, crossing, pair=True):
    _, _, vectors, width = chunks[0].shape
    counts = [len(chunks)] * pair + [len(crossing)] * bool(crossing)
    shapes = [(edge_base(n, 0, 0, vectors), width) for n in counts]
    return pl.pallas_call(
        functools.partial(edges_kernel, len(chunks), crossing),
        out_shape=[jax.ShapeDtypeStruct(shape, jnp.float32) for shape in shapes],
        compiler_params=params(),
        cost_estimate=cost(0, 16 * shapes[0][0] * width),
        name="edges",
    )(*chunks)


def smooth_kernel(pair_slot, cross_slot, chunk, pair, cross, own_c, pair_c, cross_c, out):
    _, rows, vectors, width = chunk.shape
    rim = PASSES - 1
    even = even_strip()
    part = math.gcd(vectors, 2 * GROUP)
    strip = lax.axis_index("seabed")
    inside = (strip > 0) & (strip < lax.axis_size("seabed") - 1)

    def rims(one, other):
        other = pick(inside, other, jnp.zeros_like(other))
        return pick(even, one, other), pick(even, other, one)

    def rim_of(ref):
        base = ref.shape[0] - GROUP
        return ref[base : base + rim]

    high_c, low_c = rims(rim_of(pair_c), rim_of(cross_c))
    coefficients = [low_c[i : i + 1] for i in range(rim)]
    coefficients += [own_c[i : i + 1] for i in range(rows)]
    coefficients += [high_c[i : i + 1] for i in range(rim)]
    coefficients = [jnp.broadcast_to(c, (part, width)) for c in coefficients]
    for b in range(2):
        for start in range(0, vectors, part):
            span = slice(start, start + part)
            low, high = [], []
            for r in range(PASSES):
                at = edge_base(pair_slot, b, r, vectors) + start
                to = edge_base(cross_slot, b, r, vectors) + start
                above, below = rims(pair[at : at + part], cross[to : to + part])
                high.append(above)
                low.append(below)
            values = low + [chunk[b, r, span] for r in range(rows)] + high
            for step in range(PASSES):
                values = relaxed_rows(values, coefficients[step : len(coefficients) - step])
            for r in range(rows):
                out[b, r, span] = values[r]


def smooth(chunk, pair, pair_slot, cross, cross_slot, coefficients):
    return pl.pallas_call(
        functools.partial(smooth_kernel, pair_slot, cross_slot),
        out_shape=jax.ShapeDtypeStruct(chunk.shape, jnp.float32),
        compiler_params=params(),
        cost_estimate=cost(30 * chunk.size, 10 * chunk.size),
        name="smooth",
    )(chunk, pair, cross, *coefficients)


def place_of(index, o, owners_in):
    owner = (lax.axis_index("freq") ^ index) * owners_in + o
    apart = owner ^ lax.axis_index("seabed")
    return apart & 1, apart >> 1


def combine_kernel(indices, owners_in, paired, absent, *refs):
    count = len(indices)
    chunks, transfer, (out, held) = refs[:count], refs[count : count + 4], refs[-2:]
    _, rows, vectors, width = chunks[0].shape
    owned = vectors // owners_in
    for at, ref in enumerate(chunks):
        for b in range(2):
            for r in range(rows):
                held[b, at, :, r * width : (r + 1) * width] = ref[b, r]
    half = count * vectors
    lhs_high, lhs_low = split_bf16(held[...].reshape(2 * half, rows * width))
    lhs_both = jnp.concatenate([lhs_high, lhs_low], axis=0)

    def times(t_high, t_low):
        def dot(x, w):
            return lax.dot_general(
                x, w, (((1,), (0,)), ((), ())), preferred_element_type=jnp.float32
            )

        by_high = dot(lhs_both, t_high[...])
        return (by_high[2 * half :] + dot(lhs_high, t_low[...])) + by_high[: 2 * half]

    by_real, by_imag = times(*transfer[:2]), times(*transfer[2:])
    real = by_real[:half] - by_imag[half:]
    imag = by_imag[:half] + by_real[half:]

    def place(index, o):
        if not paired:
            return index * owners_in + o
        core, chip = place_of(index, o, owners_in)
        return core * (out.shape[0] // 2) + (chip if absent else indices.index(index))

    for at, index in enumerate(indices):
        for o in range(owners_in):
            span = slice((at * owners_in + o) * owned, (at * owners_in + o + 1) * owned)
            out[place(index, o), 0] = real[span]
            out[place(index, o), 1] = imag[span]
    for index in absent:
        for o in range(owners_in):
            out[place(index, o)] = jnp.zeros(out.shape[1:], out.dtype)


def combine(chunks, split, owners_in, places, paired, absent=()):
    cells, sensors = split[0].shape
    indices = sorted(chunks)
    _, _, vectors, _ = chunks[indices[0]].shape
    owned = vectors // owners_in
    whole = len(indices) * vectors
    return pl.pallas_call(
        functools.partial(combine_kernel, indices, owners_in, paired, absent),
        out_shape=jax.ShapeDtypeStruct((places, 2, owned, sensors), jnp.float32),
        scratch_shapes=[pltpu.VMEM((2, len(indices), vectors, cells), jnp.float32)],
        compiler_params=params(),
        cost_estimate=cost(
            24 * whole * sensors * cells,
            8 * sensors * cells + 8 * whole * cells + 16 * whole * sensors,
        ),
        name="combine",
    )(*[chunks[i] for i in indices], *split)


def merge_kernel(late, owners_in, most, most_moved, tail, tail_moved, *outs):
    chips = [place_of(index, 0, owners_in)[1] for index in late]
    final = [tail[i] + tail_moved[i] for i in range(len(late))]
    for d, out in enumerate(outs):
        value = most[d] + most_moved[d]
        for chip, add in zip(chips, final):
            value = value + pick(chip == d, add, jnp.zeros_like(add))
        out[...] = value


def merge(late, owners_in, most, most_moved, tail, tail_moved):
    shape = jax.ShapeDtypeStruct(most.shape[1:], jnp.float32)
    return pl.pallas_call(
        functools.partial(merge_kernel, late, owners_in),
        out_shape=[shape] * most_moved.shape[0],
        compiler_params=params(),
        cost_estimate=cost(4 * most.size, 12 * most.size),
        name="merge",
    )(most, most_moved, tail, tail_moved)


def xor_pairs(count, apart):
    return [(i, i ^ apart) for i in range(count)]


def to_pair(edge, strips):
    return lax.ppermute(edge, "seabed", xor_pairs(strips, 1))


def to_cross(edge, strips):
    inner = [(i, (i + 1) % strips) for i in range(1, strips, 2)]
    return lax.ppermute(edge, "seabed", inner + [(b, a) for a, b in inner])


def paired_shards(field, coefficient, split_of, table, freq_count, strips):
    chunks, pair, crosses, coefficient = transform(
        field, table, coefficient, freq_count, ((2,), (0,))
    )

    def swap(m, chunk):
        return lax.ppermute(chunk, "freq", xor_pairs(freq_count, m))

    def relax(chunk, pair, pair_slot, cross):
        return smooth(chunk, pair, pair_slot, cross, 0, coefficients)

    first = swap(1, chunks[1])
    third = swap(3, chunks[3])
    cross2 = to_cross(crosses[0], strips)
    pair = to_pair(pair, strips)
    cross0 = to_cross(crosses[1], strips)
    coefficients = (coefficient, pair, cross2)
    real = split_of(0)
    split = (*real, *split_of(1))
    second = swap(2, relax(chunks[2], pair, 0, cross2))
    own = relax(chunks[0], pair, 1, cross0)
    (cross1,) = edges([first], (0,), False)
    cross1 = to_cross(cross1, strips)
    pair, cross3 = edges([first, third], (1,))
    cross3 = to_cross(cross3, strips)
    pair = to_pair(pair, strips)
    first = relax(first, pair, 0, cross1)
    third = relax(third, pair, 1, cross3)
    most = combine({0: own, 1: first}, split, 2, strips, True, (2, 3))

    def to_core(partial):
        send = partial[partial.shape[0] // 2 :]
        return lax.ppermute(send, "seabed", xor_pairs(strips, 1))

    most_moved = to_core(most)
    tail = combine({2: second, 3: third}, split, 2, strips // 2, True)
    chips = merge((2, 3), 2, most, most_moved, tail, to_core(tail))
    total = chips[0]
    for d in range(1, strips // 2):
        total = total + lax.ppermute(chips[d], "seabed", xor_pairs(strips, 2 * d))
    return total


def plain_shards(field, coefficient, split_of, table, freq_count, strips):
    spectrum, pair_c, (cross_c,), coefficient = transform(
        field, table, coefficient, freq_count, ((),)
    )
    spectrum = jnp.stack(spectrum)
    spectrum = lax.all_to_all(spectrum, "freq", split_axis=0, concat_axis=0, tiled=True)
    chunks = list(spectrum)
    pair_c = to_pair(pair_c, strips)
    cross_c = to_cross(cross_c, strips)
    coefficients = (coefficient, pair_c, cross_c)
    pair, cross = edges(chunks, tuple(range(len(chunks))))
    pair, cross = to_pair(pair, strips), to_cross(cross, strips)
    chunks = [smooth(c, pair, i, cross, i, coefficients) for i, c in enumerate(chunks)]
    owners_in = strips // freq_count
    partial = combine(dict(enumerate(chunks)), (*split_of(0), *split_of(1)), owners_in, strips, False)
    got = lax.all_to_all(partial, "seabed", split_axis=0, concat_axis=0, tiled=True)
    return got.sum(0)


def shards(uplift, coefficient, transfer):
    vectors, steps, _, _ = uplift.shape
    freq_count, strips = FD * lax.axis_size("freq"), lax.axis_size("seabed")
    owned = vectors * freq_count // strips
    paired = (
        strips == 8
        and freq_count == 4
        and vectors == 2 * owned
        and owned == 2 * GROUP
    )
    slots = np.arange(freq_count)
    order = slots[:, None] ^ slots[None, :] if paired else slots[None, :]
    table = transform_operand(steps, freq_count, order)
    field = jnp.transpose(uplift, (0, 2, 1, 3))
    run = paired_shards if paired else plain_shards
    total = run(
        field,
        coefficient,
        lambda part: split_transfer(transfer[0], part),
        table,
        freq_count,
        strips,
    )
    return jnp.transpose(total, (1, 0, 2))[:, None]


def solution(mesh):
    placed = (P("freq", None, "seabed", None), P("seabed", None), P("freq", None, None, "seabed"))
    return jax.shard_map(
        shards,
        mesh=mesh,
        in_specs=placed,
        out_specs=P("seabed", "freq", None, None),
        check_vma=False,
    )
```

```python
import functools
import math

import jax
import jax.numpy as jnp
import numpy as np
from jax import lax
from jax.experimental import pallas as pl
from jax.experimental.pallas import tpu as pltpu
from jax.sharding import PartitionSpec as P


FD = 1
PASSES = 3
GROUP = 8
GRANT = 16 * 1024 * 1024


def params():
    return pltpu.CompilerParams(vmem_limit_bytes=GRANT)


def cost(flops, moved):
    return pl.CostEstimate(flops=flops, bytes_accessed=moved, transcendentals=0)


def in_hbm(array):
    return pltpu.with_memory_space_constraint(array, pltpu.HBM)


def even_strip():
    return lax.rem(lax.axis_index("seabed"), 2) == 0


def pick(flag, one, other):
    return jnp.where(jnp.full(one.shape, flag), one, other)


def dft_table(steps_count, freq_count):
    times = np.arange(steps_count)
    freqs = np.arange(freq_count)
    phase = (freqs[:, None] * times[None, :] % steps_count) * (2.0 * math.pi / steps_count)
    scale = 1.0 / math.sqrt(steps_count)
    return (np.stack([np.cos(phase), -np.sin(phase)], 1) * scale).astype(np.float32)


def split_bf16(values):
    high = values.astype(jnp.bfloat16)
    low = (values - high.astype(values.dtype)).astype(jnp.bfloat16)
    return high, low


def transform_operand(steps_count, freq_count, order):
    table = dft_table(steps_count, freq_count)[order]
    parts = np.stack([x.astype(np.float32) for x in split_bf16(table)], 1)
    sources = parts.shape[0]
    wide = np.broadcast_to(parts[..., None, :], (*parts.shape[:-1], GROUP, steps_count))
    return jnp.asarray(wide.reshape(sources, -1, GROUP * steps_count), jnp.float32)


def edge_base(slot, b, r, vectors):
    return ((slot * 2 + b) * PASSES + r) * vectors


def transform_kernel(slots, edged, field_hbm, table_hbm, own_hbm, *refs):
    outs, pair, crosses = refs[:slots], refs[slots], refs[slots + 1 : -6]
    own_c, field, table, field_sem, table_sem, own_sem = refs[-6:]
    vectors, rows, steps, width = field.shape
    blocks = vectors // GROUP
    even = even_strip()
    source = lax.axis_index("freq") if table_hbm.shape[0] > 1 else 0
    get_field = pltpu.make_async_copy(field_hbm, field, field_sem)
    get_field.start()
    get_table = pltpu.make_async_copy(table_hbm.at[source], table, table_sem)
    get_table.start()
    get_own = pltpu.make_async_copy(own_hbm, own_c, own_sem)
    get_own.start()
    get_own.wait()
    rim = PASSES - 1
    last_c, first_c = own_c[rows - rim :], own_c[:rim]
    for ref, one, other in ((pair, last_c, first_c), (crosses[0], first_c, last_c)):
        base = ref.shape[0] - GROUP
        ref[base : base + rim] = pick(even, one, other)
        ref[base + rim :] = jnp.zeros((GROUP - rim, width), jnp.float32)
    get_table.wait()
    short = table[...]
    shape = (short.shape[0], GROUP, short.shape[1])
    mine = lax.broadcasted_iota(jnp.int32, shape, 1)
    column = lax.broadcasted_iota(jnp.int32, shape, 2)
    full = jnp.where(
        (column >= mine * steps) & (column < (mine + 1) * steps), short[:, None], 0.0
    )
    full = full.reshape(-1, short.shape[1]).astype(jnp.bfloat16)
    get_field.wait()
    for i in range(blocks):
        span = slice(i * GROUP, (i + 1) * GROUP)
        data = jnp.concatenate(
            [field[span, r].reshape(GROUP * steps, width) for r in range(rows)], axis=1
        )
        both = jnp.dot(full, data, preferred_element_type=jnp.float32)
        half = both.shape[0] // 2
        values = both[:half] + both[half:]
        for slot in range(slots):
            for b in range(2):
                at = (slot * 2 + b) * GROUP
                for r in range(rows):
                    piece = values[at : at + GROUP, r * width : (r + 1) * width]
                    outs[slot][b, r, span] = piece
                if slot not in sum(edged, ()):
                    continue
                group = [slot in g for g in edged].index(True)
                for r in range(PASSES):
                    row = (rows - PASSES + r) * width
                    last = values[at : at + GROUP, row : row + width]
                    first = values[at : at + GROUP, r * width : (r + 1) * width]
                    to = edge_base(sum(edged, ()).index(slot), b, r, vectors) + i * GROUP
                    pair[to : to + GROUP] = pick(even, last, first)
                    to = edge_base(edged[group].index(slot), b, r, vectors) + i * GROUP
                    crosses[group][to : to + GROUP] = pick(even, first, last)


def transform(field, table, coefficient, slots, edged):
    vectors, rows, steps, width = field.shape
    chunk = jax.ShapeDtypeStruct((2, rows, vectors, width), jnp.float32)
    size = edge_base(1, 0, 0, vectors)
    pair = (sum(map(len, edged)) * size + GROUP, width)
    crosses = [(len(g) * size + GROUP * (i == 0), width) for i, g in enumerate(edged)]
    edges = [jax.ShapeDtypeStruct(shape, jnp.float32) for shape in (pair, *crosses, coefficient.shape)]
    hbm = pl.BlockSpec(memory_space=pltpu.HBM)
    vmem = pl.BlockSpec(memory_space=pltpu.VMEM)
    outs = pl.pallas_call(
        functools.partial(transform_kernel, slots, edged),
        out_shape=[chunk] * slots + edges,
        in_specs=[hbm, hbm, hbm],
        out_specs=[vmem] * (slots + len(edges)),
        scratch_shapes=[
            pltpu.VMEM(field.shape, field.dtype),
            pltpu.VMEM(table.shape[1:], table.dtype),
            pltpu.SemaphoreType.DMA(()),
            pltpu.SemaphoreType.DMA(()),
            pltpu.SemaphoreType.DMA(()),
        ],
        compiler_params=params(),
        cost_estimate=cost(
            2 * table.shape[1] * table.shape[2] * rows * width * vectors,
            vectors * rows * width * (2 * steps + 8 * slots),
        ),
        name="transform",
    )(*map(in_hbm, (field, table, coefficient)))
    return outs[:slots], outs[slots], outs[slots + 1 : -1], outs[-1]


def split_kernel(x_ref, high_ref, low_ref):
    high_ref[...], low_ref[...] = split_bf16(jnp.transpose(x_ref[0]))


def split_transfer(transfer, part):
    _, sensors, cells = transfer.shape
    block = pl.BlockSpec((cells, sensors), lambda i: (0, 0))
    return pl.pallas_call(
        split_kernel,
        out_shape=[jax.ShapeDtypeStruct((cells, sensors), jnp.bfloat16)] * 2,
        grid=(1,),
        in_specs=[pl.BlockSpec((1, sensors, cells), lambda i: (part, 0, 0))],
        out_specs=[block, block],
        compiler_params=params(),
        cost_estimate=cost(2 * sensors * cells, 8 * sensors * cells),
        name="split_transfer",
    )(in_hbm(transfer))


def relaxed_rows(rows, coefficients):
    width = rows[0].shape[-1]
    lane = lax.broadcasted_iota(jnp.int32, rows[0].shape, 1)
    first, last = lane == 0, lane == width - 1
    out = []
    for i in range(1, len(rows) - 1):
        centre = rows[i]
        left = jnp.where(first, 0.0, pltpu.roll(centre, 1, 1))
        right = jnp.where(last, 0.0, pltpu.roll(centre, width - 1, 1))
        beside = (rows[i + 1] + rows[i - 1]) + (left + right)
        out.append(centre + coefficients[i - 1] * (beside - 4.0 * centre))
    return out


def edges_kernel(count, crossing, *refs):
    chunks, outs = refs[:count], refs[count:]
    _, rows, vectors, _ = chunks[0].shape
    even = even_strip().astype(jnp.int32)

    def put(ref, slot, chunk, last):
        for b in range(2):
            for r in range(PASSES):
                at = edge_base(slot, b, r, vectors)
                ref[at : at + vectors] = chunk[b, last * (rows - PASSES) + r]

    if crossing:
        for slot, index in enumerate(crossing):
            put(outs[-1], slot, chunks[index], 1 - even)
    if len(outs) > 1 or not crossing:
        for index, chunk in enumerate(chunks):
            put(outs[0], index, chunk, even)


def edges(chunks, crossing, pair=True):
    _, _, vectors, width = chunks[0].shape
    counts = [len(chunks)] * pair + [len(crossing)] * bool(crossing)
    shapes = [(edge_base(n, 0, 0, vectors), width) for n in counts]
    return pl.pallas_call(
        functools.partial(edges_kernel, len(chunks), crossing),
        out_shape=[jax.ShapeDtypeStruct(shape, jnp.float32) for shape in shapes],
        compiler_params=params(),
        cost_estimate=cost(0, 16 * shapes[0][0] * width),
        name="edges",
    )(*chunks)


def smooth_kernel(pair_slot, cross_slot, chunk, pair, cross, own_c, pair_c, cross_c, out):
    _, rows, vectors, width = chunk.shape
    rim = PASSES - 1
    even = even_strip()
    part = math.gcd(vectors, 2 * GROUP)
    strip = lax.axis_index("seabed")
    inside = (strip > 0) & (strip < lax.axis_size("seabed") - 1)

    def rims(one, other):
        other = pick(inside, other, jnp.zeros_like(other))
        return pick(even, one, other), pick(even, other, one)

    def rim_of(ref):
        base = ref.shape[0] - GROUP
        return ref[base : base + rim]

    high_c, low_c = rims(rim_of(pair_c), rim_of(cross_c))
    coefficients = [low_c[i : i + 1] for i in range(rim)]
    coefficients += [own_c[i : i + 1] for i in range(rows)]
    coefficients += [high_c[i : i + 1] for i in range(rim)]
    coefficients = [jnp.broadcast_to(c, (part, width)) for c in coefficients]
    for b in range(2):
        for start in range(0, vectors, part):
            span = slice(start, start + part)
            low, high = [], []
            for r in range(PASSES):
                at = edge_base(pair_slot, b, r, vectors) + start
                to = edge_base(cross_slot, b, r, vectors) + start
                above, below = rims(pair[at : at + part], cross[to : to + part])
                high.append(above)
                low.append(below)
            values = low + [chunk[b, r, span] for r in range(rows)] + high
            for step in range(PASSES):
                values = relaxed_rows(values, coefficients[step : len(coefficients) - step])
            for r in range(rows):
                out[b, r, span] = values[r]


def smooth(chunk, pair, pair_slot, cross, cross_slot, coefficients):
    return pl.pallas_call(
        functools.partial(smooth_kernel, pair_slot, cross_slot),
        out_shape=jax.ShapeDtypeStruct(chunk.shape, jnp.float32),
        compiler_params=params(),
        cost_estimate=cost(30 * chunk.size, 10 * chunk.size),
        name="smooth",
    )(chunk, pair, cross, *coefficients)


def place_of(index, o, owners_in):
    owner = (lax.axis_index("freq") ^ index) * owners_in + o
    apart = owner ^ lax.axis_index("seabed")
    return apart & 1, apart >> 1


def combine_kernel(indices, owners_in, paired, absent, *refs):
    count = len(indices)
    chunks, transfer, (out, held) = refs[:count], refs[count : count + 4], refs[-2:]
    _, rows, vectors, width = chunks[0].shape
    owned = vectors // owners_in
    for at, ref in enumerate(chunks):
        for b in range(2):
            for r in range(rows):
                held[b, at, :, r * width : (r + 1) * width] = ref[b, r]
    half = count * vectors
    lhs_high, lhs_low = split_bf16(held[...].reshape(2 * half, rows * width))
    lhs_both = jnp.concatenate([lhs_high, lhs_low], axis=0)

    def times(t_high, t_low):
        def dot(x, w):
            return lax.dot_general(
                x, w, (((1,), (0,)), ((), ())), preferred_element_type=jnp.float32
            )

        by_high = dot(lhs_both, t_high[...])
        return (by_high[2 * half :] + dot(lhs_high, t_low[...])) + by_high[: 2 * half]

    by_real, by_imag = times(*transfer[:2]), times(*transfer[2:])
    real = by_real[:half] - by_imag[half:]
    imag = by_imag[:half] + by_real[half:]

    def place(index, o):
        if not paired:
            return index * owners_in + o
        core, chip = place_of(index, o, owners_in)
        return core * (out.shape[0] // 2) + (chip if absent else indices.index(index))

    for at, index in enumerate(indices):
        for o in range(owners_in):
            span = slice((at * owners_in + o) * owned, (at * owners_in + o + 1) * owned)
            out[place(index, o), 0] = real[span]
            out[place(index, o), 1] = imag[span]
    for index in absent:
        for o in range(owners_in):
            out[place(index, o)] = jnp.zeros(out.shape[1:], out.dtype)


def combine(chunks, split, owners_in, places, paired, absent=()):
    cells, sensors = split[0].shape
    indices = sorted(chunks)
    _, _, vectors, _ = chunks[indices[0]].shape
    owned = vectors // owners_in
    whole = len(indices) * vectors
    return pl.pallas_call(
        functools.partial(combine_kernel, indices, owners_in, paired, absent),
        out_shape=jax.ShapeDtypeStruct((places, 2, owned, sensors), jnp.float32),
        scratch_shapes=[pltpu.VMEM((2, len(indices), vectors, cells), jnp.float32)],
        compiler_params=params(),
        cost_estimate=cost(
            24 * whole * sensors * cells,
            8 * sensors * cells + 8 * whole * cells + 16 * whole * sensors,
        ),
        name="combine",
    )(*[chunks[i] for i in indices], *split)


def merge_kernel(late, owners_in, most, most_moved, tail, tail_moved, *outs):
    chips = [place_of(index, 0, owners_in)[1] for index in late]
    final = [tail[i] + tail_moved[i] for i in range(len(late))]
    for d, out in enumerate(outs):
        value = most[d] + most_moved[d]
        for chip, add in zip(chips, final):
            value = value + pick(chip == d, add, jnp.zeros_like(add))
        out[...] = value


def merge(late, owners_in, most, most_moved, tail, tail_moved):
    shape = jax.ShapeDtypeStruct(most.shape[1:], jnp.float32)
    return pl.pallas_call(
        functools.partial(merge_kernel, late, owners_in),
        out_shape=[shape] * most_moved.shape[0],
        compiler_params=params(),
        cost_estimate=cost(4 * most.size, 12 * most.size),
        name="merge",
    )(most, most_moved, tail, tail_moved)


def xor_pairs(count, apart):
    return [(i, i ^ apart) for i in range(count)]


def to_pair(edge, strips):
    return lax.ppermute(edge, "seabed", xor_pairs(strips, 1))


def to_cross(edge, strips):
    inner = [(i, (i + 1) % strips) for i in range(1, strips, 2)]
    return lax.ppermute(edge, "seabed", inner + [(b, a) for a, b in inner])


def paired_shards(field, coefficient, split_of, table, freq_count, strips):
    chunks, pair, crosses, coefficient = transform(
        field, table, coefficient, freq_count, ((2,), (0,))
    )

    def swap(m, chunk):
        return lax.ppermute(chunk, "freq", xor_pairs(freq_count, m))

    def relax(chunk, pair, pair_slot, cross):
        return smooth(chunk, pair, pair_slot, cross, 0, coefficients)

    first = swap(1, chunks[1])
    third = swap(3, chunks[3])
    cross2 = to_cross(crosses[0], strips)
    pair = to_pair(pair, strips)
    cross0 = to_cross(crosses[1], strips)
    coefficients = (coefficient, pair, cross2)
    real = split_of(0)
    split = (*real, *split_of(1))
    second = swap(2, relax(chunks[2], pair, 0, cross2))
    own = relax(chunks[0], pair, 1, cross0)
    (cross3,) = edges([third], (0,), False)
    cross3 = to_cross(cross3, strips)
    pair, cross1 = edges([third, first], (1,))
    cross1 = to_cross(cross1, strips)
    pair = to_pair(pair, strips)
    third = relax(third, pair, 0, cross3)
    first = relax(first, pair, 1, cross1)
    most = combine({0: own, 3: third}, split, 2, strips, True, (1, 2))

    def to_core(partial):
        send = partial[partial.shape[0] // 2 :]
        return lax.ppermute(send, "seabed", xor_pairs(strips, 1))

    most_moved = to_core(most)
    tail = combine({1: first, 2: second}, split, 2, strips // 2, True)
    chips = merge((1, 2), 2, most, most_moved, tail, to_core(tail))
    total = chips[0]
    for d in range(1, strips // 2):
        total = total + lax.ppermute(chips[d], "seabed", xor_pairs(strips, 2 * d))
    return total


def plain_shards(field, coefficient, split_of, table, freq_count, strips):
    spectrum, pair_c, (cross_c,), coefficient = transform(
        field, table, coefficient, freq_count, ((),)
    )
    spectrum = jnp.stack(spectrum)
    spectrum = lax.all_to_all(spectrum, "freq", split_axis=0, concat_axis=0, tiled=True)
    chunks = list(spectrum)
    pair_c = to_pair(pair_c, strips)
    cross_c = to_cross(cross_c, strips)
    coefficients = (coefficient, pair_c, cross_c)
    pair, cross = edges(chunks, tuple(range(len(chunks))))
    pair, cross = to_pair(pair, strips), to_cross(cross, strips)
    chunks = [smooth(c, pair, i, cross, i, coefficients) for i, c in enumerate(chunks)]
    owners_in = strips // freq_count
    partial = combine(dict(enumerate(chunks)), (*split_of(0), *split_of(1)), owners_in, strips, False)
    got = lax.all_to_all(partial, "seabed", split_axis=0, concat_axis=0, tiled=True)
    return got.sum(0)


def shards(uplift, coefficient, transfer):
    vectors, steps, _, _ = uplift.shape
    freq_count, strips = FD * lax.axis_size("freq"), lax.axis_size("seabed")
    owned = vectors * freq_count // strips
    paired = (
        strips == 8
        and freq_count == 4
        and vectors == 2 * owned
        and owned == 2 * GROUP
    )
    slots = np.arange(freq_count)
    order = slots[:, None] ^ slots[None, :] if paired else slots[None, :]
    table = transform_operand(steps, freq_count, order)
    field = jnp.transpose(uplift, (0, 2, 1, 3))
    run = paired_shards if paired else plain_shards
    total = run(
        field,
        coefficient,
        lambda part: split_transfer(transfer[0], part),
        table,
        freq_count,
        strips,
    )
    return jnp.transpose(total, (1, 0, 2))[:, None]


def solution(mesh):
    placed = (P("freq", None, "seabed", None), P("seabed", None), P("freq", None, None, "seabed"))
    return jax.shard_map(
        shards,
        mesh=mesh,
        in_specs=placed,
        out_specs=P("seabed", "freq", None, None),
        check_vma=False,
    )
```
